128 devices in a mesh: lon: 8 (over z, core), lat: 16 (over x, y).
Axes of the slice: x: 4, y: 4, z: 4, core: 2. Of those that a mesh axis runs over, the one named last changes fastest.
Arguments:
- travel_times: float32 [4096], P(('lon', 'lat')), may hold values from -6 to 6
- ray_counts: int32 [128], P(('lon', 'lat')), may hold values from 4 to 32
- tile_brick: int32 [4096, 4], P(('lon', 'lat')), may hold values from 0 to 127, all different within a row; in each aligned block of 32 rows (0 to 31, 32 to 63, ...) at most 2 rows name the same one
- cell_offsets: int32 [4096, 4, 128], P(('lon', 'lat')), may hold values from 0 to 1023
- cell_depths: int32 [4096, 4, 128], P(('lon', 'lat')), may hold values from 0 to 127
- seg_lengths: float32 [4096, 4, 128], P(('lon', 'lat')), may hold values from 0.002 to 0.02
Outputs:
- model: float32 [256, 512, 128], P('lon', 'lat')
- misfit: float32 [4096], P(('lon', 'lat'))
The draws below stay inside these ranges and needn't reach their ends.
Inputs may be any that keep to these rules, and one draw needn't show every extreme that they name: `tile_brick`: among the 4 tiles of all rays of one device, no brick is named more than 2 times, a bound that some block reaches; a ray's tiles name different bricks; brick k lives on the device at position k of lon+lat. Only the first ray_counts rays of a device's 32 slots are live.
All inputs are finite; a program needn't handle non-finite values.
Results may differ from the reference program's by a relative error of at most 0.0014.
Values sent between devices are 32-bit elements; how exact they have to be, the bound alone decides.
A program may use at most 64 MiB of HBM per device.

```python
import math
import jax
import jax.numpy as jnp
import numpy as np
from jax import lax

CLON = 32
CLAT = 32
DEP = 128
SEG = 128
TPR = 4
RAYS_DEV = 32
ITERS = 2
CAP = 2
RAYS = 4096
N_LON = 8
N_LAT = 16
DEVICES = 128


def touch_ends(values, stream_key, smallest, largest):
    longest = values.shape.index(max(values.shape))
    spots = []
    for shift in (0, 1):
        where = [jax.random.randint(jax.random.fold_in(stream_key, axis), (), 0, length) for axis, length in enumerate(values.shape)]
        where[longest] = (where[longest] + shift) % values.shape[longest]
        spots.append(tuple(where))
    return values.at[spots[0]].set(smallest).at[spots[1]].set(largest)


def shard_levels(own_key, extent, pieces, smallest, high):
    def one(axis_at, shards_of):
        steps = jax.random.uniform(jax.random.fold_in(jax.random.fold_in(own_key, 6), axis_at), (shards_of,), jnp.float32, smallest / len(pieces), high / len(pieces))
        return jnp.repeat(jnp.exp(steps), extent[axis_at] // shards_of).reshape((-1,) + (1,) * (len(extent) - axis_at - 1))

    factor_of = one(*pieces[0])
    for cut in pieces[1:]:
        factor_of = factor_of * one(*cut)
    return factor_of


def shared_out(stream_key, own, number, rows, count, top, bound, lean):
    sequence = jax.random.permutation(stream_key, count)
    heavy_load, usual = portions_of(count, rows * top, bound, lean, True), portions_of(count, rows * top, bound, lean, False)
    places = jnp.arange(count)

    def named(lengths, rotation):
        used = int((lengths > 0).sum())
        fixed = max(1, used // 4)
        passed = fixed + (places - fixed + rotation * (used - fixed)) % max(1, count - fixed)
        return jnp.zeros((count,), jnp.int32).at[sequence[jnp.where(places < fixed, places, passed)]].set(jnp.asarray(lengths, jnp.int32))

    lengths = jnp.where(number % 4 == 0, named(heavy_load, number // 4), named(usual, number - number // 4 - 1))
    mixed = jax.random.permutation(jax.random.fold_in(own, 3), count)
    donor, sink = mixed[0:count // 2 * 2:2], mixed[1:count // 2 * 2:2]
    margin = jnp.minimum(lengths[donor] - 1, bound - lengths[sink]) // 2
    margin = jnp.where((donor == sequence[0]) | (sink == sequence[0]) | (lengths[sink] == 0), 0, jnp.maximum(margin, 0))
    passed = jax.random.randint(jax.random.fold_in(own, 4), (count // 2,), 0, 1 << 20) % (margin + 1)
    lengths = lengths.at[donor].add(-passed).at[sink].add(passed)
    labels = jnp.searchsorted(jnp.cumsum(lengths), jnp.arange(rows * top), side="right").astype(jnp.int32)
    listing = labels.reshape(top, rows).T
    listing = listing[jax.random.permutation(jax.random.fold_in(own, 1), rows)]
    rotation = jax.random.randint(jax.random.fold_in(own, 2), (rows, 1), 0, top)
    return jnp.take_along_axis(listing, (jnp.arange(top)[None, :] + rotation) % top, axis=1)


def portions_of(number_of, total, most, lean, full):
    portions = [(1 << 20) // math.isqrt(grade ** lean) + 1 for grade in range(1, number_of + 1)]
    largest = most if full else min(most, max(-(-total // number_of), total * portions[0] // sum(portions)))
    least = 1 if total - largest >= number_of - 1 else 0
    holding, surplus = [largest] + [least] * (number_of - 1), total - largest - least * (number_of - 1)
    while surplus > 0:
        movable = [i for i in range(1, number_of) if holding[i] < largest] or [i for i in range(1, number_of) if holding[i] < most]
        whole, budget = sum([portions[i] for i in movable]), surplus
        for i in movable:
            extra = min(most - holding[i], max(1, budget * portions[i] // whole), surplus)
            holding[i] = holding[i] + extra
            surplus = surplus - extra
    return np.array(holding)


def normal_values(own_key, dims, spread, limit, split=(), held_as=jnp.bfloat16):
    values = spread * jax.random.normal(own_key, dims, jnp.float32)
    if split:
        values = values * shard_levels(own_key, dims, split, -0.22, 0.18)
    return jnp.clip(values, -limit, limit).astype(held_as)


def setup_inputs(seed: int = 0) -> dict:
    keys = jax.random.split(jax.random.key(seed), 7)
    travel_times = normal_values(keys[0], (RAYS,), 1.0, 6.0, ((0, 128),), jnp.float32)
    ray_counts = touch_ends(jax.random.randint(keys[1], (DEVICES,), RAYS_DEV // 8, RAYS_DEV + 1), jax.random.fold_in(keys[1], 1), RAYS_DEV // 8, RAYS_DEV).astype(jnp.int32)
    tile_brick_keys = jax.random.split(jax.random.fold_in(keys[2], 1), RAYS // RAYS_DEV)
    tile_brick_turns = jax.random.permutation(jax.random.fold_in(keys[2], 3), RAYS // RAYS_DEV)
    tile_brick = jax.vmap(lambda own, number: shared_out(jax.random.fold_in(keys[2], 2), own, number, RAYS_DEV, DEVICES, TPR, CAP, 2))(tile_brick_keys, tile_brick_turns).reshape((RAYS, TPR))
    cell_offsets = touch_ends(jax.random.randint(keys[3], (RAYS, TPR, SEG), 0, CLON * CLAT), jax.random.fold_in(keys[3], 1), 0, (CLON * CLAT) - 1).astype(jnp.int32)
    cell_depths = touch_ends(jax.random.randint(keys[4], (RAYS, TPR, SEG), 0, DEP), jax.random.fold_in(keys[4], 1), 0, DEP - 1).astype(jnp.int32)
    seg_lengths = jnp.clip(0.002 + 0.018 * jax.random.uniform(keys[5], (RAYS, TPR, SEG), jnp.float32) ** shard_levels(keys[5], (RAYS, TPR, SEG), ((0, 128),), -0.2, 0.2), 0.002, 0.02)
    return {"travel_times": travel_times, "ray_counts": ray_counts, "tile_brick": tile_brick, "cell_offsets": cell_offsets, "cell_depths": cell_depths, "seg_lengths": seg_lengths}


damping = 0.01

def to_bricks(grid):
    parts = grid.reshape(N_LON, CLON, N_LAT, CLAT, DEP).transpose(0, 2, 1, 3, 4)
    return parts.reshape(N_LON * N_LAT * CLON * CLAT * DEP)

def from_bricks(flat_cells):
    parts = flat_cells.reshape(N_LON, N_LAT, CLON, CLAT, DEP).transpose(0, 2, 1, 3, 4)
    return parts.reshape(N_LON * CLON, N_LAT * CLAT, DEP)

def smoothing(field):
    lon_pad = jnp.concatenate([field[-1:], field, field[:1]], axis=0)
    lat_pad = jnp.pad(field, ((0, 0), (1, 1), (0, 0)))
    dep_pad = jnp.pad(field, ((0, 0), (0, 0), (1, 1)))
    result = 6.0 * field - lon_pad[2:] - lon_pad[:-2] - lat_pad[:, 2:] - lat_pad[:, :-2]
    return result - dep_pad[:, :, 2:] - dep_pad[:, :, :-2]

def reference(travel_times, ray_counts, tile_brick, cell_offsets, cell_depths, seg_lengths):
    rays_all = travel_times.shape[0]
    ray_pos = jnp.arange(rays_all, dtype=jnp.int32)
    owner_dev = ray_pos // RAYS_DEV
    live_mask = (ray_pos % RAYS_DEV < ray_counts[owner_dev]).astype(jnp.float32)
    weights = (seg_lengths * live_mask[:, None, None]).reshape(-1)
    brick_cells = CLON * CLAT * DEP
    inside = cell_offsets * DEP + cell_depths
    cell_index = (tile_brick[:, :, None] * brick_cells + inside).astype(jnp.int32).reshape(-1)
    total_cells = N_LON * N_LAT * brick_cells

    def forward(grid):
        cells = to_bricks(grid)
        return lax.optimization_barrier(jnp.sum((weights * cells[cell_index]).reshape(rays_all, -1), axis=1))

    def backward(ray_vals):
        terms = (weights.reshape(rays_all, -1) * ray_vals[:, None]).reshape(-1)
        cells = jnp.zeros((total_cells,), jnp.float32).at[cell_index].add(terms)
        return from_bricks(cells)
    data = travel_times * live_mask
    beta_now = jnp.sqrt(jnp.sum(data * data))
    u_ray = data / beta_now
    u_grid = jnp.zeros((N_LON * CLON, N_LAT * CLAT, DEP), jnp.float32)
    v_dir = backward(u_ray)
    alpha_now = jnp.sqrt(jnp.sum(v_dir * v_dir))
    v_dir = v_dir / alpha_now
    search = v_dir
    model = jnp.zeros_like(v_dir)
    phi_bar = beta_now
    rho_bar = alpha_now
    for turn_index in range(ITERS):
        u_ray = forward(v_dir) - alpha_now * u_ray
        u_grid = damping * smoothing(v_dir) - alpha_now * u_grid
        beta_now = jnp.sqrt(jnp.sum(u_ray * u_ray) + jnp.sum(u_grid * u_grid))
        u_ray = u_ray / beta_now
        u_grid = u_grid / beta_now
        v_dir = backward(u_ray) + damping * smoothing(u_grid) - beta_now * v_dir
        alpha_now = jnp.sqrt(jnp.sum(v_dir * v_dir))
        v_dir = v_dir / alpha_now
        rho_new = jnp.sqrt(rho_bar * rho_bar + beta_now * beta_now)
        cosine = rho_bar / rho_new
        sine_val = beta_now / rho_new
        theta_val = sine_val * alpha_now
        rho_bar = -cosine * alpha_now
        phi_val = cosine * phi_bar
        phi_bar = sine_val * phi_bar
        model = model + phi_val / rho_new * search
        search = v_dir - theta_val / rho_new * search
    misfit = data - forward(model)
    return (model, misfit)
```

```python
import functools

import jax
import jax.numpy as jnp
from jax import lax
from jax.experimental import pallas as pl
from jax.experimental.pallas import tpu as pltpu
from jax.sharding import Mesh
from jax.sharding import PartitionSpec as P

CLON, CLAT, DEP, SEG = 32, 32, 128, 128
COLS = CLON * CLAT
RAYS, TPR = 32, 4
NDEV = 128
SLOTS = 2 * NDEV
CHUNK = 8
SCALE = 8.0
DAMP = 0.01 * SCALE
LON_LAT = ("lon_0", "lon_1", "lat_0", "lat_1")
LON = ("lon_0", "lon_1")
LAT = ("lat_0", "lat_1")

f32, bf16, i32 = jnp.float32, jnp.bfloat16, jnp.int32
VMEM = pl.BlockSpec(memory_space=pltpu.VMEM)
SMEM = pl.BlockSpec(memory_space=pltpu.SMEM)
PARAMS = pltpu.CompilerParams(vmem_limit_bytes=48 << 20)


def iota(shape, dim):
    return lax.broadcasted_iota(i32, shape, dim)


def split2(x):
    hi = x.astype(bf16)
    return hi, (x - hi.astype(f32)).astype(bf16)


def split3(x):
    hi = x.astype(bf16)
    rest = x - hi.astype(f32)
    mid = rest.astype(bf16)
    return hi, mid, (rest - mid.astype(f32)).astype(bf16)


def as_payload(cell, lens):
    col = cell >> 7
    parts = [(cell & 127), (col & 127), (col >> 7)]
    return jnp.concatenate([p.astype(f32).astype(bf16) for p in parts] + list(split3(lens)), axis=1)


def from_payload(rows):
    z, low, high, hi, mid, lo = [rows[:, k * 128:(k + 1) * 128] for k in range(6)]
    return z, high * 128.0 + low, (hi + mid) + lo


def pack_kernel(count, brick, times, offs, deps, lens, out, pay):
    lane = iota((RAYS, 128), 1)
    mine = iota((RAYS, 128), 0) == (lane & 31)
    tb = brick[...]
    wide = jnp.zeros((RAYS, 128), i32)
    for k in range(TPR):
        wide = jnp.where((lane >> 5) == k, tb[:, k:k + 1], wide)
    brick_row = jnp.sum(jnp.where(mine, wide, 0).astype(f32), axis=0, keepdims=True)
    time_row = jnp.concatenate([times[...]] * TPR, axis=1)
    ray_row = iota((1, 128), 1) & 31
    live = ray_row < count[0]
    as_rows = jnp.broadcast_to(brick_row, (128, 128))
    same = (as_rows == as_rows.T) & (iota((128, 128), 0) < iota((128, 128), 1))
    rank_row = jnp.sum(jnp.where(same, 1.0, 0.0), axis=0, keepdims=True)
    for k in range(TPR):
        cell = offs[:, k, :] * DEP + deps[:, k, :]
        pay[k * RAYS:(k + 1) * RAYS, :] = as_payload(cell, lens[:, k, :] * SCALE)
    target = iota((128, 128), 0).astype(f32)
    meta = jnp.zeros((128, 128), f32)
    lanes = iota((128, 128), 1)
    for k in range(2):
        picked = jnp.where((target == brick_row) & (rank_row == k) & live, 1.0, 0.0)
        z, col, w = from_payload(jnp.dot(picked.astype(bf16), pay[...], preferred_element_type=f32))
        out[:, k, :] = col * 128.0 + z
        out[:, 2 + k, :] = w
        value = jnp.sum(picked * time_row, axis=1, keepdims=True)
        ray = jnp.sum(picked * (ray_row + 1).astype(f32), axis=1, keepdims=True)
        meta = jnp.where(lanes == k, value, jnp.where(lanes == 2 + k, ray, meta))
    out[:, 4, :] = meta


def onehot_cols(col_row):
    at = jnp.broadcast_to(col_row.astype(jnp.int16), (COLS, 128))
    return jnp.where(lax.broadcasted_iota(jnp.int16, (COLS, 128), 0) == at, jnp.ones((), bf16), jnp.zeros((), bf16))


def scatter_into(acc, n, col, dep, wy, oht, vt):
    acc[...] = jnp.zeros_like(acc)

    def body(c, carry):
        for j in range(CHUNK):
            row = pl.ds(c * CHUNK + j, 1)
            at = slice(j * 128, (j + 1) * 128)
            oht[:, at] = onehot_cols(col[row, :])
            w = wy[row, :]
            hi = w.astype(bf16).astype(f32)
            here = iota((DEP, 128), 0) == dep[row, :]
            vt[0:128, at] = jnp.where(here, hi, 0.0).astype(bf16)
            vt[128:256, at] = jnp.where(here, w - hi, 0.0).astype(bf16)
        acc[...] += lax.dot_general(oht[...], vt[...], (((1,), (1,)), ((), ())), preferred_element_type=f32)
        return carry

    lax.fori_loop(0, (n + CHUNK - 1) // CHUNK, body, 0)


def gather_from(grid, n, col, dep, w, out, oht, gt):
    hi, lo = split2(grid.T)
    gt[0:128, :] = hi
    gt[128:256, :] = lo
    out[...] = jnp.zeros_like(out)

    def body(c, carry):
        for j in range(CHUNK):
            oht[:, j * 128:(j + 1) * 128] = onehot_cols(col[pl.ds(c * CHUNK + j, 1), :])
        res = jnp.dot(gt[...], oht[...], preferred_element_type=f32)
        for j in range(CHUNK):
            row = pl.ds(c * CHUNK + j, 1)
            at = slice(j * 128, (j + 1) * 128)
            both = res[0:128, at] + res[128:256, at]
            here = iota((DEP, 128), 0) == dep[row, :]
            out[row, :] = jnp.sum(jnp.where(here, both, 0.0), axis=0, keepdims=True) * w[row, :]
        return carry

    lax.fori_loop(0, (n + CHUNK - 1) // CHUNK, body, 0)


def place_of(slot_info):
    return jnp.where(iota((SLOTS, SLOTS), 0) == slot_info, 1.0, 0.0)


def to_rays(partial, place, rays):
    row = jnp.sum(place * partial, axis=0, keepdims=True)
    total = jnp.zeros((RAYS, NDEV), f32)
    for k in range(2):
        at = slice(k * 128, (k + 1) * 128)
        total += jnp.where(iota((RAYS, NDEV), 0) == rays[:, at], row[:, at], 0.0)
    return total


def from_rays(values, place, rays):
    rows = [
        jnp.sum(jnp.where(iota((RAYS, NDEV), 0) == rays[:, k * 128:(k + 1) * 128], values, 0.0), axis=0, keepdims=True)
        for k in range(2)
    ]
    return jnp.sum(place * jnp.concatenate(rows, axis=1), axis=1, keepdims=True)


def first_kernel(held, q_out, p_out, col, dep, w, info, count, oht, vt, acc, gt, wy):
    meta = held[:, 4, :].T
    y_row = jnp.concatenate([meta[0:1, :], meta[1:2, :]], axis=1)
    ray_row = jnp.concatenate([meta[2:3, :], meta[3:4, :]], axis=1).astype(i32) - 1
    live = ray_row >= 0
    flags = jnp.broadcast_to(jnp.where(live, 1.0, 0.0), (8, SLOTS)).astype(bf16)
    before = jnp.where(iota((SLOTS, SLOTS), 0) < iota((SLOTS, SLOTS), 1), 1.0, 0.0).astype(bf16)
    at = jnp.dot(flags, before, preferred_element_type=f32)[0:1, :].astype(i32)
    at = jnp.where(live, at, -1)
    info[0:1, :] = at
    info[1:2, :] = ray_row
    n = jnp.sum(jnp.where(live, 1.0, 0.0)).astype(i32)
    count[0] = n
    place = place_of(at)
    pay = jnp.concatenate([as_payload(held[:, k, :].astype(i32), held[:, 2 + k, :]) for k in range(2)], axis=0)
    z, c, lens = from_payload(jnp.dot(place.astype(bf16), pay, preferred_element_type=f32))
    col[...] = c.astype(i32)
    dep[...] = z.astype(i32)
    w[...] = lens
    wy[...] = lens * jnp.sum(place * y_row, axis=1, keepdims=True)
    scatter_into(acc, n, col, dep, wy, oht, vt)
    q = acc[:, 0:128] + acc[:, 128:256]
    q_out[...] = q
    gather_from(q, n, col, dep, w, wy, oht, gt)
    p_out[...] = to_rays(jnp.sum(wy[...], axis=1, keepdims=True), place, ray_row)


def second_kernel(p, smooth, col, dep, w, info, count, q_out, p_out, oht, vt, acc, gt, wy):
    n = count[0]
    place = place_of(info[0:1, :])
    ray_row = info[1:2, :]
    wy[...] = w[...] * from_rays(p[...], place, ray_row)
    scatter_into(acc, n, col, dep, wy, oht, vt)
    q = acc[:, 0:128] + acc[:, 128:256] + smooth[...]
    q_out[...] = q
    gather_from(q, n, col, dep, w, wy, oht, gt)
    p_out[...] = to_rays(jnp.sum(wy[...], axis=1, keepdims=True), place, ray_row)


def shape(dims, dtype=f32):
    return jax.ShapeDtypeStruct(dims, dtype)


SCRATCH = [
    pltpu.VMEM((COLS, CHUNK * 128), bf16),
    pltpu.VMEM((256, CHUNK * 128), bf16),
    pltpu.VMEM((COLS, 256), f32),
    pltpu.VMEM((256, COLS), bf16),
    pltpu.VMEM((SLOTS, SEG), f32),
]


def padded(array, sides, width, wrap):
    for axis, dim in sides:
        devices, length = (lax.axis_size(axis), array.shape[dim])
        up = [(i, (i + 1) % devices) for i in range(devices if wrap else devices - 1)]
        down = [(j, i) for i, j in up]
        last = lax.slice_in_dim(array, length - width, length, axis=dim)
        leading = lax.slice_in_dim(array, 0, width, axis=dim)
        before = lax.ppermute(last, axis, up)
        after = lax.ppermute(leading, axis, down)
        array = jnp.concatenate([before, array, after], axis=dim)
    return array


def smoothing(flat):
    field = flat.reshape(CLON, CLAT, DEP)
    lon_pad = padded(field, ((LON, 0),), 1, True)
    lat_pad = padded(field, ((LAT, 1),), 1, False)
    dep_pad = jnp.pad(field, ((0, 0), (0, 0), (1, 1)))
    result = 6.0 * field - lon_pad[2:] - lon_pad[:-2] - lat_pad[:, 2:] - lat_pad[:, :-2]
    return (result - dep_pad[:, :, 2:] - dep_pad[:, :, :-2]).reshape(COLS, DEP)


def shards(travel_times, ray_counts, tile_brick, cell_offsets, cell_depths, seg_lengths):
    live_mask = (jnp.arange(RAYS, dtype=i32) < ray_counts[0]).astype(f32)
    send = pl.pallas_call(
        pack_kernel,
        out_shape=shape((NDEV, 5, SEG)),
        in_specs=[SMEM] + [VMEM] * 5,
        out_specs=VMEM,
        scratch_shapes=[pltpu.VMEM((128, 768), bf16)],
        compiler_params=PARAMS,
    )(ray_counts, tile_brick, travel_times.reshape(1, RAYS), cell_offsets, cell_depths, seg_lengths)
    held = lax.all_to_all(send, LON_LAT, split_axis=0, concat_axis=0, tiled=True)
    q0, p_part, col, dep, w, info, count = pl.pallas_call(
        first_kernel,
        out_shape=(shape((COLS, DEP)), shape((RAYS, NDEV)), shape((SLOTS, SEG), i32), shape((SLOTS, SEG), i32),
                   shape((SLOTS, SEG)), shape((2, SLOTS), i32), shape((1,), i32)),
        in_specs=[VMEM],
        out_specs=(VMEM,) * 6 + (SMEM,),
        scratch_shapes=SCRATCH,
        compiler_params=PARAMS,
    )(held)
    p0 = lax.psum(p_part, LON_LAT)
    g0 = DAMP * smoothing(q0)
    smooth = DAMP * smoothing(g0)
    q1, p_part = pl.pallas_call(
        second_kernel,
        out_shape=(shape((COLS, DEP)), shape((RAYS, NDEV))),
        in_specs=[VMEM] * 6 + [SMEM],
        out_specs=(VMEM,) * 2,
        scratch_shapes=SCRATCH,
        compiler_params=PARAMS,
    )(p0, smooth, col, dep, w, info, count)
    g1 = DAMP * smoothing(q1)
    dots = jnp.stack([jnp.sum(q0 * q0), jnp.sum(g0 * g0), jnp.sum(q1 * q1), jnp.sum(g1 * g1)])
    row = jnp.concatenate([dots, jnp.zeros((NDEV - 4,), f32)])
    both = lax.psum(jnp.concatenate([p_part, row[None, :]], axis=0), LON_LAT)
    p1 = both[:RAYS]
    m0 = both[RAYS, 0]
    m1 = both[RAYS, 1] + jnp.sum(p0 * p0)
    m2 = both[RAYS, 2]
    m3 = both[RAYS, 3] + jnp.sum(p1 * p1)
    r1, r2, r3 = m1 / m0, m2 / m1, m3 / m2
    c0 = (r3 - r1) / (r3 - r2) / r1
    c1 = (r1 - r2) / (r3 - r2) / (r1 * r2)
    model = SCALE * (c0 * q0 + c1 * q1)
    me = lax.axis_index(LON_LAT)
    mine = lambda p: lax.dynamic_slice_in_dim(p, me, 1, axis=1)[:, 0]
    misfit = travel_times * live_mask - c0 * mine(p0) - c1 * mine(p1)
    return (model.reshape(CLON, CLAT, DEP), misfit)


def solution(mesh):
    torus = Mesh(mesh.devices.reshape(4, 2, 4, 4), LON_LAT)
    in_specs = (
        P(LON_LAT),
        P(LON_LAT),
        P(LON_LAT, None),
        P(LON_LAT, None, None),
        P(LON_LAT, None, None),
        P(LON_LAT, None, None),
    )
    out_specs = (P(LON, LAT, None), P(LON_LAT))
    return jax.shard_map(shards, mesh=torus, in_specs=in_specs, out_specs=out_specs, check_vma=False)
```

```python
import itertools

import jax
import jax.numpy as jnp
from jax import lax
from jax.experimental import pallas as pl
from jax.experimental.pallas import tpu as pltpu
from jax.sharding import Mesh
from jax.sharding import PartitionSpec as P

CLON, CLAT, DEP, SEG = 32, 32, 128, 128
COLS = CLON * CLAT
RAYS, TPR = 32, 4
NDEV = 128
SLOTS = 2 * NDEV
CHUNK = 8
SCALE = 8.0
DAMP = 0.01 * SCALE
LON_LAT = ("lon_0", "lon_1", "lat_0", "lat_1")
LON = ("lon_0", "lon_1")
LAT = ("lat_0", "lat_1")

f32, bf16, i32 = jnp.float32, jnp.bfloat16, jnp.int32
VMEM = pl.BlockSpec(memory_space=pltpu.VMEM)
SMEM = pl.BlockSpec(memory_space=pltpu.SMEM)
PARAMS = pltpu.CompilerParams(vmem_limit_bytes=48 << 20)


def iota(shape, dim):
    return lax.broadcasted_iota(i32, shape, dim)


def split2(x):
    hi = x.astype(bf16)
    return hi, (x - hi.astype(f32)).astype(bf16)


def split3(x):
    hi = x.astype(bf16)
    rest = x - hi.astype(f32)
    mid = rest.astype(bf16)
    return hi, mid, (rest - mid.astype(f32)).astype(bf16)


def as_payload(cell, lens):
    col = cell >> 7
    parts = [(cell & 127), (col & 127), (col >> 7)]
    return jnp.concatenate([p.astype(f32).astype(bf16) for p in parts] + list(split3(lens)), axis=1)


def from_payload(rows):
    z, low, high, hi, mid, lo = [rows[:, k * 128:(k + 1) * 128] for k in range(6)]
    return z, high * 128.0 + low, (hi + mid) + lo


def pack_kernel(count, brick, times, offs, deps, lens, out, pay):
    lane = iota((RAYS, 128), 1)
    mine = iota((RAYS, 128), 0) == (lane & 31)
    tb = brick[...]
    wide = jnp.zeros((RAYS, 128), i32)
    for k in range(TPR):
        wide = jnp.where((lane >> 5) == k, tb[:, k:k + 1], wide)
    brick_row = jnp.sum(jnp.where(mine, wide, 0).astype(f32), axis=0, keepdims=True)
    time_row = jnp.concatenate([times[...]] * TPR, axis=1)
    ray_row = iota((1, 128), 1) & 31
    live = ray_row < count[0]
    as_rows = jnp.broadcast_to(brick_row, (128, 128))
    same = (as_rows == as_rows.T) & (iota((128, 128), 0) < iota((128, 128), 1))
    rank_row = jnp.sum(jnp.where(same, 1.0, 0.0), axis=0, keepdims=True)
    for k in range(TPR):
        cell = offs[:, k, :] * DEP + deps[:, k, :]
        pay[k * RAYS:(k + 1) * RAYS, :] = as_payload(cell, lens[:, k, :] * SCALE)
    target = iota((128, 128), 0).astype(f32)
    meta = jnp.zeros((128, 128), f32)
    lanes = iota((128, 128), 1)
    for k in range(2):
        picked = jnp.where((target == brick_row) & (rank_row == k) & live, 1.0, 0.0)
        z, col, w = from_payload(jnp.dot(picked.astype(bf16), pay[...], preferred_element_type=f32))
        out[:, k, :] = col * 128.0 + z
        out[:, 2 + k, :] = w
        value = jnp.sum(picked * time_row, axis=1, keepdims=True)
        ray = jnp.sum(picked * (ray_row + 1).astype(f32), axis=1, keepdims=True)
        meta = jnp.where(lanes == k, value, jnp.where(lanes == 2 + k, ray, meta))
    out[:, 4, :] = meta


def onehot_cols(col_row):
    at = jnp.broadcast_to(col_row.astype(jnp.int16), (COLS, 128))
    return jnp.where(lax.broadcasted_iota(jnp.int16, (COLS, 128), 0) == at, jnp.ones((), bf16), jnp.zeros((), bf16))


def scatter_into(acc, n, col, dep, wy, oht, vt):
    acc[...] = jnp.zeros_like(acc)

    def body(c, carry):
        for j in range(CHUNK):
            row = pl.ds(c * CHUNK + j, 1)
            at = slice(j * 128, (j + 1) * 128)
            oht[:, at] = onehot_cols(col[row, :])
            w = wy[row, :]
            hi = w.astype(bf16).astype(f32)
            here = iota((DEP, 128), 0) == dep[row, :]
            vt[0:128, at] = jnp.where(here, hi, 0.0).astype(bf16)
            vt[128:256, at] = jnp.where(here, w - hi, 0.0).astype(bf16)
        acc[...] += lax.dot_general(oht[...], vt[...], (((1,), (1,)), ((), ())), preferred_element_type=f32)
        return carry

    lax.fori_loop(0, (n + CHUNK - 1) // CHUNK, body, 0)


def gather_from(grid, n, col, dep, w, out, oht, gt):
    hi, lo = split2(grid.T)
    gt[0:128, :] = hi
    gt[128:256, :] = lo
    out[...] = jnp.zeros_like(out)

    def body(c, carry):
        for j in range(CHUNK):
            oht[:, j * 128:(j + 1) * 128] = onehot_cols(col[pl.ds(c * CHUNK + j, 1), :])
        res = jnp.dot(gt[...], oht[...], preferred_element_type=f32)
        for j in range(CHUNK):
            row = pl.ds(c * CHUNK + j, 1)
            at = slice(j * 128, (j + 1) * 128)
            both = res[0:128, at] + res[128:256, at]
            here = iota((DEP, 128), 0) == dep[row, :]
            out[row, :] = jnp.sum(jnp.where(here, both, 0.0), axis=0, keepdims=True) * w[row, :]
        return carry

    lax.fori_loop(0, (n + CHUNK - 1) // CHUNK, body, 0)


def place_of(slot_info):
    return jnp.where(iota((SLOTS, SLOTS), 0) == slot_info, 1.0, 0.0)


def to_rays(partial, place, rays):
    row = jnp.sum(place * partial, axis=0, keepdims=True)
    total = jnp.zeros((RAYS, NDEV), f32)
    for k in range(2):
        at = slice(k * 128, (k + 1) * 128)
        total += jnp.where(iota((RAYS, NDEV), 0) == rays[:, at], row[:, at], 0.0)
    return total


def from_rays(values, place, rays):
    rows = [
        jnp.sum(jnp.where(iota((RAYS, NDEV), 0) == rays[:, k * 128:(k + 1) * 128], values, 0.0), axis=0, keepdims=True)
        for k in range(2)
    ]
    return jnp.sum(place * jnp.concatenate(rows, axis=1), axis=1, keepdims=True)


def first_kernel(held, q_out, p_out, col, dep, w, info, count, oht, vt, acc, gt, wy):
    meta = held[:, 4, :].T
    y_row = jnp.concatenate([meta[0:1, :], meta[1:2, :]], axis=1)
    ray_row = jnp.concatenate([meta[2:3, :], meta[3:4, :]], axis=1).astype(i32) - 1
    live = ray_row >= 0
    flags = jnp.broadcast_to(jnp.where(live, 1.0, 0.0), (8, SLOTS)).astype(bf16)
    before = jnp.where(iota((SLOTS, SLOTS), 0) < iota((SLOTS, SLOTS), 1), 1.0, 0.0).astype(bf16)
    at = jnp.dot(flags, before, preferred_element_type=f32)[0:1, :].astype(i32)
    at = jnp.where(live, at, -1)
    info[0:1, :] = at
    info[1:2, :] = ray_row
    n = jnp.sum(jnp.where(live, 1.0, 0.0)).astype(i32)
    count[0] = n
    place = place_of(at)
    pay = jnp.concatenate([as_payload(held[:, k, :].astype(i32), held[:, 2 + k, :]) for k in range(2)], axis=0)
    z, c, lens = from_payload(jnp.dot(place.astype(bf16), pay, preferred_element_type=f32))
    col[...] = c.astype(i32)
    dep[...] = z.astype(i32)
    w[...] = lens
    wy[...] = lens * jnp.sum(place * y_row, axis=1, keepdims=True)
    scatter_into(acc, n, col, dep, wy, oht, vt)
    q = acc[:, 0:128] + acc[:, 128:256]
    q_out[...] = q
    gather_from(q, n, col, dep, w, wy, oht, gt)
    p_out[...] = to_rays(jnp.sum(wy[...], axis=1, keepdims=True), place, ray_row)


def second_kernel(p, smooth, col, dep, w, info, count, q_out, p_out, oht, vt, acc, gt, wy):
    n = count[0]
    place = place_of(info[0:1, :])
    ray_row = info[1:2, :]
    wy[...] = w[...] * from_rays(p[...], place, ray_row)
    scatter_into(acc, n, col, dep, wy, oht, vt)
    q = acc[:, 0:128] + acc[:, 128:256] + smooth[...]
    q_out[...] = q
    gather_from(q, n, col, dep, w, wy, oht, gt)
    p_out[...] = to_rays(jnp.sum(wy[...], axis=1, keepdims=True), place, ray_row)


def shape(dims, dtype=f32):
    return jax.ShapeDtypeStruct(dims, dtype)


SCRATCH = [
    pltpu.VMEM((COLS, CHUNK * 128), bf16),
    pltpu.VMEM((256, CHUNK * 128), bf16),
    pltpu.VMEM((COLS, 256), f32),
    pltpu.VMEM((256, COLS), bf16),
    pltpu.VMEM((SLOTS, SEG), f32),
]


MESH = pl.DeviceIdType.MESH
SIZES = (4, 2, 4, 4)
STAGES = ((1, 0), (2,), (3,))
PEERS = max(len(list(itertools.product(*[range(SIZES[a]) for a in g]))) for g in STAGES) - 1


def coords():
    return tuple(lax.axis_index(a) for a in LON_LAT)


def stage_peers(here, group):
    found = []
    for steps in itertools.product(*[range(SIZES[a]) for a in group]):
        if any(steps):
            add = dict(zip(group, steps))
            found.append(tuple((v + add.get(i, 0)) % SIZES[i] for i, v in enumerate(here)))
    return found


def ring_peers(here):
    lon, lat = here[0] * 2 + here[1], here[2] * 4 + here[3]
    found = []
    for step in (1, 7):
        to = (lon + step) % 8
        found.append((to // 2, to % 2, here[2], here[3]))
    for step in (1, 15):
        to = (lat + step) % 16
        found.append((here[0], here[1], to // 4, to % 4))
    return found


def meet(here):
    barrier = pltpu.get_barrier_semaphore()
    peers = [p for g in STAGES for p in stage_peers(here, g)] + ring_peers(here)
    for peer in peers:
        pl.semaphore_signal(barrier, inc=1, device_id=peer, device_id_type=MESH)
    pl.semaphore_wait(barrier, len(peers))


def send_stage(s, here, buf, got, send_sem, recv_sem):
    copies = []
    for k, peer in enumerate(stage_peers(here, STAGES[s])):
        copy = pltpu.make_async_remote_copy(
            buf.at[s], got.at[s, k], send_sem.at[s, k], recv_sem.at[s, k], device_id=peer, device_id_type=MESH)
        copy.start()
        copies.append(copy)
    return copies


def add_stage(s, copies, buf, got):
    total = buf[s]
    for k, copy in enumerate(copies):
        copy.wait_recv()
        total = total + got[s, k]
    return total


def send_halo(here, field, edge, halo, send_sem, recv_sem):
    edge[0] = field[pl.ds(CLAT - 1, CLON, stride=CLAT), :]
    edge[1] = field[pl.ds(0, CLON, stride=CLAT), :]
    faces = (field.at[pl.ds(COLS - CLAT, CLAT)], field.at[pl.ds(0, CLAT)], edge.at[0], edge.at[1])
    copies = []
    for k, (face, peer) in enumerate(zip(faces, ring_peers(here))):
        copy = pltpu.make_async_remote_copy(
            face, halo.at[k], send_sem.at[k], recv_sem.at[k], device_id=peer, device_id_type=MESH)
        copy.start()
        copies.append(copy)
    return copies


def stencil_rows(here, field, halo, put):
    lat = here[2] * 4 + here[3]
    has_before = jnp.where(lat > 0, 1.0, 0.0)
    has_after = jnp.where(lat < 15, 1.0, 0.0)
    row, lane = iota((CLAT, DEP), 0), iota((CLAT, DEP), 1)

    def layer(i, before, after):
        mine = pl.ds(pl.multiple_of(i * CLAT, CLAT), CLAT)
        f = field[mine, :]
        lat_before = jnp.where(row == 0, halo[2, pl.ds(i, 1), :] * has_before, pltpu.roll(f, 1, 0))
        lat_after = jnp.where(row == CLAT - 1, halo[3, pl.ds(i, 1), :] * has_after, pltpu.roll(f, CLAT - 1, 0))
        up = jnp.where(lane == 0, 0.0, pltpu.roll(f, 1, 1))
        down = jnp.where(lane == DEP - 1, 0.0, pltpu.roll(f, DEP - 1, 1))
        put(mine, DAMP * (6.0 * f - before - after - lat_before - lat_after - up - down))

    def inner(i, carry):
        layer(i, field[pl.ds(pl.multiple_of((i - 1) * CLAT, CLAT), CLAT), :],
              field[pl.ds(pl.multiple_of((i + 1) * CLAT, CLAT), CLAT), :])
        return carry

    layer(0, halo[0], field[CLAT:2 * CLAT, :])
    layer(CLON - 1, field[COLS - 2 * CLAT:COLS - CLAT, :], halo[1])
    lax.fori_loop(1, CLON - 1, inner, 0)


def finish(copies):
    for copy in copies:
        copy.wait_send()


def middle_kernel(p_part, q, p_out, smooth, buf, got, g, edge, halo, send_sem, recv_sem, face_send, face_recv):
    here = coords()
    meet(here)
    buf[0] = p_part[...]
    first = send_stage(0, here, buf, got, send_sem, recv_sem)
    faces = send_halo(here, q, edge.at[0], halo.at[0], face_send.at[0], face_recv.at[0])
    buf[1] = add_stage(0, first, buf, got)
    second = send_stage(1, here, buf, got, send_sem, recv_sem)
    for copy in faces:
        copy.wait_recv()

    def to_g(rows, value):
        g[rows, :] = value

    stencil_rows(here, q, halo.at[0], to_g)
    more = send_halo(here, g, edge.at[1], halo.at[1], face_send.at[1], face_recv.at[1])
    buf[2] = add_stage(1, second, buf, got)
    third = send_stage(2, here, buf, got, send_sem, recv_sem)
    for copy in more:
        copy.wait_recv()

    def to_smooth(rows, value):
        smooth[rows, :] = value

    stencil_rows(here, g, halo.at[1], to_smooth)
    p_out[...] = add_stage(2, third, buf, got)
    finish(first + second + third + faces + more)


def last_kernel(count, times, p_part, p0, q0, q1, model, misfit, buf, got, norm, edge, halo, send_sem, recv_sem,
                face_send, face_recv):
    here = coords()
    meet(here)
    faces = send_halo(here, q1, edge, halo, face_send, face_recv)
    buf[0, 0:RAYS, :] = p_part[...]
    a, b = q0[...], q1[...]
    dots = [jnp.sum(jnp.sum(x, axis=0, keepdims=True), axis=1, keepdims=True) for x in (a * a, a * b, b * b)]
    norm[...] = jnp.zeros_like(norm)
    for copy in faces:
        copy.wait_recv()

    def to_norm(rows, value):
        norm[...] += value * value

    stencil_rows(here, q1, halo, to_norm)
    dots.append(jnp.sum(jnp.sum(norm[...], axis=0, keepdims=True), axis=1, keepdims=True))
    lane = iota((8, NDEV), 1)
    row = jnp.zeros((8, NDEV), f32)
    for k, dot in enumerate(dots):
        row = jnp.where(lane == k, dot, row)
    buf[0, RAYS:RAYS + 8, :] = row
    sent = []
    for s in range(len(STAGES)):
        copies = send_stage(s, here, buf, got, send_sem, recv_sem)
        total = add_stage(s, copies, buf, got)
        buf[s + 1] = total
        sent += copies
    p1 = total[0:RAYS, :]
    m0, m1, m2, m3 = [total[RAYS:RAYS + 1, k:k + 1] for k in range(4)]
    m3 = m3 + jnp.sum(jnp.sum(p1 * p1, axis=0, keepdims=True), axis=1, keepdims=True)
    r1, r2, r3 = m1 / m0, m2 / m1, m3 / m2
    c0 = (r3 - r1) / (r3 - r2) / r1
    c1 = (r1 - r2) / (r3 - r2) / (r1 * r2)
    model[...] = (SCALE * c0) * a + (SCALE * c1) * b
    me = ((here[0] * 2 + here[1]) * 4 + here[2]) * 4 + here[3]
    fit = jnp.where(iota((RAYS, NDEV), 1) == me, c0 * p0[...] + c1 * p1, 0.0)
    column = jnp.sum(fit, axis=1, keepdims=True)
    own = jnp.sum(jnp.where(iota((RAYS, RAYS), 0) == iota((RAYS, RAYS), 1), column, 0.0), axis=0, keepdims=True)
    data = jnp.where(iota((1, RAYS), 1) < count[0], times[...], 0.0)
    misfit[...] = data - own
    finish(faces + sent)


def comm_scratch(rows, faces):
    return [
        pltpu.VMEM((len(STAGES) + 1, rows, NDEV), f32),
        pltpu.VMEM((len(STAGES), PEERS, rows, NDEV), f32),
    ], [
        pltpu.VMEM(faces + (2, CLON, DEP), f32),
        pltpu.VMEM(faces + (4, CLON, DEP), f32),
        pltpu.SemaphoreType.DMA((len(STAGES), PEERS)),
        pltpu.SemaphoreType.DMA((len(STAGES), PEERS)),
        pltpu.SemaphoreType.DMA(faces + (4,)),
        pltpu.SemaphoreType.DMA(faces + (4,)),
    ]


def comm_params(number):
    return pltpu.CompilerParams(vmem_limit_bytes=16 << 20, collective_id=number, has_side_effects=True)


def shards(travel_times, ray_counts, tile_brick, cell_offsets, cell_depths, seg_lengths):
    times = travel_times.reshape(1, RAYS)
    send = pl.pallas_call(
        pack_kernel,
        out_shape=shape((NDEV, 5, SEG)),
        in_specs=[SMEM] + [VMEM] * 5,
        out_specs=VMEM,
        scratch_shapes=[pltpu.VMEM((128, 768), bf16)],
        compiler_params=PARAMS,
    )(ray_counts, tile_brick, times, cell_offsets, cell_depths, seg_lengths)
    held = lax.all_to_all(send, LON_LAT, split_axis=0, concat_axis=0, tiled=True)
    q0, p_part, col, dep, w, info, count = pl.pallas_call(
        first_kernel,
        out_shape=(shape((COLS, DEP)), shape((RAYS, NDEV)), shape((SLOTS, SEG), i32), shape((SLOTS, SEG), i32),
                   shape((SLOTS, SEG)), shape((2, SLOTS), i32), shape((1,), i32)),
        in_specs=[VMEM],
        out_specs=(VMEM,) * 6 + (SMEM,),
        scratch_shapes=SCRATCH,
        compiler_params=PARAMS,
    )(held)
    bufs, faces = comm_scratch(RAYS, (2,))
    p0, smooth = pl.pallas_call(
        middle_kernel,
        out_shape=(shape((RAYS, NDEV)), shape((COLS, DEP))),
        in_specs=[VMEM] * 2,
        out_specs=(VMEM,) * 2,
        scratch_shapes=bufs + [pltpu.VMEM((COLS, DEP), f32)] + faces,
        compiler_params=comm_params(0),
    )(p_part, q0)
    q1, p_part = pl.pallas_call(
        second_kernel,
        out_shape=(shape((COLS, DEP)), shape((RAYS, NDEV))),
        in_specs=[VMEM] * 6 + [SMEM],
        out_specs=(VMEM,) * 2,
        scratch_shapes=SCRATCH,
        compiler_params=PARAMS,
    )(p0, smooth, col, dep, w, info, count)
    bufs, faces = comm_scratch(RAYS + 8, ())
    model, misfit = pl.pallas_call(
        last_kernel,
        out_shape=(shape((COLS, DEP)), shape((1, RAYS))),
        in_specs=[SMEM] + [VMEM] * 5,
        out_specs=(VMEM,) * 2,
        scratch_shapes=bufs + [pltpu.VMEM((CLAT, DEP), f32)] + faces,
        compiler_params=comm_params(1),
    )(ray_counts, times, p_part, p0, q0, q1)
    return (model.reshape(CLON, CLAT, DEP), misfit.reshape(RAYS))


def solution(mesh):
    torus = Mesh(mesh.devices.reshape(4, 2, 4, 4), LON_LAT)
    in_specs = (
        P(LON_LAT),
        P(LON_LAT),
        P(LON_LAT, None),
        P(LON_LAT, None, None),
        P(LON_LAT, None, None),
        P(LON_LAT, None, None),
    )
    out_specs = (P(LON, LAT, None), P(LON_LAT))
    return jax.shard_map(shards, mesh=torus, in_specs=in_specs, out_specs=out_specs, check_vma=False)
```

```python
import itertools

import jax
import jax.numpy as jnp
from jax import lax
from jax.experimental import pallas as pl
from jax.experimental.pallas import tpu as pltpu
from jax.sharding import Mesh
from jax.sharding import PartitionSpec as P

CLON, CLAT, DEP, SEG = 32, 32, 128, 128
COLS = CLON * CLAT
RAYS, TPR = 32, 4
NDEV = 128
SLOTS = 2 * NDEV
CHUNK = 8
BLOCKS, BLOCK, HALF = 4, 256, 64
SCALE = 8.0
DAMP = 0.01 * SCALE
LON_LAT = ("lon_0", "lon_1", "lat_0", "lat_1")
LON = ("lon_0", "lon_1")
LAT = ("lat_0", "lat_1")

f32, bf16, i32, i16 = jnp.float32, jnp.bfloat16, jnp.int32, jnp.int16
VMEM = pl.BlockSpec(memory_space=pltpu.VMEM)
SMEM = pl.BlockSpec(memory_space=pltpu.SMEM)
PARAMS = pltpu.CompilerParams(vmem_limit_bytes=48 << 20)


def iota(shape, dim):
    return lax.broadcasted_iota(i32, shape, dim)


def split2(x):
    hi = x.astype(bf16)
    return hi, (x - hi.astype(f32)).astype(bf16)


def split3(x):
    hi = x.astype(bf16)
    rest = x - hi.astype(f32)
    mid = rest.astype(bf16)
    return hi, mid, (rest - mid.astype(f32)).astype(bf16)


def as_payload(cell, lens):
    col = cell >> 7
    parts = [(cell & 127), (col & 127), (col >> 7)]
    return jnp.concatenate([p.astype(f32).astype(bf16) for p in parts] + list(split3(lens)), axis=1)


def from_payload(rows):
    z, low, high, hi, mid, lo = [rows[:, k * 128:(k + 1) * 128] for k in range(6)]
    return z, high * 128.0 + low, (hi + mid) + lo


def pack_kernel(count, brick, times, offs_in, deps_in, lens_in, out, pay, offs, deps, lens, sem):
    loads = [
        pltpu.make_async_copy(src, dst, sem.at[k])
        for k, (src, dst) in enumerate(((offs_in, offs), (deps_in, deps), (lens_in, lens)))
    ]
    for load in loads:
        load.start()
    tb = brick[...].astype(f32)
    brick_row = jnp.concatenate([tb[k:k + 1, :] for k in range(TPR)], axis=1)
    time_row = jnp.concatenate([times[...]] * TPR, axis=1)
    ray_row = iota((1, 128), 1) & 31
    live = ray_row < count[0]
    as_rows = jnp.broadcast_to(brick_row, (128, 128))
    same = (as_rows == as_rows.T) & (iota((128, 128), 0) < iota((128, 128), 1))
    rank_row = jnp.sum(jnp.where(same, 1.0, 0.0), axis=0, keepdims=True)
    for load in loads:
        load.wait()
    for k in range(TPR):
        cell = offs[:, k, :] * DEP + deps[:, k, :]
        pay[k * RAYS:(k + 1) * RAYS, :] = as_payload(cell, lens[:, k, :] * SCALE)
    target = iota((128, 128), 0).astype(f32)
    meta = jnp.zeros((128, 128), f32)
    lanes = iota((128, 128), 1)
    for k in range(2):
        picked = jnp.where((target == brick_row) & (rank_row == k) & live, 1.0, 0.0)
        z, col, w = from_payload(jnp.dot(picked.astype(bf16), pay[...], preferred_element_type=f32))
        out[:, k, :] = col * 128.0 + z
        out[:, 2 + k, :] = w
        value = jnp.sum(picked * time_row, axis=1, keepdims=True)
        ray = jnp.sum(picked * (ray_row + 1).astype(f32), axis=1, keepdims=True)
        meta = jnp.where(lanes == k, value, jnp.where(lanes == 2 + k, ray, meta))
    out[:, 4, :] = meta


def onehot_cols(col_row):
    at = jnp.broadcast_to(col_row.astype(i16), (BLOCK, 128))
    return jnp.where(lax.broadcasted_iota(i16, (BLOCK, 128), 0) == at, jnp.ones((), bf16), jnp.zeros((), bf16))


def onehot_values(dep_row, val_row):
    at = jnp.broadcast_to(dep_row.astype(i16), (DEP, 128))
    here = lax.broadcasted_iota(i16, (DEP, 128), 0) == at
    return jnp.concatenate(
        [jnp.where(here, jnp.broadcast_to(part, (DEP, 128)), jnp.zeros((), bf16)) for part in split2(val_row)], axis=0)


def scatter_rows(acc, chunks, col, dep, val):
    acc[...] = jnp.zeros_like(acc)

    def body(c, carry):
        rows = [pl.ds(c * CHUNK + j, 1) for j in range(CHUNK)]
        for b in range(BLOCKS):
            left = jnp.concatenate([onehot_cols(col(b, r)) for r in rows], axis=1)
            right = jnp.concatenate([onehot_values(dep(b, r), val(b, r)) for r in rows], axis=1)
            acc[b] += lax.dot_general(left, right, (((1,), (1,)), ((), ())), preferred_element_type=f32)
        return carry

    lax.fori_loop(0, chunks, body, 0)


def gather_rows(gt, chunks, col, dep, w, out):
    out[...] = jnp.zeros_like(out)

    def body(c, carry):
        rows = [pl.ds(c * CHUNK + j, 1) for j in range(CHUNK)]
        sums = [jnp.zeros((8, 128), f32)] * CHUNK
        for b in range(BLOCKS):
            right = jnp.concatenate([onehot_cols(col(b, r)) for r in rows], axis=1)
            res = jnp.dot(gt[:, b * BLOCK:(b + 1) * BLOCK], right, preferred_element_type=f32)
            for j, r in enumerate(rows):
                at = slice(j * 128, (j + 1) * 128)
                both = res[0:128, at] + res[128:256, at]
                here = jnp.where(iota((DEP, 128), 0) == dep(b, r), both, 0.0)
                sums[j] = sums[j] + here.reshape(16, 8, 128).sum(axis=0) * w(b, r)
        for j, r in enumerate(rows):
            out[r, :] = jnp.sum(sums[j], axis=0, keepdims=True)
        return carry

    lax.fori_loop(0, chunks, body, 0)


def pair(x):
    x = x.reshape(16, 16, 128)
    return jnp.where(iota((16, 8, 128), 2) < HALF, x[:, 0:8], x[:, 8:16]).reshape(128, 128)


def unpair(x):
    low = iota((128, 128), 1) < HALF
    halves = [jnp.sum(jnp.where(m, x, 0.0), axis=1, keepdims=True) for m in (low, ~low)]
    return jnp.concatenate([h.reshape(16, 8, 1) for h in halves], axis=1).reshape(SLOTS, 1)


def take(x, index):
    return jnp.take_along_axis(x, index, axis=1, mode="promise_in_bounds")


def bucket(n, col, dep, w, bcol, bdep, bw):
    upto = jnp.where(iota((128, 128), 0) <= iota((128, 128), 1), 1.0, 0.0).astype(bf16)
    rank = iota((SLOTS, 128), 1) & (HALF - 1)
    most = jnp.zeros((SLOTS, 1), i32)
    for b in range(BLOCKS):
        inside = jnp.where((col >> 8) == b, 1.0, 0.0).astype(bf16)
        counts = jnp.dot(inside, upto, preferred_element_type=f32).astype(i32)
        at = jnp.zeros((SLOTS, 128), i32)
        for step in (64, 32, 16, 8, 4, 2, 1):
            at = jnp.where(take(counts, at + (step - 1)) <= rank, at + step, at)
        held = counts[:, 127:128]
        bcol[b] = pair(take(col, at) - b * BLOCK)
        bdep[b] = pair(take(dep, at))
        bw[b] = pair(jnp.where(rank < held, take(w, at), 0.0))
        most = jnp.maximum(most, held)
    most = jnp.where(iota((SLOTS, 1), 0) < n, most, 0)
    return jnp.max(most.astype(f32)).astype(i32)


def both_passes(n, most, y_col, col, dep, w, bcol, bdep, bw, extra, q_out, acc, gt, wy, vals, part):
    fits = most <= HALF

    def whole():
        q = jnp.concatenate([acc[b, :, 0:128] + acc[b, :, 128:256] for b in range(BLOCKS)], axis=0)
        if extra is not None:
            q = q + extra[...]
        q_out[...] = q
        hi, lo = split2(q.T)
        gt[0:128, :] = hi
        gt[128:256, :] = lo

    @pl.when(fits)
    def _():
        chunks = (n + 2 * CHUNK - 1) // (2 * CHUNK)
        y = pair(jnp.broadcast_to(y_col, (SLOTS, 128)))
        for b in range(BLOCKS):
            wy[b] = bw[b] * y
        cols, deps = (lambda b, r: bcol[b, r, :]), (lambda b, r: bdep[b, r, :])
        scatter_rows(acc, chunks, cols, deps, lambda b, r: wy[b, r, :])
        whole()
        gather_rows(gt, chunks, cols, deps, lambda b, r: bw[b, r, :], vals.at[pl.ds(0, 128)])
        part[...] = unpair(vals[0:128, :])

    @pl.when(jnp.logical_not(fits))
    def _():
        chunks = (n + CHUNK - 1) // CHUNK
        vals[...] = w[...] * y_col
        cols, deps = (lambda b, r: col[r, :] - b * BLOCK), (lambda b, r: dep[r, :])
        scatter_rows(acc, chunks, cols, deps, lambda b, r: vals[r, :])
        whole()
        gather_rows(gt, chunks, cols, deps, lambda b, r: w[r, :], vals)
        part[...] = jnp.sum(vals[...], axis=1, keepdims=True)


def place_of(slot_info):
    return jnp.where(iota((SLOTS, SLOTS), 0) == slot_info, 1.0, 0.0)


def to_rays(partial, place, rays):
    row = jnp.sum(place * partial, axis=0, keepdims=True)
    total = jnp.zeros((RAYS, NDEV), f32)
    for k in range(2):
        at = slice(k * 128, (k + 1) * 128)
        total += jnp.where(iota((RAYS, NDEV), 0) == rays[:, at], row[:, at], 0.0)
    return total


def from_rays(values, place, rays):
    rows = [
        jnp.sum(jnp.where(iota((RAYS, NDEV), 0) == rays[:, k * 128:(k + 1) * 128], values, 0.0), axis=0, keepdims=True)
        for k in range(2)
    ]
    return jnp.sum(place * jnp.concatenate(rows, axis=1), axis=1, keepdims=True)


def first_kernel(held, q_out, p_out, col, dep, w, bcol, bdep, bw, info, count, acc, gt, wy, vals, part):
    meta = held[:, 4, :].T
    y_row = jnp.concatenate([meta[0:1, :], meta[1:2, :]], axis=1)
    ray_row = jnp.concatenate([meta[2:3, :], meta[3:4, :]], axis=1).astype(i32) - 1
    live = ray_row >= 0
    flags = jnp.broadcast_to(jnp.where(live, 1.0, 0.0), (8, SLOTS)).astype(bf16)
    before = jnp.where(iota((SLOTS, SLOTS), 0) < iota((SLOTS, SLOTS), 1), 1.0, 0.0).astype(bf16)
    at = jnp.dot(flags, before, preferred_element_type=f32)[0:1, :].astype(i32)
    at = jnp.where(live, at, -1)
    info[0:1, :] = at
    info[1:2, :] = ray_row
    n = jnp.sum(jnp.where(live, 1.0, 0.0)).astype(i32)
    place = place_of(at)
    pay = jnp.concatenate([as_payload(held[:, k, :].astype(i32), held[:, 2 + k, :]) for k in range(2)], axis=0)
    z, c, lens = from_payload(jnp.dot(place.astype(bf16), pay, preferred_element_type=f32))
    col[...] = c.astype(i32)
    dep[...] = z.astype(i32)
    w[...] = lens
    most = bucket(n, col[...], dep[...], lens, bcol, bdep, bw)
    count[0] = n
    count[1] = most
    y_col = jnp.sum(place * y_row, axis=1, keepdims=True)
    both_passes(n, most, y_col, col, dep, w, bcol, bdep, bw, None, q_out, acc, gt, wy, vals, part)
    p_out[...] = to_rays(part[...], place_of(at), ray_row)


def second_kernel(p, smooth, col, dep, w, bcol, bdep, bw, info, count, q_out, p_out, acc, gt, wy, vals, part):
    place = place_of(info[0:1, :])
    ray_row = info[1:2, :]
    y_col = from_rays(p[...], place, ray_row)
    both_passes(count[0], count[1], y_col, col, dep, w, bcol, bdep, bw, smooth, q_out, acc, gt, wy, vals, part)
    p_out[...] = to_rays(part[...], place, ray_row)


def shape(dims, dtype=f32):
    return jax.ShapeDtypeStruct(dims, dtype)


SCRATCH = [
    pltpu.VMEM((BLOCKS, BLOCK, 256), f32),
    pltpu.VMEM((256, COLS), bf16),
    pltpu.VMEM((BLOCKS, 128, 128), f32),
    pltpu.VMEM((SLOTS, SEG), f32),
    pltpu.VMEM((SLOTS, 1), f32),
]


MESH = pl.DeviceIdType.MESH
SIZES = (4, 2, 4, 4)
STAGES = ((1, 0), (2,), (3,))
PEERS = max(len(list(itertools.product(*[range(SIZES[a]) for a in g]))) for g in STAGES) - 1


def coords():
    return tuple(lax.axis_index(a) for a in LON_LAT)


def stage_peers(here, group):
    found = []
    for steps in itertools.product(*[range(SIZES[a]) for a in group]):
        if any(steps):
            add = dict(zip(group, steps))
            found.append(tuple((v + add.get(i, 0)) % SIZES[i] for i, v in enumerate(here)))
    return found


def ring_peers(here):
    lon, lat = here[0] * 2 + here[1], here[2] * 4 + here[3]
    found = []
    for step in (1, 7):
        to = (lon + step) % 8
        found.append((to // 2, to % 2, here[2], here[3]))
    for step in (1, 15):
        to = (lat + step) % 16
        found.append((here[0], here[1], to // 4, to % 4))
    return found


def meet(here):
    barrier = pltpu.get_barrier_semaphore()
    peers = [p for g in STAGES for p in stage_peers(here, g)] + ring_peers(here)
    for peer in peers:
        pl.semaphore_signal(barrier, inc=1, device_id=peer, device_id_type=MESH)
    pl.semaphore_wait(barrier, len(peers))


def send_stage(s, here, buf, got, send_sem, recv_sem):
    copies = []
    for k, peer in enumerate(stage_peers(here, STAGES[s])):
        copy = pltpu.make_async_remote_copy(
            buf.at[s], got.at[s, k], send_sem.at[s, k], recv_sem.at[s, k], device_id=peer, device_id_type=MESH)
        copy.start()
        copies.append(copy)
    return copies


def add_stage(s, copies, buf, got):
    total = buf[s]
    for k, copy in enumerate(copies):
        copy.wait_recv()
        total = total + got[s, k]
    return total


def send_halo(here, field, edge, halo, send_sem, recv_sem):
    edge[0] = field[pl.ds(CLAT - 1, CLON, stride=CLAT), :]
    edge[1] = field[pl.ds(0, CLON, stride=CLAT), :]
    faces = (field.at[pl.ds(COLS - CLAT, CLAT)], field.at[pl.ds(0, CLAT)], edge.at[0], edge.at[1])
    copies = []
    for k, (face, peer) in enumerate(zip(faces, ring_peers(here))):
        copy = pltpu.make_async_remote_copy(
            face, halo.at[k], send_sem.at[k], recv_sem.at[k], device_id=peer, device_id_type=MESH)
        copy.start()
        copies.append(copy)
    return copies


def stencil_rows(here, field, halo, put):
    lat = here[2] * 4 + here[3]
    has_before = jnp.where(lat > 0, 1.0, 0.0)
    has_after = jnp.where(lat < 15, 1.0, 0.0)
    row, lane = iota((CLAT, DEP), 0), iota((CLAT, DEP), 1)

    def layer(i, before, after):
        mine = pl.ds(pl.multiple_of(i * CLAT, CLAT), CLAT)
        f = field[mine, :]
        lat_before = jnp.where(row == 0, halo[2, pl.ds(i, 1), :] * has_before, pltpu.roll(f, 1, 0))
        lat_after = jnp.where(row == CLAT - 1, halo[3, pl.ds(i, 1), :] * has_after, pltpu.roll(f, CLAT - 1, 0))
        up = jnp.where(lane == 0, 0.0, pltpu.roll(f, 1, 1))
        down = jnp.where(lane == DEP - 1, 0.0, pltpu.roll(f, DEP - 1, 1))
        put(mine, DAMP * (6.0 * f - before - after - lat_before - lat_after - up - down))

    def inner(i, carry):
        layer(i, field[pl.ds(pl.multiple_of((i - 1) * CLAT, CLAT), CLAT), :],
              field[pl.ds(pl.multiple_of((i + 1) * CLAT, CLAT), CLAT), :])
        return carry

    layer(0, halo[0], field[CLAT:2 * CLAT, :])
    layer(CLON - 1, field[COLS - 2 * CLAT:COLS - CLAT, :], halo[1])
    lax.fori_loop(1, CLON - 1, inner, 0)


def finish(copies):
    for copy in copies:
        copy.wait_send()


def middle_kernel(p_part, q, p_out, smooth, buf, got, g, edge, halo, send_sem, recv_sem, face_send, face_recv):
    here = coords()
    meet(here)
    buf[0] = p_part[...]
    first = send_stage(0, here, buf, got, send_sem, recv_sem)
    faces = send_halo(here, q, edge.at[0], halo.at[0], face_send.at[0], face_recv.at[0])
    buf[1] = add_stage(0, first, buf, got)
    second = send_stage(1, here, buf, got, send_sem, recv_sem)
    for copy in faces:
        copy.wait_recv()

    def to_g(rows, value):
        g[rows, :] = value

    stencil_rows(here, q, halo.at[0], to_g)
    more = send_halo(here, g, edge.at[1], halo.at[1], face_send.at[1], face_recv.at[1])
    buf[2] = add_stage(1, second, buf, got)
    third = send_stage(2, here, buf, got, send_sem, recv_sem)
    for copy in more:
        copy.wait_recv()

    def to_smooth(rows, value):
        smooth[rows, :] = value

    stencil_rows(here, g, halo.at[1], to_smooth)
    p_out[...] = add_stage(2, third, buf, got)
    finish(first + second + third + faces + more)


def last_kernel(count, times, p_part, p0, q0, q1, model, misfit, buf, got, norm, edge, halo, send_sem, recv_sem,
                face_send, face_recv):
    here = coords()
    meet(here)
    faces = send_halo(here, q1, edge, halo, face_send, face_recv)
    buf[0, 0:RAYS, :] = p_part[...]
    a, b = q0[...], q1[...]
    dots = [jnp.sum(jnp.sum(x, axis=0, keepdims=True), axis=1, keepdims=True) for x in (a * a, a * b, b * b)]
    norm[...] = jnp.zeros_like(norm)
    for copy in faces:
        copy.wait_recv()

    def to_norm(rows, value):
        norm[...] += value * value

    stencil_rows(here, q1, halo, to_norm)
    dots.append(jnp.sum(jnp.sum(norm[...], axis=0, keepdims=True), axis=1, keepdims=True))
    lane = iota((8, NDEV), 1)
    row = jnp.zeros((8, NDEV), f32)
    for k, dot in enumerate(dots):
        row = jnp.where(lane == k, dot, row)
    buf[0, RAYS:RAYS + 8, :] = row
    sent = []
    for s in range(len(STAGES)):
        copies = send_stage(s, here, buf, got, send_sem, recv_sem)
        total = add_stage(s, copies, buf, got)
        buf[s + 1] = total
        sent += copies
    p1 = total[0:RAYS, :]
    m0, m1, m2, m3 = [total[RAYS:RAYS + 1, k:k + 1] for k in range(4)]
    m3 = m3 + jnp.sum(jnp.sum(p1 * p1, axis=0, keepdims=True), axis=1, keepdims=True)
    r1, r2, r3 = m1 / m0, m2 / m1, m3 / m2
    c0 = (r3 - r1) / (r3 - r2) / r1
    c1 = (r1 - r2) / (r3 - r2) / (r1 * r2)
    model[...] = (SCALE * c0) * a + (SCALE * c1) * b
    me = ((here[0] * 2 + here[1]) * 4 + here[2]) * 4 + here[3]
    fit = jnp.where(iota((RAYS, NDEV), 1) == me, c0 * p0[...] + c1 * p1, 0.0)
    column = jnp.sum(fit, axis=1, keepdims=True)
    own = jnp.sum(jnp.where(iota((RAYS, RAYS), 0) == iota((RAYS, RAYS), 1), column, 0.0), axis=0, keepdims=True)
    data = jnp.where(iota((1, RAYS), 1) < count[0], times[...], 0.0)
    misfit[...] = data - own
    finish(faces + sent)


def comm_scratch(rows, faces):
    return [
        pltpu.VMEM((len(STAGES) + 1, rows, NDEV), f32),
        pltpu.VMEM((len(STAGES), PEERS, rows, NDEV), f32),
    ], [
        pltpu.VMEM(faces + (2, CLON, DEP), f32),
        pltpu.VMEM(faces + (4, CLON, DEP), f32),
        pltpu.SemaphoreType.DMA((len(STAGES), PEERS)),
        pltpu.SemaphoreType.DMA((len(STAGES), PEERS)),
        pltpu.SemaphoreType.DMA(faces + (4,)),
        pltpu.SemaphoreType.DMA(faces + (4,)),
    ]


def comm_params(number):
    return pltpu.CompilerParams(vmem_limit_bytes=16 << 20, collective_id=number, has_side_effects=True)


def shards(travel_times, ray_counts, tile_brick, cell_offsets, cell_depths, seg_lengths):
    times = travel_times.reshape(1, RAYS)
    send = pl.pallas_call(
        pack_kernel,
        out_shape=shape((NDEV, 5, SEG)),
        in_specs=[SMEM] + [VMEM] * 2 + [pl.BlockSpec(memory_space=pl.ANY)] * 3,
        out_specs=VMEM,
        scratch_shapes=[pltpu.VMEM((128, 768), bf16)] + [pltpu.VMEM((RAYS, TPR, SEG), d) for d in (i32, i32, f32)]
        + [pltpu.SemaphoreType.DMA((3,))],
        compiler_params=PARAMS,
    )(ray_counts, tile_brick.T, times, cell_offsets, cell_depths, seg_lengths)
    held = lax.all_to_all(send, LON_LAT, split_axis=0, concat_axis=0, tiled=True)
    entries = [shape((SLOTS, SEG), d) for d in (i32, i32, f32)] + [shape((BLOCKS, 128, 128), d) for d in (i32, i32, f32)]
    q0, p_part, *lists, info, count = pl.pallas_call(
        first_kernel,
        out_shape=(shape((COLS, DEP)), shape((RAYS, NDEV)), *entries, shape((2, SLOTS), i32), shape((2,), i32)),
        in_specs=[VMEM],
        out_specs=(VMEM,) * 9 + (SMEM,),
        scratch_shapes=SCRATCH,
        compiler_params=PARAMS,
    )(held)
    bufs, faces = comm_scratch(RAYS, (2,))
    p0, smooth = pl.pallas_call(
        middle_kernel,
        out_shape=(shape((RAYS, NDEV)), shape((COLS, DEP))),
        in_specs=[VMEM] * 2,
        out_specs=(VMEM,) * 2,
        scratch_shapes=bufs + [pltpu.VMEM((COLS, DEP), f32)] + faces,
        compiler_params=comm_params(0),
    )(p_part, q0)
    q1, p_part = pl.pallas_call(
        second_kernel,
        out_shape=(shape((COLS, DEP)), shape((RAYS, NDEV))),
        in_specs=[VMEM] * 9 + [SMEM],
        out_specs=(VMEM,) * 2,
        scratch_shapes=SCRATCH,
        compiler_params=PARAMS,
    )(p0, smooth, *lists, info, count)
    bufs, faces = comm_scratch(RAYS + 8, ())
    model, misfit = pl.pallas_call(
        last_kernel,
        out_shape=(shape((COLS, DEP)), shape((1, RAYS))),
        in_specs=[SMEM] + [VMEM] * 5,
        out_specs=(VMEM,) * 2,
        scratch_shapes=bufs + [pltpu.VMEM((CLAT, DEP), f32)] + faces,
        compiler_params=comm_params(1),
    )(ray_counts, times, p_part, p0, q0, q1)
    return (model.reshape(CLON, CLAT, DEP), misfit.reshape(RAYS))


def solution(mesh):
    torus = Mesh(mesh.devices.reshape(4, 2, 4, 4), LON_LAT)
    in_specs = (
        P(LON_LAT),
        P(LON_LAT),
        P(LON_LAT, None),
        P(LON_LAT, None, None),
        P(LON_LAT, None, None),
        P(LON_LAT, None, None),
    )
    out_specs = (P(LON, LAT, None), P(LON_LAT))
    return jax.shard_map(shards, mesh=torus, in_specs=in_specs, out_specs=out_specs, check_vma=False)
```

```python
import itertools

import jax
import jax.numpy as jnp
from jax import lax
from jax.experimental import pallas as pl
from jax.experimental.pallas import tpu as pltpu
from jax.sharding import Mesh
from jax.sharding import PartitionSpec as P

CLON, CLAT, DEP, SEG = 32, 32, 128, 128
COLS = CLON * CLAT
RAYS, TPR = 32, 4
NDEV = 128
SLOTS = 2 * NDEV
CHUNK = 8
BLOCKS, BLOCK, HALF = 4, 256, 64
SCALE = 8.0
DAMP = 0.01 * SCALE
LON_LAT = ("lon_0", "lon_1", "lat_0", "lat_1")
LON = ("lon_0", "lon_1")
LAT = ("lat_0", "lat_1")

f32, bf16, i32, i16 = jnp.float32, jnp.bfloat16, jnp.int32, jnp.int16
VMEM = pl.BlockSpec(memory_space=pltpu.VMEM)
SMEM = pl.BlockSpec(memory_space=pltpu.SMEM)
PARAMS = pltpu.CompilerParams(vmem_limit_bytes=48 << 20)


MESH = pl.DeviceIdType.MESH
SIZES = (4, 2, 4, 4)


def coords():
    return tuple(lax.axis_index(a) for a in LON_LAT)


def flat(at):
    return ((at[0] * 2 + at[1]) * 4 + at[2]) * 4 + at[3]


def stage_peers(here, group):
    found = []
    for steps in itertools.product(*[range(SIZES[a]) for a in group]):
        if any(steps):
            add = dict(zip(group, steps))
            found.append(tuple((v + add.get(i, 0)) % SIZES[i] for i, v in enumerate(here)))
    return found


def ring_peers(here):
    lon, lat = here[0] * 2 + here[1], here[2] * 4 + here[3]
    found = []
    for step in (1, 7):
        to = (lon + step) % 8
        found.append((to // 2, to % 2, here[2], here[3]))
    for step in (1, 15):
        to = (lat + step) % 16
        found.append((here[0], here[1], to // 4, to % 4))
    return found


def meet(peers):
    barrier = pltpu.get_barrier_semaphore()
    for peer in peers:
        pl.semaphore_signal(barrier, inc=1, device_id=peer, device_id_type=MESH)
    pl.semaphore_wait(barrier, len(peers))


def iota(shape, dim):
    return lax.broadcasted_iota(i32, shape, dim)


def split2(x):
    hi = x.astype(bf16)
    return hi, (x - hi.astype(f32)).astype(bf16)


def split3(x):
    hi = x.astype(bf16)
    rest = x - hi.astype(f32)
    mid = rest.astype(bf16)
    return hi, mid, (rest - mid.astype(f32)).astype(bf16)


def as_payload(cell, lens):
    col = cell >> 7
    parts = [(cell & 127), (col & 127), (col >> 7)]
    return jnp.concatenate([p.astype(f32).astype(bf16) for p in parts] + list(split3(lens)), axis=1)


def from_payload(rows):
    z, low, high, hi, mid, lo = [rows[:, k * 128:(k + 1) * 128] for k in range(6)]
    return z, high * 128.0 + low, (hi + mid) + lo


def prefix(flags):
    upto = jnp.where(iota((128, 128), 0) <= iota((128, 128), 1), 1.0, 0.0).astype(bf16)
    return jnp.dot(jnp.where(flags, 1.0, 0.0).astype(bf16), upto, preferred_element_type=f32).astype(i32)


def take(x, index):
    return jnp.take_along_axis(x, index, axis=1, mode="promise_in_bounds")


def by_block(cell, w):
    counts = [prefix((cell >> 15) == b) for b in range(BLOCKS)]
    starts = [jnp.zeros((128, 1), i32)]
    for b in range(BLOCKS - 1):
        starts.append(starts[-1] + counts[b][:, 127:128])
    lane = iota((128, 128), 1)
    block, rank = jnp.zeros((128, 128), i32), lane
    for b in range(1, BLOCKS):
        block = jnp.where(lane >= starts[b], b, block)
        rank = jnp.where(lane >= starts[b], lane - starts[b], rank)
    at = jnp.zeros((128, 128), i32)
    for step in (64, 32, 16, 8, 4, 2, 1):
        probe = at + (step - 1)
        seen = take(counts[0], probe)
        for b in range(1, BLOCKS):
            seen = jnp.where(block == b, take(counts[b], probe), seen)
        at = jnp.where(seen <= rank, at + step, at)
    marks = jnp.zeros((128, 128), f32)
    for b in range(1, BLOCKS):
        marks = jnp.where((lane == 4 + b) | (lane == 8 + b), starts[b].astype(f32), marks)
    return take(cell, at), take(w, at), marks


def send_kernel(count, brick, times, offs_in, deps_in, lens_in, held, send, pay, offs, deps, lens, load_sem, meet_sem,
                send_sem, recv_sem):
    here = coords()
    loads = [
        pltpu.make_async_copy(src, dst, load_sem.at[k])
        for k, (src, dst) in enumerate(((offs_in, offs), (deps_in, deps), (lens_in, lens)))
    ]
    for load in loads:
        load.start()
    barrier = pltpu.get_barrier_semaphore()
    lines = [p for axis in range(4) for p in stage_peers(here, (axis,))]
    for peer in lines:
        pl.semaphore_signal(barrier, inc=1, device_id=peer, device_id_type=MESH)
    tb = brick[...].astype(f32)
    brick_row = jnp.concatenate([tb[k:k + 1, :] for k in range(TPR)], axis=1)
    time_row = jnp.concatenate([times[...]] * TPR, axis=1)
    ray_row = iota((1, 128), 1) & 31
    live = ray_row < count[0]
    as_rows = jnp.broadcast_to(brick_row, (128, 128))
    same = (as_rows == as_rows.T) & (iota((128, 128), 0) < iota((128, 128), 1))
    rank_row = jnp.sum(jnp.where(same, 1.0, 0.0), axis=0, keepdims=True)
    for load in loads:
        load.wait()
    cell = jnp.concatenate([offs[:, k, :] * DEP + deps[:, k, :] for k in range(TPR)], axis=0)
    w = jnp.concatenate([lens[:, k, :] * SCALE for k in range(TPR)], axis=0)
    cell, w, marks = by_block(cell, w)
    pay[:, 0:768] = as_payload(cell, w)
    pay[:, 768:896] = marks.astype(bf16)
    pl.semaphore_wait(barrier, len(lines))
    for s, axis in enumerate((0, 2, 3)):
        peers = stage_peers(here, (axis,))
        for peer in peers:
            pl.semaphore_signal(meet_sem.at[s], inc=1, device_id=peer, device_id_type=MESH)
        if s < 2:
            place_rank(s, brick_row, rank_row, live, time_row, ray_row, pay, send)
        pl.semaphore_wait(meet_sem.at[s], len(peers))
    me = flat(here)

    def go(step, carry):
        steps = (step // 32, (step // 16) % 2, (step // 4) % 4, step % 4)
        peer = tuple((v + d) % n for v, d, n in zip(here, steps, SIZES))
        pltpu.make_async_remote_copy(
            send.at[flat(peer)], held.at[me], send_sem, recv_sem, device_id=peer, device_id_type=MESH).start()
        return carry

    lax.fori_loop(1, NDEV, go, 0)
    held[me] = send[me]
    rest = pl.ds(0, NDEV - 1)
    every = pltpu.make_async_remote_copy(
        send.at[rest], held.at[rest], send_sem, recv_sem, device_id=here, device_id_type=MESH)
    every.wait_recv()
    every.wait_send()


def place_rank(k, brick_row, rank_row, live, time_row, ray_row, pay, send):
    lanes = iota((128, 128), 1)
    picked = jnp.where((iota((128, 128), 0).astype(f32) == brick_row) & (rank_row == k) & live, 1.0, 0.0)
    rows = jnp.dot(picked.astype(bf16), pay[...], preferred_element_type=f32)
    z, col, w = from_payload(rows)
    send[:, k, :] = col * 128.0 + z
    send[:, 2 + k, :] = w
    value = jnp.sum(picked * time_row, axis=1, keepdims=True)
    ray = jnp.sum(picked * (ray_row + 1).astype(f32), axis=1, keepdims=True)
    marks = rows[:, 768:896]
    if k == 0:
        send[:, 4, :] = jnp.where(lanes == 0, value, jnp.where(lanes == 2, ray, jnp.where(lanes < 8, marks, 0.0)))
    else:
        send[:, 4, :] = jnp.where(lanes == 1, value, jnp.where(lanes == 3, ray, jnp.where(lanes < 8, send[:, 4, :], marks)))


def onehot_cols(col_row):
    at = jnp.broadcast_to(col_row.astype(i16), (BLOCK, 128))
    return jnp.where(lax.broadcasted_iota(i16, (BLOCK, 128), 0) == at, jnp.ones((), bf16), jnp.zeros((), bf16))


def onehot_values(dep_row, val_row):
    at = jnp.broadcast_to(dep_row.astype(i16), (DEP, 128))
    here = lax.broadcasted_iota(i16, (DEP, 128), 0) == at
    return jnp.concatenate(
        [jnp.where(here, jnp.broadcast_to(part, (DEP, 128)), jnp.zeros((), bf16)) for part in split2(val_row)], axis=0)


def scatter_rows(acc, chunks, col, dep, val):
    acc[...] = jnp.zeros_like(acc)

    def body(c, carry):
        rows = [pl.ds(c * CHUNK + j, 1) for j in range(CHUNK)]
        for b in range(BLOCKS):
            left = jnp.concatenate([onehot_cols(col(b, r)) for r in rows], axis=1)
            right = jnp.concatenate([onehot_values(dep(b, r), val(b, r)) for r in rows], axis=1)
            acc[b] += lax.dot_general(left, right, (((1,), (1,)), ((), ())), preferred_element_type=f32)
        return carry

    lax.fori_loop(0, chunks, body, 0)


def gather_rows(gt, chunks, col, dep, w, out):
    out[...] = jnp.zeros_like(out)

    def body(c, carry):
        rows = [pl.ds(c * CHUNK + j, 1) for j in range(CHUNK)]
        sums = [jnp.zeros((8, 128), f32)] * CHUNK
        for b in range(BLOCKS):
            right = jnp.concatenate([onehot_cols(col(b, r)) for r in rows], axis=1)
            res = jnp.dot(gt[:, b * BLOCK:(b + 1) * BLOCK], right, preferred_element_type=f32)
            for j, r in enumerate(rows):
                at = slice(j * 128, (j + 1) * 128)
                both = res[0:128, at] + res[128:256, at]
                here = jnp.where(iota((DEP, 128), 0) == dep(b, r), both, 0.0)
                sums[j] = sums[j] + here.reshape(16, 8, 128).sum(axis=0) * w(b, r)
        for j, r in enumerate(rows):
            out[r, :] = jnp.sum(sums[j], axis=0, keepdims=True)
        return carry

    lax.fori_loop(0, chunks, body, 0)


def pair(x):
    x = x.reshape(16, 16, 128)
    return jnp.where(iota((16, 8, 128), 2) < HALF, x[:, 0:8], x[:, 8:16]).reshape(128, 128)


def unpair(x):
    low = iota((128, 128), 1) < HALF
    halves = [jnp.sum(jnp.where(m, x, 0.0), axis=1, keepdims=True) for m in (low, ~low)]
    return jnp.concatenate([h.reshape(16, 8, 1) for h in halves], axis=1).reshape(SLOTS, 1)


def bucket(n, starts, col, dep, w, bcol, bdep, bw):
    rank = iota((SLOTS, 128), 1) & (HALF - 1)
    most = jnp.zeros((SLOTS, 1), i32)
    for b in range(BLOCKS):
        first = starts[:, b:b + 1]
        held = (starts[:, b + 1:b + 2] if b + 1 < BLOCKS else SEG) - first
        at = (first + rank) & (SEG - 1)
        bcol[b] = pair(take(col, at) - b * BLOCK)
        bdep[b] = pair(take(dep, at))
        bw[b] = pair(jnp.where(rank < held, take(w, at), 0.0))
        most = jnp.maximum(most, held)
    most = jnp.where(iota((SLOTS, 1), 0) < n, most, 0)
    return jnp.max(most.astype(f32)).astype(i32)


def both_passes(n, most, y_col, col, dep, w, bcol, bdep, bw, finish_q, q_out, acc, gt, wy, vals, part):
    fits = most <= HALF

    def whole():
        q = jnp.concatenate([acc[b, :, 0:128] + acc[b, :, 128:256] for b in range(BLOCKS)], axis=0)
        q = finish_q(q)
        q_out[...] = q
        hi, lo = split2(q.T)
        gt[0:128, :] = hi
        gt[128:256, :] = lo

    @pl.when(fits)
    def _():
        chunks = (n + 2 * CHUNK - 1) // (2 * CHUNK)
        y = pair(jnp.broadcast_to(y_col, (SLOTS, 128)))
        for b in range(BLOCKS):
            wy[b] = bw[b] * y
        cols, deps = (lambda b, r: bcol[b, r, :]), (lambda b, r: bdep[b, r, :])
        scatter_rows(acc, chunks, cols, deps, lambda b, r: wy[b, r, :])
        whole()
        gather_rows(gt, chunks, cols, deps, lambda b, r: bw[b, r, :], vals.at[pl.ds(0, 128)])
        part[...] = unpair(vals[0:128, :])

    @pl.when(jnp.logical_not(fits))
    def _():
        chunks = (n + CHUNK - 1) // CHUNK
        vals[...] = w[...] * y_col
        cols, deps = (lambda b, r: col[r, :] - b * BLOCK), (lambda b, r: dep[r, :])
        scatter_rows(acc, chunks, cols, deps, lambda b, r: vals[r, :])
        whole()
        gather_rows(gt, chunks, cols, deps, lambda b, r: w[r, :], vals)
        part[...] = jnp.sum(vals[...], axis=1, keepdims=True)


def place_of(slot_info):
    return jnp.where(iota((SLOTS, SLOTS), 0) == slot_info, 1.0, 0.0)


def to_rays(partial, place, rays):
    row = jnp.sum(place * partial, axis=0, keepdims=True)
    total = jnp.zeros((RAYS, NDEV), f32)
    for k in range(2):
        at = slice(k * 128, (k + 1) * 128)
        total += jnp.where(iota((RAYS, NDEV), 0) == rays[:, at], row[:, at], 0.0)
    return total


def from_rays(values, place, rays):
    rows = [
        jnp.sum(jnp.where(iota((RAYS, NDEV), 0) == rays[:, k * 128:(k + 1) * 128], values, 0.0), axis=0, keepdims=True)
        for k in range(2)
    ]
    return jnp.sum(place * jnp.concatenate(rows, axis=1), axis=1, keepdims=True)


def total_of(x):
    return jnp.sum(jnp.sum(x, axis=0, keepdims=True), axis=1, keepdims=True)


def as_row(values):
    row = jnp.zeros((8, NDEV), f32)
    for k, value in enumerate(values):
        row = jnp.where(iota((8, NDEV), 1) == k, value, row)
    return row


def first_kernel(held, q_out, p_out, col, dep, w, bcol, bdep, bw, info, count, acc, gt, wy, vals, part):
    meta = held[:, 4, :]
    across = meta.T
    y_row = jnp.concatenate([across[0:1, :], across[1:2, :]], axis=1)
    ray_row = jnp.concatenate([across[2:3, :], across[3:4, :]], axis=1).astype(i32) - 1
    live = ray_row >= 0
    flags = jnp.broadcast_to(jnp.where(live, 1.0, 0.0), (8, SLOTS)).astype(bf16)
    before = jnp.where(iota((SLOTS, SLOTS), 0) < iota((SLOTS, SLOTS), 1), 1.0, 0.0).astype(bf16)
    at = jnp.dot(flags, before, preferred_element_type=f32)[0:1, :].astype(i32)
    at = jnp.where(live, at, -1)
    info[0:1, :] = at
    info[1:2, :] = ray_row
    n = jnp.sum(jnp.where(live, 1.0, 0.0)).astype(i32)
    place = place_of(at)
    pay = jnp.concatenate([as_payload(held[:, k, :].astype(i32), held[:, 2 + k, :]) for k in range(2)], axis=0)
    marks = jnp.concatenate([meta, pltpu.roll(meta, 124, 1)], axis=0).astype(bf16)
    rows = jnp.dot(place.astype(bf16), jnp.concatenate([pay, marks], axis=1), preferred_element_type=f32)
    z, c, lens = from_payload(rows)
    col[...] = c.astype(i32)
    dep[...] = z.astype(i32)
    w[...] = lens
    most = bucket(n, rows[:, 772:776].astype(i32), col[...], dep[...], lens, bcol, bdep, bw)
    count[0] = n
    count[1] = most
    y_col = jnp.sum(place * y_row, axis=1, keepdims=True)
    both_passes(n, most, y_col, col, dep, w, bcol, bdep, bw, lambda q: q, q_out, acc, gt, wy, vals, part)
    p_out[0:RAYS, :] = to_rays(part[...], place_of(at), ray_row)
    q = q_out[...]
    p_out[RAYS:RAYS + 8, :] = as_row([total_of(q * q)])


def second_kernel(p, shift, q0, smooth, col, dep, w, bcol, bdep, bw, info, count, e_out, p_out, dots, acc, gt, wy, vals,
                  part):
    place = place_of(info[0:1, :])
    ray_row = info[1:2, :]
    y_col = from_rays(p[...], place, ray_row)
    finish_q = lambda q: q + smooth[...] - shift[0:1, 0:1] * q0[...]
    both_passes(count[0], count[1], y_col, col, dep, w, bcol, bdep, bw, finish_q, e_out, acc, gt, wy, vals, part)
    p_out[...] = to_rays(part[...], place, ray_row)
    e = e_out[...]
    dots[...] = as_row([total_of(e * q0[...]), total_of(e * e)])


def shape(dims, dtype=f32):
    return jax.ShapeDtypeStruct(dims, dtype)


SCRATCH = [
    pltpu.VMEM((BLOCKS, BLOCK, 256), f32),
    pltpu.VMEM((256, COLS), bf16),
    pltpu.VMEM((BLOCKS, 128, 128), f32),
    pltpu.VMEM((SLOTS, SEG), f32),
    pltpu.VMEM((SLOTS, 1), f32),
]


STAGES = ((1, 0), (2,), (3,))
ROUNDS = ((1, 0), (2, 3))


def send_stage(s, here, group, buf, got, send_sem, recv_sem):
    copies = []
    for k, peer in enumerate(stage_peers(here, group)):
        copy = pltpu.make_async_remote_copy(
            buf.at[s], got.at[s, k], send_sem.at[s, k], recv_sem.at[s, k], device_id=peer, device_id_type=MESH)
        copy.start()
        copies.append(copy)
    return copies


def add_stage(s, copies, buf, got):
    total = buf[s]
    for k, copy in enumerate(copies):
        copy.wait_recv()
        total = total + got[s, k]
    return total


def send_halo(here, field, edge, halo, send_sem, recv_sem):
    edge[0] = field[pl.ds(CLAT - 1, CLON, stride=CLAT), :]
    edge[1] = field[pl.ds(0, CLON, stride=CLAT), :]
    faces = (field.at[pl.ds(COLS - CLAT, CLAT)], field.at[pl.ds(0, CLAT)], edge.at[0], edge.at[1])
    copies = []
    for k, (face, peer) in enumerate(zip(faces, ring_peers(here))):
        copy = pltpu.make_async_remote_copy(
            face, halo.at[k], send_sem.at[k], recv_sem.at[k], device_id=peer, device_id_type=MESH)
        copy.start()
        copies.append(copy)
    return copies


def stencil_rows(here, field, halo, put):
    lat = here[2] * 4 + here[3]
    has_before = jnp.where(lat > 0, 1.0, 0.0)
    has_after = jnp.where(lat < 15, 1.0, 0.0)
    row, lane = iota((CLAT, DEP), 0), iota((CLAT, DEP), 1)

    def layer(i, before, after):
        mine = pl.ds(pl.multiple_of(i * CLAT, CLAT), CLAT)
        f = field[mine, :]
        lat_before = jnp.where(row == 0, halo[2, pl.ds(i, 1), :] * has_before, pltpu.roll(f, 1, 0))
        lat_after = jnp.where(row == CLAT - 1, halo[3, pl.ds(i, 1), :] * has_after, pltpu.roll(f, CLAT - 1, 0))
        up = jnp.where(lane == 0, 0.0, pltpu.roll(f, 1, 1))
        down = jnp.where(lane == DEP - 1, 0.0, pltpu.roll(f, DEP - 1, 1))
        put(mine, DAMP * (6.0 * f - before - after - lat_before - lat_after - up - down))

    def inner(i, carry):
        layer(i, field[pl.ds(pl.multiple_of((i - 1) * CLAT, CLAT), CLAT), :],
              field[pl.ds(pl.multiple_of((i + 1) * CLAT, CLAT), CLAT), :])
        return carry

    layer(0, halo[0], field[CLAT:2 * CLAT, :])
    layer(CLON - 1, field[COLS - 2 * CLAT:COLS - CLAT, :], halo[1])
    lax.fori_loop(1, CLON - 1, inner, 0)


def finish(copies):
    for copy in copies:
        copy.wait_send()


def middle_kernel(p_part, q, p_out, shift, smooth, buf, got, g, edge, halo, send_sem, recv_sem, face_send, face_recv):
    here = coords()
    meet([p for group in STAGES for p in stage_peers(here, group)] + ring_peers(here)[2:])
    buf[0] = p_part[...]
    first = send_stage(0, here, STAGES[0], buf, got, send_sem, recv_sem)
    faces = send_halo(here, q, edge.at[0], halo.at[0], face_send.at[0], face_recv.at[0])
    buf[1] = add_stage(0, first, buf, got)
    second = send_stage(1, here, STAGES[1], buf, got, send_sem, recv_sem)
    for copy in faces:
        copy.wait_recv()

    def to_g(rows, value):
        g[rows, :] = value

    stencil_rows(here, q, halo.at[0], to_g)
    more = send_halo(here, g, edge.at[1], halo.at[1], face_send.at[1], face_recv.at[1])
    buf[2] = add_stage(1, second, buf, got)
    third = send_stage(2, here, STAGES[2], buf, got, send_sem, recv_sem)
    for copy in more:
        copy.wait_recv()

    def to_smooth(rows, value):
        smooth[rows, :] = value

    stencil_rows(here, g, halo.at[1], to_smooth)
    total = add_stage(2, third, buf, got)
    p = total[0:RAYS, :]
    p_out[...] = p
    shift[...] = as_row([total_of(p * p) / total[RAYS:RAYS + 1, 0:1], total[RAYS:RAYS + 1, 0:1]])
    finish(first + second + third + faces + more)


def last_kernel(count, times, p_part, p0, shift, dots, q0, e, model, misfit, buf, got, small, small_got, norm, edge, halo,
                send_sem, recv_sem, small_send, small_recv, face_send, face_recv):
    here = coords()
    meet([p for group in ROUNDS for p in stage_peers(here, group)])
    faces = send_halo(here, e, edge, halo, face_send, face_recv)
    buf[0] = p_part[...]
    first = send_stage(0, here, STAGES[0], buf, got, send_sem, recv_sem)
    norm[...] = jnp.zeros_like(norm)
    for copy in faces:
        copy.wait_recv()

    def to_norm(rows, value):
        norm[...] += value * value

    stencil_rows(here, e, halo, to_norm)
    small[0] = jnp.where(iota((8, NDEV), 1) == 2, total_of(norm[...]), dots[...])
    one = send_stage(0, here, ROUNDS[0], small, small_got, small_send, small_recv)
    buf[1] = add_stage(0, first, buf, got)
    second = send_stage(1, here, STAGES[1], buf, got, send_sem, recv_sem)
    small[1] = add_stage(0, one, small, small_got)
    two = send_stage(1, here, ROUNDS[1], small, small_got, small_send, small_recv)
    buf[2] = add_stage(1, second, buf, got)
    third = send_stage(2, here, STAGES[2], buf, got, send_sem, recv_sem)
    moments = add_stage(1, two, small, small_got)
    pe = add_stage(2, third, buf, got)
    mu, m0 = shift[0:1, 0:1], shift[0:1, 1:2]
    s, big = moments[0:1, 0:1] / m0, moments[0:1, 1:2] / m0
    r = (moments[0:1, 2:3] + total_of(pe * pe)) / m0
    cross = big + mu * s
    det = (s + mu) * r - cross * cross
    a, b = (r - s * cross) / det, (s * s - big) / det
    model[...] = (SCALE * a) * q0[...] + (SCALE * b) * e[...]
    fit = jnp.where(iota((RAYS, NDEV), 1) == flat(here), a * p0[...] + b * pe, 0.0)
    column = jnp.sum(fit, axis=1, keepdims=True)
    own = jnp.sum(jnp.where(iota((RAYS, RAYS), 0) == iota((RAYS, RAYS), 1), column, 0.0), axis=0, keepdims=True)
    data = jnp.where(iota((1, RAYS), 1) < count[0], times[...], 0.0)
    misfit[...] = data - own
    finish(faces + first + second + third + one + two)


def comm_params(number):
    return pltpu.CompilerParams(vmem_limit_bytes=16 << 20, collective_id=number, has_side_effects=True)


def face_scratch(*dims):
    return [pltpu.VMEM(dims + (2, CLON, DEP), f32), pltpu.VMEM(dims + (4, CLON, DEP), f32)]


def sems(*dims):
    return [pltpu.SemaphoreType.DMA(dims), pltpu.SemaphoreType.DMA(dims)]


def shards(travel_times, ray_counts, tile_brick, cell_offsets, cell_depths, seg_lengths):
    times = travel_times.reshape(1, RAYS)
    held = pl.pallas_call(
        send_kernel,
        out_shape=shape((NDEV, 5, SEG)),
        in_specs=[SMEM] + [VMEM] * 2 + [pl.BlockSpec(memory_space=pltpu.MemorySpace.HBM)] * 3,
        out_specs=VMEM,
        scratch_shapes=[pltpu.VMEM((NDEV, 5, SEG), f32), pltpu.VMEM((128, 896), bf16)]
        + [pltpu.VMEM((RAYS, TPR, SEG), d) for d in (i32, i32, f32)]
        + [pltpu.SemaphoreType.DMA((3,)), pltpu.SemaphoreType.REGULAR((3,)), pltpu.SemaphoreType.DMA, pltpu.SemaphoreType.DMA],
        compiler_params=comm_params(2),
    )(ray_counts, tile_brick.T, times, cell_offsets, cell_depths, seg_lengths)
    entries = [shape((SLOTS, SEG), d) for d in (i32, i32, f32)] + [shape((BLOCKS, 128, 128), d) for d in (i32, i32, f32)]
    q0, p_part, *lists, info, count = pl.pallas_call(
        first_kernel,
        out_shape=(shape((COLS, DEP)), shape((RAYS + 8, NDEV)), *entries, shape((2, SLOTS), i32), shape((2,), i32)),
        in_specs=[VMEM],
        out_specs=(VMEM,) * 9 + (SMEM,),
        scratch_shapes=SCRATCH,
        compiler_params=PARAMS,
    )(held)
    p0, shift, smooth = pl.pallas_call(
        middle_kernel,
        out_shape=(shape((RAYS, NDEV)), shape((8, NDEV)), shape((COLS, DEP))),
        in_specs=[VMEM] * 2,
        out_specs=(VMEM,) * 3,
        scratch_shapes=[pltpu.VMEM((3, RAYS + 8, NDEV), f32), pltpu.VMEM((3, 7, RAYS + 8, NDEV), f32),
                        pltpu.VMEM((COLS, DEP), f32)] + face_scratch(2) + sems(3, 7) + sems(2, 4),
        compiler_params=comm_params(0),
    )(p_part, q0)
    e, p_part, dots = pl.pallas_call(
        second_kernel,
        out_shape=(shape((COLS, DEP)), shape((RAYS, NDEV)), shape((8, NDEV))),
        in_specs=[VMEM] * 11 + [SMEM],
        out_specs=(VMEM,) * 3,
        scratch_shapes=SCRATCH,
        compiler_params=PARAMS,
    )(p0, shift, q0, smooth, *lists, info, count)
    model, misfit = pl.pallas_call(
        last_kernel,
        out_shape=(shape((COLS, DEP)), shape((1, RAYS))),
        in_specs=[SMEM] + [VMEM] * 7,
        out_specs=(VMEM,) * 2,
        scratch_shapes=[pltpu.VMEM((3, RAYS, NDEV), f32), pltpu.VMEM((3, 7, RAYS, NDEV), f32),
                        pltpu.VMEM((2, 8, NDEV), f32), pltpu.VMEM((2, 15, 8, NDEV), f32), pltpu.VMEM((CLAT, DEP), f32)]
        + face_scratch() + sems(3, 7) + sems(2, 15) + sems(4),
        compiler_params=comm_params(1),
    )(ray_counts, times, p_part, p0, shift, dots, q0, e)
    return (model.reshape(CLON, CLAT, DEP), misfit.reshape(RAYS))


def solution(mesh):
    torus = Mesh(mesh.devices.reshape(4, 2, 4, 4), LON_LAT)
    in_specs = (
        P(LON_LAT),
        P(LON_LAT),
        P(LON_LAT, None),
        P(LON_LAT, None, None),
        P(LON_LAT, None, None),
        P(LON_LAT, None, None),
    )
    out_specs = (P(LON, LAT, None), P(LON_LAT))
    return jax.shard_map(shards, mesh=torus, in_specs=in_specs, out_specs=out_specs, check_vma=False)
```

```python
import itertools

import jax
import jax.numpy as jnp
from jax import lax
from jax.experimental import pallas as pl
from jax.experimental.pallas import tpu as pltpu
from jax.sharding import Mesh
from jax.sharding import PartitionSpec as P

CLON, CLAT, DEP, SEG = 32, 32, 128, 128
COLS = CLON * CLAT
RAYS, TPR = 32, 4
NDEV = 128
SLOTS = 2 * NDEV
CHUNK = 8
BLOCKS, BLOCK, HALF = 4, 256, 64
SCALE = 8.0
DAMP = 0.01 * SCALE
LON_LAT = ("lon_0", "lon_1", "lat_0", "lat_1")
LON = ("lon_0", "lon_1")
LAT = ("lat_0", "lat_1")

f32, bf16, i32, i16 = jnp.float32, jnp.bfloat16, jnp.int32, jnp.int16
VMEM = pl.BlockSpec(memory_space=pltpu.VMEM)
SMEM = pl.BlockSpec(memory_space=pltpu.SMEM)
PARAMS = pltpu.CompilerParams(vmem_limit_bytes=48 << 20)


MESH = pl.DeviceIdType.MESH
SIZES = (4, 2, 4, 4)


def coords():
    return tuple(lax.axis_index(a) for a in LON_LAT)


def flat(at):
    return ((at[0] * 2 + at[1]) * 4 + at[2]) * 4 + at[3]


def stage_peers(here, group):
    found = []
    for steps in itertools.product(*[range(SIZES[a]) for a in group]):
        if any(steps):
            add = dict(zip(group, steps))
            found.append(tuple((v + add.get(i, 0)) % SIZES[i] for i, v in enumerate(here)))
    return found


def ring_peers(here):
    lon, lat = here[0] * 2 + here[1], here[2] * 4 + here[3]
    found = []
    for step in (1, 7):
        to = (lon + step) % 8
        found.append((to // 2, to % 2, here[2], here[3]))
    for step in (1, 15):
        to = (lat + step) % 16
        found.append((here[0], here[1], to // 4, to % 4))
    return found


def meet(peers):
    barrier = pltpu.get_barrier_semaphore()
    for peer in peers:
        pl.semaphore_signal(barrier, inc=1, device_id=peer, device_id_type=MESH)
    pl.semaphore_wait(barrier, len(peers))


def iota(shape, dim):
    return lax.broadcasted_iota(i32, shape, dim)


def split2(x):
    hi = x.astype(bf16)
    return hi, (x - hi.astype(f32)).astype(bf16)


def split3(x):
    hi = x.astype(bf16)
    rest = x - hi.astype(f32)
    mid = rest.astype(bf16)
    return hi, mid, (rest - mid.astype(f32)).astype(bf16)


def as_payload(cell, lens):
    col = cell >> 7
    parts = [(cell & 127), (col & 127), (col >> 7)]
    return jnp.concatenate([p.astype(f32).astype(bf16) for p in parts] + list(split3(lens)), axis=1)


def from_payload(rows):
    z, low, high, hi, mid, lo = [rows[:, k * 128:(k + 1) * 128] for k in range(6)]
    return z, high * 128.0 + low, (hi + mid) + lo


def prefix(flags):
    upto = jnp.where(iota((128, 128), 0) <= iota((128, 128), 1), 1.0, 0.0).astype(bf16)
    return jnp.dot(jnp.where(flags, 1.0, 0.0).astype(bf16), upto, preferred_element_type=f32).astype(i32)


def take(x, index):
    return jnp.take_along_axis(x, index, axis=1, mode="promise_in_bounds")


def by_block(cell, w):
    counts = [prefix((cell >> 15) == b) for b in range(BLOCKS)]
    starts = [jnp.zeros((128, 1), i32)]
    for b in range(BLOCKS - 1):
        starts.append(starts[-1] + counts[b][:, 127:128])
    lane = iota((128, 128), 1)
    block, rank = jnp.zeros((128, 128), i32), lane
    for b in range(1, BLOCKS):
        block = jnp.where(lane >= starts[b], b, block)
        rank = jnp.where(lane >= starts[b], lane - starts[b], rank)
    at = jnp.zeros((128, 128), i32)
    for step in (64, 32, 16, 8, 4, 2, 1):
        probe = at + (step - 1)
        seen = take(counts[0], probe)
        for b in range(1, BLOCKS):
            seen = jnp.where(block == b, take(counts[b], probe), seen)
        at = jnp.where(seen <= rank, at + step, at)
    marks = jnp.zeros((128, 128), f32)
    for b in range(1, BLOCKS):
        marks = jnp.where((lane == 4 + b) | (lane == 8 + b), starts[b].astype(f32), marks)
    return take(cell, at), take(w, at), marks


def send_kernel(count, brick, times, offs_in, deps_in, lens_in, held, send, pay, offs, deps, lens, load_sem, meet_sem,
                send_sem, recv_sem):
    here = coords()
    loads = [
        pltpu.make_async_copy(src, dst, load_sem.at[k])
        for k, (src, dst) in enumerate(((offs_in, offs), (deps_in, deps), (lens_in, lens)))
    ]
    for load in loads:
        load.start()
    barrier = pltpu.get_barrier_semaphore()
    lines = [p for axis in range(4) for p in stage_peers(here, (axis,))]
    for peer in lines:
        pl.semaphore_signal(barrier, inc=1, device_id=peer, device_id_type=MESH)
    tb = brick[...].astype(f32)
    brick_row = jnp.concatenate([tb[k:k + 1, :] for k in range(TPR)], axis=1)
    time_row = jnp.concatenate([times[...]] * TPR, axis=1)
    ray_row = iota((1, 128), 1) & 31
    live = ray_row < count[0]
    as_rows = jnp.broadcast_to(brick_row, (128, 128))
    same = (as_rows == as_rows.T) & (iota((128, 128), 0) < iota((128, 128), 1))
    rank_row = jnp.sum(jnp.where(same, 1.0, 0.0), axis=0, keepdims=True)
    for load in loads:
        load.wait()
    cell = jnp.concatenate([offs[:, k, :] * DEP + deps[:, k, :] for k in range(TPR)], axis=0)
    w = jnp.concatenate([lens[:, k, :] * SCALE for k in range(TPR)], axis=0)
    cell, w, marks = by_block(cell, w)
    pay[:, 0:768] = as_payload(cell, w)
    pay[:, 768:896] = marks.astype(bf16)
    pl.semaphore_wait(barrier, len(lines))
    for s, axis in enumerate((0, 2, 3)):
        peers = stage_peers(here, (axis,))
        for peer in peers:
            pl.semaphore_signal(meet_sem.at[s], inc=1, device_id=peer, device_id_type=MESH)
        if s < 2:
            place_rank(s, brick_row, rank_row, live, time_row, ray_row, pay, send)
        pl.semaphore_wait(meet_sem.at[s], len(peers))
    me = flat(here)

    def go(step, carry):
        steps = (step // 32, (step // 16) % 2, (step // 4) % 4, step % 4)
        peer = tuple((v + d) % n for v, d, n in zip(here, steps, SIZES))
        pltpu.make_async_remote_copy(
            send.at[flat(peer)], held.at[me], send_sem, recv_sem, device_id=peer, device_id_type=MESH).start()
        return carry

    lax.fori_loop(1, NDEV, go, 0)
    held[me] = send[me]
    rest = pl.ds(0, NDEV - 1)
    every = pltpu.make_async_remote_copy(
        send.at[rest], held.at[rest], send_sem, recv_sem, device_id=here, device_id_type=MESH)
    every.wait_recv()
    every.wait_send()


def place_rank(k, brick_row, rank_row, live, time_row, ray_row, pay, send):
    lanes = iota((128, 128), 1)
    picked = jnp.where((iota((128, 128), 0).astype(f32) == brick_row) & (rank_row == k) & live, 1.0, 0.0)
    rows = jnp.dot(picked.astype(bf16), pay[...], preferred_element_type=f32)
    z, col, w = from_payload(rows)
    send[:, k, :] = col * 128.0 + z
    send[:, 2 + k, :] = w
    value = jnp.sum(picked * time_row, axis=1, keepdims=True)
    ray = jnp.sum(picked * (ray_row + 1).astype(f32), axis=1, keepdims=True)
    marks = rows[:, 768:896]
    if k == 0:
        send[:, 4, :] = jnp.where(lanes == 0, value, jnp.where(lanes == 2, ray, jnp.where(lanes < 8, marks, 0.0)))
    else:
        send[:, 4, :] = jnp.where(lanes == 1, value, jnp.where(lanes == 3, ray, jnp.where(lanes < 8, send[:, 4, :], marks)))


def onehot_cols(col_row):
    at = jnp.broadcast_to(col_row.astype(i16), (BLOCK, 128))
    return jnp.where(lax.broadcasted_iota(i16, (BLOCK, 128), 0) == at, jnp.ones((), bf16), jnp.zeros((), bf16))


def onehot_values(dep_row, val_row):
    at = jnp.broadcast_to(dep_row.astype(i16), (DEP, 128))
    here = lax.broadcasted_iota(i16, (DEP, 128), 0) == at
    return jnp.concatenate(
        [jnp.where(here, jnp.broadcast_to(part, (DEP, 128)), jnp.zeros((), bf16)) for part in split2(val_row)], axis=0)


def scatter_rows(acc, chunks, col, dep, val):
    acc[...] = jnp.zeros_like(acc)

    def body(c, carry):
        rows = [pl.ds(c * CHUNK + j, 1) for j in range(CHUNK)]
        for b in range(BLOCKS):
            left = jnp.concatenate([onehot_cols(col(b, r)) for r in rows], axis=1)
            right = jnp.concatenate([onehot_values(dep(b, r), val(b, r)) for r in rows], axis=1)
            acc[b] += lax.dot_general(left, right, (((1,), (1,)), ((), ())), preferred_element_type=f32)
        return carry

    lax.fori_loop(0, chunks, body, 0)


def gather_rows(gt, chunks, col, dep, w, out):
    out[...] = jnp.zeros_like(out)

    def body(c, carry):
        rows = [pl.ds(c * CHUNK + j, 1) for j in range(CHUNK)]
        sums = [jnp.zeros((8, 128), f32)] * CHUNK
        for b in range(BLOCKS):
            right = jnp.concatenate([onehot_cols(col(b, r)) for r in rows], axis=1)
            res = jnp.dot(gt[:, b * BLOCK:(b + 1) * BLOCK], right, preferred_element_type=f32)
            for j, r in enumerate(rows):
                at = slice(j * 128, (j + 1) * 128)
                both = res[0:128, at] + res[128:256, at]
                here = jnp.where(iota((DEP, 128), 0) == dep(b, r), both, 0.0)
                sums[j] = sums[j] + here.reshape(16, 8, 128).sum(axis=0) * w(b, r)
        for j, r in enumerate(rows):
            out[r, :] = jnp.sum(sums[j], axis=0, keepdims=True)
        return carry

    lax.fori_loop(0, chunks, body, 0)


def pair(x):
    x = x.reshape(16, 16, 128)
    return jnp.where(iota((16, 8, 128), 2) < HALF, x[:, 0:8], x[:, 8:16]).reshape(128, 128)


def unpair(x):
    low = iota((128, 128), 1) < HALF
    halves = [jnp.sum(jnp.where(m, x, 0.0), axis=1, keepdims=True) for m in (low, ~low)]
    return jnp.concatenate([h.reshape(16, 8, 1) for h in halves], axis=1).reshape(SLOTS, 1)


def bucket(n, starts, col, dep, w, bcol, bdep, bw):
    rank = iota((SLOTS, 128), 1) & (HALF - 1)
    most = jnp.zeros((SLOTS, 1), i32)
    for b in range(BLOCKS):
        first = starts[:, b:b + 1]
        held = (starts[:, b + 1:b + 2] if b + 1 < BLOCKS else SEG) - first
        at = (first + rank) & (SEG - 1)
        bcol[b] = pair(take(col, at) - b * BLOCK)
        bdep[b] = pair(take(dep, at))
        bw[b] = pair(jnp.where(rank < held, take(w, at), 0.0))
        most = jnp.maximum(most, held)
    most = jnp.where(iota((SLOTS, 1), 0) < n, most, 0)
    return jnp.max(most.astype(f32)).astype(i32)


def both_passes(n, most, y_col, col, dep, w, bcol, bdep, bw, finish_q, q_out, acc, gt, wy, vals, part):
    fits = most <= HALF

    def whole():
        q = jnp.concatenate([acc[b, :, 0:128] + acc[b, :, 128:256] for b in range(BLOCKS)], axis=0)
        q = finish_q(q)
        q_out[...] = q
        hi, lo = split2(q.T)
        gt[0:128, :] = hi
        gt[128:256, :] = lo

    @pl.when(fits)
    def _():
        chunks = (n + 2 * CHUNK - 1) // (2 * CHUNK)
        y = pair(jnp.broadcast_to(y_col, (SLOTS, 128)))
        for b in range(BLOCKS):
            wy[b] = bw[b] * y
        cols, deps = (lambda b, r: bcol[b, r, :]), (lambda b, r: bdep[b, r, :])
        scatter_rows(acc, chunks, cols, deps, lambda b, r: wy[b, r, :])
        whole()
        gather_rows(gt, chunks, cols, deps, lambda b, r: bw[b, r, :], vals.at[pl.ds(0, 128)])
        part[...] = unpair(vals[0:128, :])

    @pl.when(jnp.logical_not(fits))
    def _():
        chunks = (n + CHUNK - 1) // CHUNK
        vals[...] = w[...] * y_col
        cols, deps = (lambda b, r: col[r, :] - b * BLOCK), (lambda b, r: dep[r, :])
        scatter_rows(acc, chunks, cols, deps, lambda b, r: vals[r, :])
        whole()
        gather_rows(gt, chunks, cols, deps, lambda b, r: w[r, :], vals)
        part[...] = jnp.sum(vals[...], axis=1, keepdims=True)


def place_of(slot_info):
    return jnp.where(iota((SLOTS, SLOTS), 0) == slot_info, 1.0, 0.0)


def to_rays(partial, place, rays):
    row = jnp.sum(place * partial, axis=0, keepdims=True)
    total = jnp.zeros((RAYS, NDEV), f32)
    for k in range(2):
        at = slice(k * 128, (k + 1) * 128)
        total += jnp.where(iota((RAYS, NDEV), 0) == rays[:, at], row[:, at], 0.0)
    return total


def from_rays(values, place, rays):
    rows = [
        jnp.sum(jnp.where(iota((RAYS, NDEV), 0) == rays[:, k * 128:(k + 1) * 128], values, 0.0), axis=0, keepdims=True)
        for k in range(2)
    ]
    return jnp.sum(place * jnp.concatenate(rows, axis=1), axis=1, keepdims=True)


def total_of(x):
    return jnp.sum(jnp.sum(x, axis=0, keepdims=True), axis=1, keepdims=True)


def as_row(values):
    row = jnp.zeros((8, NDEV), f32)
    for k, value in enumerate(values):
        row = jnp.where(iota((8, NDEV), 1) == k, value, row)
    return row


def first_kernel(held, q_out, p_out, col, dep, w, bcol, bdep, bw, info, count, acc, gt, wy, vals, part):
    meta = held[:, 4, :]
    across = meta.T
    y_row = jnp.concatenate([across[0:1, :], across[1:2, :]], axis=1)
    ray_row = jnp.concatenate([across[2:3, :], across[3:4, :]], axis=1).astype(i32) - 1
    live = ray_row >= 0
    flags = jnp.broadcast_to(jnp.where(live, 1.0, 0.0), (8, SLOTS)).astype(bf16)
    before = jnp.where(iota((SLOTS, SLOTS), 0) < iota((SLOTS, SLOTS), 1), 1.0, 0.0).astype(bf16)
    at = jnp.dot(flags, before, preferred_element_type=f32)[0:1, :].astype(i32)
    at = jnp.where(live, at, -1)
    info[0:1, :] = at
    info[1:2, :] = ray_row
    n = jnp.sum(jnp.where(live, 1.0, 0.0)).astype(i32)
    place = place_of(at)
    pay = jnp.concatenate([as_payload(held[:, k, :].astype(i32), held[:, 2 + k, :]) for k in range(2)], axis=0)
    marks = jnp.concatenate([meta, pltpu.roll(meta, 124, 1)], axis=0).astype(bf16)
    rows = jnp.dot(place.astype(bf16), jnp.concatenate([pay, marks], axis=1), preferred_element_type=f32)
    z, c, lens = from_payload(rows)
    col[...] = c.astype(i32)
    dep[...] = z.astype(i32)
    w[...] = lens
    most = bucket(n, rows[:, 772:776].astype(i32), col[...], dep[...], lens, bcol, bdep, bw)
    count[0] = n
    count[1] = most
    y_col = jnp.sum(place * y_row, axis=1, keepdims=True)
    both_passes(n, most, y_col, col, dep, w, bcol, bdep, bw, lambda q: q, q_out, acc, gt, wy, vals, part)
    p_out[0:RAYS, :] = to_rays(part[...], place_of(at), ray_row)
    q = q_out[...]
    p_out[RAYS:RAYS + 8, :] = as_row([total_of(q * q)])


def second_kernel(p, shift, q0, smooth, col, dep, w, bcol, bdep, bw, info, count, e_out, p_out, dots, acc, gt, wy, vals,
                  part):
    place = place_of(info[0:1, :])
    ray_row = info[1:2, :]
    y_col = from_rays(p[...], place, ray_row)
    finish_q = lambda q: q + smooth[...] - shift[0:1, 0:1] * q0[...]
    both_passes(count[0], count[1], y_col, col, dep, w, bcol, bdep, bw, finish_q, e_out, acc, gt, wy, vals, part)
    p_out[...] = to_rays(part[...], place, ray_row)
    e = e_out[...]
    dots[...] = as_row([total_of(e * q0[...]), total_of(e * e)])


def shape(dims, dtype=f32):
    return jax.ShapeDtypeStruct(dims, dtype)


SCRATCH = [
    pltpu.VMEM((BLOCKS, BLOCK, 256), f32),
    pltpu.VMEM((256, COLS), bf16),
    pltpu.VMEM((BLOCKS, 128, 128), f32),
    pltpu.VMEM((SLOTS, SEG), f32),
    pltpu.VMEM((SLOTS, 1), f32),
]


STAGES = ((1, 0), (2,), (3,))
ROUNDS = ((1, 0), (2, 3))


def send_stage(s, here, group, buf, got, send_sem, recv_sem):
    copies = []
    for k, peer in enumerate(stage_peers(here, group)):
        copy = pltpu.make_async_remote_copy(
            buf.at[s], got.at[s, k], send_sem.at[s, k], recv_sem.at[s, k], device_id=peer, device_id_type=MESH)
        copy.start()
        copies.append(copy)
    return copies


def add_stage(s, copies, buf, got):
    total = buf[s]
    for k, copy in enumerate(copies):
        copy.wait_recv()
        total = total + got[s, k]
    return total


def send_halo(here, field, edge, halo, send_sem, recv_sem):
    edge[0] = field[pl.ds(CLAT - 1, CLON, stride=CLAT), :]
    edge[1] = field[pl.ds(0, CLON, stride=CLAT), :]
    faces = (field.at[pl.ds(COLS - CLAT, CLAT)], field.at[pl.ds(0, CLAT)], edge.at[0], edge.at[1])
    copies = []
    for k, (face, peer) in enumerate(zip(faces, ring_peers(here))):
        copy = pltpu.make_async_remote_copy(
            face, halo.at[k], send_sem.at[k], recv_sem.at[k], device_id=peer, device_id_type=MESH)
        copy.start()
        copies.append(copy)
    return copies


def stencil_rows(here, field, halo, put):
    lat = here[2] * 4 + here[3]
    has_before = jnp.where(lat > 0, 1.0, 0.0)
    has_after = jnp.where(lat < 15, 1.0, 0.0)
    row, lane = iota((CLAT, DEP), 0), iota((CLAT, DEP), 1)

    def layer(i, before, after):
        mine = pl.ds(i * CLAT, CLAT)
        f = field[mine, :]
        lat_before = jnp.where(row == 0, halo[2, i:i + 1, :] * has_before, pltpu.roll(f, 1, 0))
        lat_after = jnp.where(row == CLAT - 1, halo[3, i:i + 1, :] * has_after, pltpu.roll(f, CLAT - 1, 0))
        up = jnp.where(lane == 0, 0.0, pltpu.roll(f, 1, 1))
        down = jnp.where(lane == DEP - 1, 0.0, pltpu.roll(f, DEP - 1, 1))
        put(mine, DAMP * (6.0 * f - before - after - lat_before - lat_after - up - down))

    for i in range(CLON):
        before = field[(i - 1) * CLAT:i * CLAT, :] if i else halo[0]
        after = field[(i + 1) * CLAT:(i + 2) * CLAT, :] if i < CLON - 1 else halo[1]
        layer(i, before, after)


def finish(copies):
    for copy in copies:
        copy.wait_send()


def middle_kernel(p_part, q, p_out, shift, smooth, buf, got, g, edge, halo, send_sem, recv_sem, face_send, face_recv):
    here = coords()
    meet([p for group in STAGES for p in stage_peers(here, group)] + ring_peers(here)[2:])
    buf[0] = p_part[...]
    first = send_stage(0, here, STAGES[0], buf, got, send_sem, recv_sem)
    faces = send_halo(here, q, edge.at[0], halo.at[0], face_send.at[0], face_recv.at[0])
    buf[1] = add_stage(0, first, buf, got)
    second = send_stage(1, here, STAGES[1], buf, got, send_sem, recv_sem)
    for copy in faces:
        copy.wait_recv()

    def to_g(rows, value):
        g[rows, :] = value

    stencil_rows(here, q, halo.at[0], to_g)
    more = send_halo(here, g, edge.at[1], halo.at[1], face_send.at[1], face_recv.at[1])
    buf[2] = add_stage(1, second, buf, got)
    third = send_stage(2, here, STAGES[2], buf, got, send_sem, recv_sem)
    for copy in more:
        copy.wait_recv()

    def to_smooth(rows, value):
        smooth[rows, :] = value

    stencil_rows(here, g, halo.at[1], to_smooth)
    total = add_stage(2, third, buf, got)
    p = total[0:RAYS, :]
    p_out[...] = p
    shift[...] = as_row([total_of(p * p) / total[RAYS:RAYS + 1, 0:1], total[RAYS:RAYS + 1, 0:1]])
    finish(first + second + third + faces + more)


def last_kernel(count, times, p_part, p0, shift, dots, q0, e, model, misfit, buf, got, small, small_got, norm, edge, halo,
                send_sem, recv_sem, small_send, small_recv, face_send, face_recv):
    here = coords()
    meet([p for group in ROUNDS for p in stage_peers(here, group)])
    faces = send_halo(here, e, edge, halo, face_send, face_recv)
    buf[0] = p_part[...]
    first = send_stage(0, here, STAGES[0], buf, got, send_sem, recv_sem)
    norm[...] = jnp.zeros_like(norm)
    for copy in faces:
        copy.wait_recv()

    def to_norm(rows, value):
        norm[...] += value * value

    stencil_rows(here, e, halo, to_norm)
    small[0] = jnp.where(iota((8, NDEV), 1) == 2, total_of(norm[...]), dots[...])
    one = send_stage(0, here, ROUNDS[0], small, small_got, small_send, small_recv)
    buf[1] = add_stage(0, first, buf, got)
    second = send_stage(1, here, STAGES[1], buf, got, send_sem, recv_sem)
    small[1] = add_stage(0, one, small, small_got)
    two = send_stage(1, here, ROUNDS[1], small, small_got, small_send, small_recv)
    buf[2] = add_stage(1, second, buf, got)
    third = send_stage(2, here, STAGES[2], buf, got, send_sem, recv_sem)
    moments = add_stage(1, two, small, small_got)
    pe = add_stage(2, third, buf, got)
    mu, m0 = shift[0:1, 0:1], shift[0:1, 1:2]
    s, big = moments[0:1, 0:1] / m0, moments[0:1, 1:2] / m0
    r = (moments[0:1, 2:3] + total_of(pe * pe)) / m0
    cross = big + mu * s
    det = (s + mu) * r - cross * cross
    a, b = (r - s * cross) / det, (s * s - big) / det
    model[...] = (SCALE * a) * q0[...] + (SCALE * b) * e[...]
    fit = jnp.where(iota((RAYS, NDEV), 1) == flat(here), a * p0[...] + b * pe, 0.0)
    column = jnp.sum(fit, axis=1, keepdims=True)
    own = jnp.sum(jnp.where(iota((RAYS, RAYS), 0) == iota((RAYS, RAYS), 1), column, 0.0), axis=0, keepdims=True)
    data = jnp.where(iota((1, RAYS), 1) < count[0], times[...], 0.0)
    misfit[...] = data - own
    finish(faces + first + second + third + one + two)


def comm_params(number, room=16 << 20):
    return pltpu.CompilerParams(vmem_limit_bytes=room, collective_id=number, has_side_effects=True)


def face_scratch(*dims):
    return [pltpu.VMEM(dims + (2, CLON, DEP), f32), pltpu.VMEM(dims + (4, CLON, DEP), f32)]


def sems(*dims):
    return [pltpu.SemaphoreType.DMA(dims), pltpu.SemaphoreType.DMA(dims)]


def shards(travel_times, ray_counts, tile_brick, cell_offsets, cell_depths, seg_lengths):
    times = travel_times.reshape(1, RAYS)
    held = pl.pallas_call(
        send_kernel,
        out_shape=shape((NDEV, 5, SEG)),
        in_specs=[SMEM] + [VMEM] * 2 + [pl.BlockSpec(memory_space=pltpu.MemorySpace.HBM)] * 3,
        out_specs=VMEM,
        scratch_shapes=[pltpu.VMEM((NDEV, 5, SEG), f32), pltpu.VMEM((128, 896), bf16)]
        + [pltpu.VMEM((RAYS, TPR, SEG), d) for d in (i32, i32, f32)]
        + [pltpu.SemaphoreType.DMA((3,)), pltpu.SemaphoreType.REGULAR((3,)), pltpu.SemaphoreType.DMA, pltpu.SemaphoreType.DMA],
        compiler_params=comm_params(2, 60 << 20),
    )(ray_counts, tile_brick.T, times, cell_offsets, cell_depths, seg_lengths)
    entries = [shape((SLOTS, SEG), d) for d in (i32, i32, f32)] + [shape((BLOCKS, 128, 128), d) for d in (i32, i32, f32)]
    q0, p_part, *lists, info, count = pl.pallas_call(
        first_kernel,
        out_shape=(shape((COLS, DEP)), shape((RAYS + 8, NDEV)), *entries, shape((2, SLOTS), i32), shape((2,), i32)),
        in_specs=[VMEM],
        out_specs=(VMEM,) * 9 + (SMEM,),
        scratch_shapes=SCRATCH,
        compiler_params=PARAMS,
    )(held)
    p0, shift, smooth = pl.pallas_call(
        middle_kernel,
        out_shape=(shape((RAYS, NDEV)), shape((8, NDEV)), shape((COLS, DEP))),
        in_specs=[VMEM] * 2,
        out_specs=(VMEM,) * 3,
        scratch_shapes=[pltpu.VMEM((3, RAYS + 8, NDEV), f32), pltpu.VMEM((3, 7, RAYS + 8, NDEV), f32),
                        pltpu.VMEM((COLS, DEP), f32)] + face_scratch(2) + sems(3, 7) + sems(2, 4),
        compiler_params=comm_params(0),
    )(p_part, q0)
    e, p_part, dots = pl.pallas_call(
        second_kernel,
        out_shape=(shape((COLS, DEP)), shape((RAYS, NDEV)), shape((8, NDEV))),
        in_specs=[VMEM] * 11 + [SMEM],
        out_specs=(VMEM,) * 3,
        scratch_shapes=SCRATCH,
        compiler_params=PARAMS,
    )(p0, shift, q0, smooth, *lists, info, count)
    model, misfit = pl.pallas_call(
        last_kernel,
        out_shape=(shape((COLS, DEP)), shape((1, RAYS))),
        in_specs=[SMEM] + [VMEM] * 7,
        out_specs=(VMEM,) * 2,
        scratch_shapes=[pltpu.VMEM((3, RAYS, NDEV), f32), pltpu.VMEM((3, 7, RAYS, NDEV), f32),
                        pltpu.VMEM((2, 8, NDEV), f32), pltpu.VMEM((2, 15, 8, NDEV), f32), pltpu.VMEM((CLAT, DEP), f32)]
        + face_scratch() + sems(3, 7) + sems(2, 15) + sems(4),
        compiler_params=comm_params(1),
    )(ray_counts, times, p_part, p0, shift, dots, q0, e)
    return (model.reshape(CLON, CLAT, DEP), misfit.reshape(RAYS))


def solution(mesh):
    torus = Mesh(mesh.devices.reshape(4, 2, 4, 4), LON_LAT)
    in_specs = (
        P(LON_LAT),
        P(LON_LAT),
        P(LON_LAT, None),
        P(LON_LAT, None, None),
        P(LON_LAT, None, None),
        P(LON_LAT, None, None),
    )
    out_specs = (P(LON, LAT, None), P(LON_LAT))
    return jax.shard_map(shards, mesh=torus, in_specs=in_specs, out_specs=out_specs, check_vma=False)
```

```python
import itertools

import jax
import jax.numpy as jnp
from jax import lax
from jax.experimental import pallas as pl
from jax.experimental.pallas import tpu as pltpu
from jax.sharding import Mesh
from jax.sharding import PartitionSpec as P

CLON, CLAT, DEP, SEG = 32, 32, 128, 128
COLS = CLON * CLAT
RAYS, TPR = 32, 4
NDEV = 128
SLOTS = 2 * NDEV
CHUNK = 8
BLOCKS, BLOCK = 4, 256
GROUPS, SHARE = 6, 6
TILES, PLACES, ROWS = 8 * SHARE, 8 * SHARE * GROUPS, 16 * GROUPS
SCALE = 8.0
DAMP = 0.01 * SCALE
LON_LAT = ("lon_0", "lon_1", "lat_0", "lat_1")
LON = ("lon_0", "lon_1")
LAT = ("lat_0", "lat_1")

f32, bf16, i32, i16 = jnp.float32, jnp.bfloat16, jnp.int32, jnp.int16
VMEM = pl.BlockSpec(memory_space=pltpu.VMEM)
SMEM = pl.BlockSpec(memory_space=pltpu.SMEM)
PARAMS = pltpu.CompilerParams(vmem_limit_bytes=48 << 20)


MESH = pl.DeviceIdType.MESH
SIZES = (4, 2, 4, 4)


def coords():
    return tuple(lax.axis_index(a) for a in LON_LAT)


def flat(at):
    return ((at[0] * 2 + at[1]) * 4 + at[2]) * 4 + at[3]


def stage_peers(here, group):
    found = []
    for steps in itertools.product(*[range(SIZES[a]) for a in group]):
        if any(steps):
            add = dict(zip(group, steps))
            found.append(tuple((v + add.get(i, 0)) % SIZES[i] for i, v in enumerate(here)))
    return found


def ring_peers(here):
    lon, lat = here[0] * 2 + here[1], here[2] * 4 + here[3]
    found = []
    for step in (1, 7):
        to = (lon + step) % 8
        found.append((to // 2, to % 2, here[2], here[3]))
    for step in (1, 15):
        to = (lat + step) % 16
        found.append((here[0], here[1], to // 4, to % 4))
    return found


def meet(peers):
    barrier = pltpu.get_barrier_semaphore()
    for peer in peers:
        pl.semaphore_signal(barrier, inc=1, device_id=peer, device_id_type=MESH)
    pl.semaphore_wait(barrier, len(peers))


def iota(shape, dim):
    return lax.broadcasted_iota(i32, shape, dim)


def split2(x):
    hi = x.astype(bf16)
    return hi, (x - hi.astype(f32)).astype(bf16)


def split3(x):
    hi = x.astype(bf16)
    rest = x - hi.astype(f32)
    mid = rest.astype(bf16)
    return hi, mid, (rest - mid.astype(f32)).astype(bf16)


def as_payload(cell, lens):
    col = cell >> 7
    parts = [(cell & 127), (col & 127), (col >> 7)]
    return jnp.concatenate([p.astype(f32).astype(bf16) for p in parts] + list(split3(lens)), axis=1)


def from_payload(rows):
    z, low, high, hi, mid, lo = [rows[:, k * 128:(k + 1) * 128] for k in range(6)]
    return z, high * 128.0 + low, (hi + mid) + lo


def prefix(flags):
    upto = jnp.where(iota((128, 128), 0) <= iota((128, 128), 1), 1.0, 0.0).astype(bf16)
    return jnp.dot(jnp.where(flags, 1.0, 0.0).astype(bf16), upto, preferred_element_type=f32).astype(i32)


def take(x, index):
    return jnp.take_along_axis(x, index, axis=1, mode="promise_in_bounds")


def by_block(cell, w):
    counts = [prefix((cell >> 15) == b) for b in range(BLOCKS)]
    starts = [jnp.zeros((128, 1), i32)]
    for b in range(BLOCKS - 1):
        starts.append(starts[-1] + counts[b][:, 127:128])
    lane = iota((128, 128), 1)
    block, rank = jnp.zeros((128, 128), i32), lane
    for b in range(1, BLOCKS):
        block = jnp.where(lane >= starts[b], b, block)
        rank = jnp.where(lane >= starts[b], lane - starts[b], rank)
    at = jnp.zeros((128, 128), i32)
    for step in (64, 32, 16, 8, 4, 2, 1):
        probe = at + (step - 1)
        seen = take(counts[0], probe)
        for b in range(1, BLOCKS):
            seen = jnp.where(block == b, take(counts[b], probe), seen)
        at = jnp.where(seen <= rank, at + step, at)
    marks = jnp.zeros((128, 128), f32)
    for b in range(1, BLOCKS):
        marks = jnp.where((lane == 4 + b) | (lane == 8 + b), starts[b].astype(f32), marks)
    return take(cell, at), take(w, at), marks


def send_kernel(count, brick, times, offs_in, deps_in, lens_in, held, send, pay, offs, deps, lens, load_sem, meet_sem,
                send_sem, recv_sem):
    here = coords()
    loads = [
        pltpu.make_async_copy(src, dst, load_sem.at[k])
        for k, (src, dst) in enumerate(((offs_in, offs), (deps_in, deps), (lens_in, lens)))
    ]
    for load in loads:
        load.start()
    barrier = pltpu.get_barrier_semaphore()
    lines = [p for axis in range(4) for p in stage_peers(here, (axis,))]
    for peer in lines:
        pl.semaphore_signal(barrier, inc=1, device_id=peer, device_id_type=MESH)
    tb = brick[...].astype(f32)
    brick_row = jnp.concatenate([tb[k:k + 1, :] for k in range(TPR)], axis=1)
    time_row = jnp.concatenate([times[...]] * TPR, axis=1)
    ray_row = iota((1, 128), 1) & 31
    live = ray_row < count[0]
    as_rows = jnp.broadcast_to(brick_row, (128, 128))
    same = (as_rows == as_rows.T) & (iota((128, 128), 0) < iota((128, 128), 1))
    rank_row = jnp.sum(jnp.where(same, 1.0, 0.0), axis=0, keepdims=True)
    for load in loads:
        load.wait()
    cell = jnp.concatenate([offs[:, k, :] * DEP + deps[:, k, :] for k in range(TPR)], axis=0)
    w = jnp.concatenate([lens[:, k, :] * SCALE for k in range(TPR)], axis=0)
    cell, w, marks = by_block(cell, w)
    pay[:, 0:768] = as_payload(cell, w)
    pay[:, 768:896] = marks.astype(bf16)
    pl.semaphore_wait(barrier, len(lines))
    for s, axis in enumerate((0, 2, 3)):
        peers = stage_peers(here, (axis,))
        for peer in peers:
            pl.semaphore_signal(meet_sem.at[s], inc=1, device_id=peer, device_id_type=MESH)
        if s < 2:
            place_rank(s, brick_row, rank_row, live, time_row, ray_row, pay, send)
        pl.semaphore_wait(meet_sem.at[s], len(peers))
    me = flat(here)

    def go(step, carry):
        steps = (step // 32, (step // 16) % 2, (step // 4) % 4, step % 4)
        peer = tuple((v + d) % n for v, d, n in zip(here, steps, SIZES))
        pltpu.make_async_remote_copy(
            send.at[flat(peer)], held.at[me], send_sem, recv_sem, device_id=peer, device_id_type=MESH).start()
        return carry

    lax.fori_loop(1, NDEV, go, 0)
    held[me] = send[me]
    rest = pl.ds(0, NDEV - 1)
    every = pltpu.make_async_remote_copy(
        send.at[rest], held.at[rest], send_sem, recv_sem, device_id=here, device_id_type=MESH)
    every.wait_recv()
    every.wait_send()


def place_rank(k, brick_row, rank_row, live, time_row, ray_row, pay, send):
    lanes = iota((128, 128), 1)
    picked = jnp.where((iota((128, 128), 0).astype(f32) == brick_row) & (rank_row == k) & live, 1.0, 0.0)
    rows = jnp.dot(picked.astype(bf16), pay[...], preferred_element_type=f32)
    z, col, w = from_payload(rows)
    send[:, k, :] = col * 128.0 + z
    send[:, 2 + k, :] = w
    value = jnp.sum(picked * time_row, axis=1, keepdims=True)
    ray = jnp.sum(picked * (ray_row + 1).astype(f32), axis=1, keepdims=True)
    marks = rows[:, 768:896]
    if k == 0:
        send[:, 4, :] = jnp.where(lanes == 0, value, jnp.where(lanes == 2, ray, jnp.where(lanes < 8, marks, 0.0)))
    else:
        send[:, 4, :] = jnp.where(lanes == 1, value, jnp.where(lanes == 3, ray, jnp.where(lanes < 8, send[:, 4, :], marks)))


def onehot_cols(col_row):
    at = jnp.broadcast_to(col_row.astype(i16), (BLOCK, 128))
    return jnp.where(lax.broadcasted_iota(i16, (BLOCK, 128), 0) == at, jnp.ones((), bf16), jnp.zeros((), bf16))


def onehot_values(dep_row, val_row):
    at = jnp.broadcast_to(dep_row.astype(i16), (DEP, 128))
    here = lax.broadcasted_iota(i16, (DEP, 128), 0) == at
    return jnp.concatenate(
        [jnp.where(here, jnp.broadcast_to(part, (DEP, 128)), jnp.zeros((), bf16)) for part in split2(val_row)], axis=0)


def scatter_rows(acc, chunks, col, dep, val):
    acc[...] = jnp.zeros_like(acc)

    def body(c, carry):
        rows = [pl.ds(c * CHUNK + j, 1) for j in range(CHUNK)]
        for b in range(BLOCKS):
            left = jnp.concatenate([onehot_cols(col(b, r)) for r in rows], axis=1)
            right = jnp.concatenate([onehot_values(dep(b, r), val(b, r)) for r in rows], axis=1)
            acc[b] += lax.dot_general(left, right, (((1,), (1,)), ((), ())), preferred_element_type=f32)
        return carry

    lax.fori_loop(0, chunks, body, 0)


def gather_rows(gt, chunks, col, dep, w, out):
    out[...] = jnp.zeros_like(out)

    def body(c, carry):
        rows = [pl.ds(c * CHUNK + j, 1) for j in range(CHUNK)]
        for b in range(BLOCKS):
            right = jnp.concatenate([onehot_cols(col(b, r)) for r in rows], axis=1)
            res = jnp.dot(gt[:, b * BLOCK:(b + 1) * BLOCK], right, preferred_element_type=f32)
            for j, r in enumerate(rows):
                at = slice(j * 128, (j + 1) * 128)
                both = res[0:128, at] + res[128:256, at]
                here = jnp.where(iota((DEP, 128), 0) == dep(b, r), both, 0.0)
                out[b, r, :] = jnp.sum(here, axis=0, keepdims=True) * w(b, r)
        return carry

    lax.fori_loop(0, chunks, body, 0)


def bucket(n, starts, cell, w, bcol, bdep, bw, btile):
    alive = iota((PLACES, 1), 0) < n
    group = iota((GROUPS, 8, 1), 0)
    last = (n - 1) // TILES
    cells = cell.reshape(GROUPS, SHARE, 8, 128)
    ws = w.reshape(GROUPS, SHARE, 8, 128)
    most = jnp.zeros((GROUPS, 8, 1), i32)
    for b in range(BLOCKS):
        first = starts[:, b:b + 1]
        held = jnp.where(alive, (starts[:, b + 1:b + 2] if b + 1 < BLOCKS else SEG) - first, 0)
        first, held = first.reshape(GROUPS, SHARE, 8, 1), held.reshape(GROUPS, SHARE, 8, 1)
        for h in range(2):
            spot = iota((GROUPS, 8, 128), 2) + h * 128
            before = jnp.zeros((GROUPS, 8, 1), i32)
            own_cell, own_w = jnp.zeros((GROUPS, 8, 128), i32), jnp.zeros((GROUPS, 8, 128), f32)
            tile = jnp.zeros((GROUPS, 8, 128), i32)
            for k in range(SHARE):
                at = ((first[:, k] + spot - before) & (SEG - 1)).reshape(GROUPS * 8, 128)
                mine = spot >= before
                own_cell = jnp.where(mine, take(cells[:, k].reshape(GROUPS * 8, 128), at).reshape(GROUPS, 8, 128), own_cell)
                own_w = jnp.where(mine, take(ws[:, k].reshape(GROUPS * 8, 128), at).reshape(GROUPS, 8, 128), own_w)
                tile = jnp.where(mine, k, tile)
                before = before + held[:, k]
            own_w = jnp.where(spot < before, own_w, 0.0)
            for g in range(GROUPS):
                rows = slice(g * 16 + h * 8, g * 16 + h * 8 + 8)
                bcol[b, rows, :] = (own_cell[g] >> 7) - b * BLOCK
                bdep[b, rows, :] = own_cell[g] & 127
                bw[b, rows, :] = own_w[g]
                btile[b, rows, :] = tile[g]
        most = jnp.maximum(most, before)
    ending = jnp.max(jnp.where(group == last, most, 0).astype(f32)).astype(i32)
    chunks = 2 * (last + 1) - jnp.where(ending <= 128, 1, 0)
    return jnp.max(most.astype(f32)).astype(i32), jnp.where(n > 0, chunks, 0)


def per_entry(y_col, tile):
    y = y_col.reshape(GROUPS, SHARE, 8, 1)
    tile = tile.reshape(GROUPS, 2, 8, 128)
    spread = jnp.zeros((GROUPS, 2, 8, 128), f32)
    for k in range(SHARE):
        spread = jnp.where(tile == k, y[:, k:k + 1], spread)
    return spread.reshape(ROWS, 128)


def per_tile(vals, btile):
    sums = [jnp.zeros((GROUPS, 8, 128), f32)] * SHARE
    for b in range(BLOCKS):
        value = vals[b, 0:ROWS, :].reshape(GROUPS, 2, 8, 128)
        tile = btile[b].reshape(GROUPS, 2, 8, 128)
        for k in range(SHARE):
            mine = jnp.where(tile == k, value, 0.0)
            sums[k] = sums[k] + mine[:, 0] + mine[:, 1]
    columns = [jnp.sum(x, axis=2, keepdims=True)[:, None] for x in sums]
    return jnp.concatenate(columns, axis=1).reshape(PLACES, 1)


def both_passes(count, y_col, cell, w, bcol, bdep, bw, btile, finish_q, q_out, acc, gt, wy, vals, part):
    fits = count[1] <= 256

    def whole():
        q = finish_q(jnp.concatenate([acc[b, :, 0:128] + acc[b, :, 128:256] for b in range(BLOCKS)], axis=0))
        q_out[...] = q
        hi, lo = split2(q.T)
        gt[0:128, :] = hi
        gt[128:256, :] = lo

    @pl.when(fits)
    def _():
        for b in range(BLOCKS):
            wy[b, 0:ROWS, :] = bw[b] * per_entry(y_col, btile[b])
        cols, deps = (lambda b, r: bcol[b, r, :]), (lambda b, r: bdep[b, r, :])
        scatter_rows(acc, count[2], cols, deps, lambda b, r: wy[b, r, :])
        whole()
        gather_rows(gt, count[2], cols, deps, lambda b, r: bw[b, r, :], vals)
        part[...] = per_tile(vals, btile)

    @pl.when(jnp.logical_not(fits))
    def _():
        chunks = (count[0] + CHUNK - 1) // CHUNK
        wy[0] = w[...] * y_col
        cols, deps = (lambda b, r: (cell[r, :] >> 7) - b * BLOCK), (lambda b, r: cell[r, :] & 127)
        scatter_rows(acc, chunks, cols, deps, lambda b, r: wy[0, r, :])
        whole()
        gather_rows(gt, chunks, cols, deps, lambda b, r: w[r, :], vals)
        part[...] = jnp.sum((vals[0] + vals[1]) + (vals[2] + vals[3]), axis=1, keepdims=True)


def place_of(slot_info):
    return jnp.where(iota((PLACES, SLOTS), 0) == slot_info, 1.0, 0.0)


def to_rays(partial, place, rays):
    row = jnp.sum(place * partial, axis=0, keepdims=True)
    total = jnp.zeros((RAYS, NDEV), f32)
    for k in range(2):
        at = slice(k * 128, (k + 1) * 128)
        total += jnp.where(iota((RAYS, NDEV), 0) == rays[:, at], row[:, at], 0.0)
    return total


def from_rays(values, place, rays):
    rows = [
        jnp.sum(jnp.where(iota((RAYS, NDEV), 0) == rays[:, k * 128:(k + 1) * 128], values, 0.0), axis=0, keepdims=True)
        for k in range(2)
    ]
    return jnp.sum(place * jnp.concatenate(rows, axis=1), axis=1, keepdims=True)


def total_of(x):
    return jnp.sum(jnp.sum(x, axis=0, keepdims=True), axis=1, keepdims=True)


def as_row(values):
    row = jnp.zeros((8, NDEV), f32)
    for k, value in enumerate(values):
        row = jnp.where(iota((8, NDEV), 1) == k, value, row)
    return row


def first_kernel(held, q_out, p_out, cell, w, bcol, bdep, bw, btile, info, count, acc, gt, wy, vals, part):
    meta = held[:, 4, :]
    across = meta.T
    y_row = jnp.concatenate([across[0:1, :], across[1:2, :]], axis=1)
    ray_row = jnp.concatenate([across[2:3, :], across[3:4, :]], axis=1).astype(i32) - 1
    live = ray_row >= 0
    flags = jnp.broadcast_to(jnp.where(live, 1.0, 0.0), (8, SLOTS)).astype(bf16)
    before = jnp.where(iota((SLOTS, SLOTS), 0) < iota((SLOTS, SLOTS), 1), 1.0, 0.0).astype(bf16)
    at = jnp.dot(flags, before, preferred_element_type=f32)[0:1, :].astype(i32)
    at = jnp.where(live, at, -1)
    info[0:1, :] = at
    info[1:2, :] = ray_row
    n = jnp.sum(jnp.where(live, 1.0, 0.0)).astype(i32)
    place = place_of(at)
    pay = jnp.concatenate([as_payload(held[:, k, :].astype(i32), held[:, 2 + k, :]) for k in range(2)], axis=0)
    marks = jnp.concatenate([meta, pltpu.roll(meta, 124, 1)], axis=0).astype(bf16)
    rows = jnp.dot(place.astype(bf16), jnp.concatenate([pay, marks], axis=1), preferred_element_type=f32)
    z, c, lens = from_payload(rows)
    cell[...] = (c * 128.0 + z).astype(i32)
    w[...] = lens
    most, chunks = bucket(n, rows[:, 772:776].astype(i32), cell[...], lens, bcol, bdep, bw, btile)
    count[0] = n
    count[1] = most
    count[2] = chunks
    y_col = jnp.sum(place * y_row, axis=1, keepdims=True)
    both_passes(count, y_col, cell, w, bcol, bdep, bw, btile, lambda q: q, q_out, acc, gt, wy, vals, part)
    p_out[0:RAYS, :] = to_rays(part[...], place_of(at), ray_row)
    q = q_out[...]
    p_out[RAYS:RAYS + 8, :] = as_row([total_of(q * q)])


def second_kernel(p, shift, q0, smooth, cell, w, bcol, bdep, bw, btile, info, count, e_out, p_out, dots, acc, gt, wy, vals,
                  part):
    place = place_of(info[0:1, :])
    ray_row = info[1:2, :]
    y_col = from_rays(p[...], place, ray_row)
    finish_q = lambda q: q + smooth[...] - shift[0:1, 0:1] * q0[...]
    both_passes(count, y_col, cell, w, bcol, bdep, bw, btile, finish_q, e_out, acc, gt, wy, vals, part)
    p_out[...] = to_rays(part[...], place, ray_row)
    e = e_out[...]
    dots[...] = as_row([total_of(e * q0[...]), total_of(e * e)])


def shape(dims, dtype=f32):
    return jax.ShapeDtypeStruct(dims, dtype)


SCRATCH = [
    pltpu.VMEM((BLOCKS, BLOCK, 256), f32),
    pltpu.VMEM((256, COLS), bf16),
    pltpu.VMEM((BLOCKS, PLACES, SEG), f32),
    pltpu.VMEM((BLOCKS, PLACES, SEG), f32),
    pltpu.VMEM((PLACES, 1), f32),
]


STAGES = ((1, 0), (2,), (3,))
ROUNDS = ((1, 0), (2, 3))


def send_stage(s, here, group, buf, got, send_sem, recv_sem):
    copies = []
    for k, peer in enumerate(stage_peers(here, group)):
        copy = pltpu.make_async_remote_copy(
            buf.at[s], got.at[s, k], send_sem.at[s, k], recv_sem.at[s, k], device_id=peer, device_id_type=MESH)
        copy.start()
        copies.append(copy)
    return copies


def add_stage(s, copies, buf, got):
    total = buf[s]
    for k, copy in enumerate(copies):
        copy.wait_recv()
        total = total + got[s, k]
    return total


def send_halo(here, field, edge, halo, send_sem, recv_sem):
    edge[0] = field[pl.ds(CLAT - 1, CLON, stride=CLAT), :]
    edge[1] = field[pl.ds(0, CLON, stride=CLAT), :]
    faces = (field.at[pl.ds(COLS - CLAT, CLAT)], field.at[pl.ds(0, CLAT)], edge.at[0], edge.at[1])
    copies = []
    for k, (face, peer) in enumerate(zip(faces, ring_peers(here))):
        copy = pltpu.make_async_remote_copy(
            face, halo.at[k], send_sem.at[k], recv_sem.at[k], device_id=peer, device_id_type=MESH)
        copy.start()
        copies.append(copy)
    return copies


def stencil_rows(here, field, halo, put):
    lat = here[2] * 4 + here[3]
    has_before = jnp.where(lat > 0, 1.0, 0.0)
    has_after = jnp.where(lat < 15, 1.0, 0.0)
    row, lane = iota((CLAT, DEP), 0), iota((CLAT, DEP), 1)

    def layer(i, before, after):
        mine = pl.ds(i * CLAT, CLAT)
        f = field[mine, :]
        lat_before = jnp.where(row == 0, halo[2, i:i + 1, :] * has_before, pltpu.roll(f, 1, 0))
        lat_after = jnp.where(row == CLAT - 1, halo[3, i:i + 1, :] * has_after, pltpu.roll(f, CLAT - 1, 0))
        up = jnp.where(lane == 0, 0.0, pltpu.roll(f, 1, 1))
        down = jnp.where(lane == DEP - 1, 0.0, pltpu.roll(f, DEP - 1, 1))
        put(mine, DAMP * (6.0 * f - before - after - lat_before - lat_after - up - down))

    for i in range(CLON):
        before = field[(i - 1) * CLAT:i * CLAT, :] if i else halo[0]
        after = field[(i + 1) * CLAT:(i + 2) * CLAT, :] if i < CLON - 1 else halo[1]
        layer(i, before, after)


def finish(copies):
    for copy in copies:
        copy.wait_send()


def middle_kernel(p_part, q, p_out, shift, smooth, buf, got, g, edge, halo, send_sem, recv_sem, face_send, face_recv):
    here = coords()
    meet([p for group in STAGES for p in stage_peers(here, group)] + ring_peers(here)[2:])
    buf[0] = p_part[...]
    first = send_stage(0, here, STAGES[0], buf, got, send_sem, recv_sem)
    faces = send_halo(here, q, edge.at[0], halo.at[0], face_send.at[0], face_recv.at[0])
    buf[1] = add_stage(0, first, buf, got)
    second = send_stage(1, here, STAGES[1], buf, got, send_sem, recv_sem)
    for copy in faces:
        copy.wait_recv()

    def to_g(rows, value):
        g[rows, :] = value

    stencil_rows(here, q, halo.at[0], to_g)
    more = send_halo(here, g, edge.at[1], halo.at[1], face_send.at[1], face_recv.at[1])
    buf[2] = add_stage(1, second, buf, got)
    third = send_stage(2, here, STAGES[2], buf, got, send_sem, recv_sem)
    for copy in more:
        copy.wait_recv()

    def to_smooth(rows, value):
        smooth[rows, :] = value

    stencil_rows(here, g, halo.at[1], to_smooth)
    total = add_stage(2, third, buf, got)
    p = total[0:RAYS, :]
    p_out[...] = p
    shift[...] = as_row([total_of(p * p) / total[RAYS:RAYS + 1, 0:1], total[RAYS:RAYS + 1, 0:1]])
    finish(first + second + third + faces + more)


def last_kernel(count, times, p_part, p0, shift, dots, q0, e, model, misfit, buf, got, small, small_got, norm, edge, halo,
                send_sem, recv_sem, small_send, small_recv, face_send, face_recv):
    here = coords()
    meet([p for group in ROUNDS for p in stage_peers(here, group)])
    faces = send_halo(here, e, edge, halo, face_send, face_recv)
    buf[0] = p_part[...]
    first = send_stage(0, here, STAGES[0], buf, got, send_sem, recv_sem)
    norm[...] = jnp.zeros_like(norm)
    for copy in faces:
        copy.wait_recv()

    def to_norm(rows, value):
        norm[...] += value * value

    stencil_rows(here, e, halo, to_norm)
    small[0] = jnp.where(iota((8, NDEV), 1) == 2, total_of(norm[...]), dots[...])
    one = send_stage(0, here, ROUNDS[0], small, small_got, small_send, small_recv)
    buf[1] = add_stage(0, first, buf, got)
    second = send_stage(1, here, STAGES[1], buf, got, send_sem, recv_sem)
    small[1] = add_stage(0, one, small, small_got)
    two = send_stage(1, here, ROUNDS[1], small, small_got, small_send, small_recv)
    buf[2] = add_stage(1, second, buf, got)
    third = send_stage(2, here, STAGES[2], buf, got, send_sem, recv_sem)
    moments = add_stage(1, two, small, small_got)
    pe = add_stage(2, third, buf, got)
    mu, m0 = shift[0:1, 0:1], shift[0:1, 1:2]
    s, big = moments[0:1, 0:1] / m0, moments[0:1, 1:2] / m0
    r = (moments[0:1, 2:3] + total_of(pe * pe)) / m0
    cross = big + mu * s
    det = (s + mu) * r - cross * cross
    a, b = (r - s * cross) / det, (s * s - big) / det
    model[...] = (SCALE * a) * q0[...] + (SCALE * b) * e[...]
    fit = jnp.where(iota((RAYS, NDEV), 1) == flat(here), a * p0[...] + b * pe, 0.0)
    column = jnp.sum(fit, axis=1, keepdims=True)
    own = jnp.sum(jnp.where(iota((RAYS, RAYS), 0) == iota((RAYS, RAYS), 1), column, 0.0), axis=0, keepdims=True)
    data = jnp.where(iota((1, RAYS), 1) < count[0], times[...], 0.0)
    misfit[...] = data - own
    finish(faces + first + second + third + one + two)


def comm_params(number, room=16 << 20):
    return pltpu.CompilerParams(vmem_limit_bytes=room, collective_id=number, has_side_effects=True)


def face_scratch(*dims):
    return [pltpu.VMEM(dims + (2, CLON, DEP), f32), pltpu.VMEM(dims + (4, CLON, DEP), f32)]


def sems(*dims):
    return [pltpu.SemaphoreType.DMA(dims), pltpu.SemaphoreType.DMA(dims)]


def shards(travel_times, ray_counts, tile_brick, cell_offsets, cell_depths, seg_lengths):
    times = travel_times.reshape(1, RAYS)
    held = pl.pallas_call(
        send_kernel,
        out_shape=shape((NDEV, 5, SEG)),
        in_specs=[SMEM] + [VMEM] * 2 + [pl.BlockSpec(memory_space=pltpu.MemorySpace.HBM)] * 3,
        out_specs=VMEM,
        scratch_shapes=[pltpu.VMEM((NDEV, 5, SEG), f32), pltpu.VMEM((128, 896), bf16)]
        + [pltpu.VMEM((RAYS, TPR, SEG), d) for d in (i32, i32, f32)]
        + [pltpu.SemaphoreType.DMA((3,)), pltpu.SemaphoreType.REGULAR((3,)), pltpu.SemaphoreType.DMA, pltpu.SemaphoreType.DMA],
        compiler_params=comm_params(2, 60 << 20),
    )(ray_counts, tile_brick.T, times, cell_offsets, cell_depths, seg_lengths)
    entries = [shape((PLACES, SEG), d) for d in (i32, f32)] + [shape((BLOCKS, ROWS, 128), d) for d in (i32, i32, f32, i32)]
    q0, p_part, *lists, info, count = pl.pallas_call(
        first_kernel,
        out_shape=(shape((COLS, DEP)), shape((RAYS + 8, NDEV)), *entries, shape((2, SLOTS), i32), shape((3,), i32)),
        in_specs=[VMEM],
        out_specs=(VMEM,) * 9 + (SMEM,),
        scratch_shapes=SCRATCH,
        compiler_params=PARAMS,
    )(held)
    p0, shift, smooth = pl.pallas_call(
        middle_kernel,
        out_shape=(shape((RAYS, NDEV)), shape((8, NDEV)), shape((COLS, DEP))),
        in_specs=[VMEM] * 2,
        out_specs=(VMEM,) * 3,
        scratch_shapes=[pltpu.VMEM((3, RAYS + 8, NDEV), f32), pltpu.VMEM((3, 7, RAYS + 8, NDEV), f32),
                        pltpu.VMEM((COLS, DEP), f32)] + face_scratch(2) + sems(3, 7) + sems(2, 4),
        compiler_params=comm_params(0),
    )(p_part, q0)
    e, p_part, dots = pl.pallas_call(
        second_kernel,
        out_shape=(shape((COLS, DEP)), shape((RAYS, NDEV)), shape((8, NDEV))),
        in_specs=[VMEM] * 11 + [SMEM],
        out_specs=(VMEM,) * 3,
        scratch_shapes=SCRATCH,
        compiler_params=PARAMS,
    )(p0, shift, q0, smooth, *lists, info, count)
    model, misfit = pl.pallas_call(
        last_kernel,
        out_shape=(shape((COLS, DEP)), shape((1, RAYS))),
        in_specs=[SMEM] + [VMEM] * 7,
        out_specs=(VMEM,) * 2,
        scratch_shapes=[pltpu.VMEM((3, RAYS, NDEV), f32), pltpu.VMEM((3, 7, RAYS, NDEV), f32),
                        pltpu.VMEM((2, 8, NDEV), f32), pltpu.VMEM((2, 15, 8, NDEV), f32), pltpu.VMEM((CLAT, DEP), f32)]
        + face_scratch() + sems(3, 7) + sems(2, 15) + sems(4),
        compiler_params=comm_params(1),
    )(ray_counts, times, p_part, p0, shift, dots, q0, e)
    return (model.reshape(CLON, CLAT, DEP), misfit.reshape(RAYS))


def solution(mesh):
    torus = Mesh(mesh.devices.reshape(4, 2, 4, 4), LON_LAT)
    in_specs = (
        P(LON_LAT),
        P(LON_LAT),
        P(LON_LAT, None),
        P(LON_LAT, None, None),
        P(LON_LAT, None, None),
        P(LON_LAT, None, None),
    )
    out_specs = (P(LON, LAT, None), P(LON_LAT))
    return jax.shard_map(shards, mesh=torus, in_specs=in_specs, out_specs=out_specs, check_vma=False)
```

```python
import itertools

import jax
import jax.numpy as jnp
from jax import lax
from jax.experimental import pallas as pl
from jax.experimental.pallas import tpu as pltpu
from jax.sharding import Mesh
from jax.sharding import PartitionSpec as P

CLON, CLAT, DEP, SEG = 32, 32, 128, 128
COLS = CLON * CLAT
RAYS, TPR = 32, 4
NDEV = 128
SLOTS = 2 * NDEV
CHUNK = 8
BLOCKS, BLOCK = 4, 256
GROUPS, SHARE = 6, 6
TILES, PLACES, ROWS = 8 * SHARE, 8 * SHARE * GROUPS, 16 * GROUPS
SCALE = 8.0
DAMP = 0.01 * SCALE
LON_LAT = ("lon_0", "lon_1", "lat_0", "lat_1")
LON = ("lon_0", "lon_1")
LAT = ("lat_0", "lat_1")

f32, bf16, i32, i16 = jnp.float32, jnp.bfloat16, jnp.int32, jnp.int16
VMEM = pl.BlockSpec(memory_space=pltpu.VMEM)
SMEM = pl.BlockSpec(memory_space=pltpu.SMEM)
PARAMS = pltpu.CompilerParams(vmem_limit_bytes=48 << 20)


MESH = pl.DeviceIdType.MESH
SIZES = (4, 2, 4, 4)


def coords():
    return tuple(lax.axis_index(a) for a in LON_LAT)


def flat(at):
    return ((at[0] * 2 + at[1]) * 4 + at[2]) * 4 + at[3]


def stage_peers(here, group):
    found = []
    for steps in itertools.product(*[range(SIZES[a]) for a in group]):
        if any(steps):
            add = dict(zip(group, steps))
            found.append(tuple((v + add.get(i, 0)) % SIZES[i] for i, v in enumerate(here)))
    return found


def ring_peers(here):
    lon, lat = here[0] * 2 + here[1], here[2] * 4 + here[3]
    found = []
    for step in (1, 7):
        to = (lon + step) % 8
        found.append((to // 2, to % 2, here[2], here[3]))
    for step in (1, 15):
        to = (lat + step) % 16
        found.append((here[0], here[1], to // 4, to % 4))
    return found


def meet(peers):
    barrier = pltpu.get_barrier_semaphore()
    for peer in peers:
        pl.semaphore_signal(barrier, inc=1, device_id=peer, device_id_type=MESH)
    pl.semaphore_wait(barrier, len(peers))


def iota(shape, dim):
    return lax.broadcasted_iota(i32, shape, dim)


def split2(x):
    hi = x.astype(bf16)
    return hi, (x - hi.astype(f32)).astype(bf16)


def split3(x):
    hi = x.astype(bf16)
    rest = x - hi.astype(f32)
    mid = rest.astype(bf16)
    return hi, mid, (rest - mid.astype(f32)).astype(bf16)


def as_payload(cell, lens):
    col = cell >> 7
    parts = [(cell & 127), (col & 127), (col >> 7)]
    return jnp.concatenate([p.astype(f32).astype(bf16) for p in parts] + list(split3(lens)), axis=1)


def from_payload(rows):
    z, low, high, hi, mid, lo = [rows[:, k * 128:(k + 1) * 128] for k in range(6)]
    return z, high * 128.0 + low, (hi + mid) + lo


def prefix(flags):
    upto = jnp.where(iota((128, 128), 0) <= iota((128, 128), 1), 1.0, 0.0).astype(bf16)
    return jnp.dot(jnp.where(flags, 1.0, 0.0).astype(bf16), upto, preferred_element_type=f32).astype(i32)


def take(x, index):
    return jnp.take_along_axis(x, index, axis=1, mode="promise_in_bounds")


def by_block(cell, w):
    counts = [prefix((cell >> 15) == b) for b in range(BLOCKS)]
    starts = [jnp.zeros((128, 1), i32)]
    for b in range(BLOCKS - 1):
        starts.append(starts[-1] + counts[b][:, 127:128])
    lane = iota((128, 128), 1)
    block, rank = jnp.zeros((128, 128), i32), lane
    for b in range(1, BLOCKS):
        block = jnp.where(lane >= starts[b], b, block)
        rank = jnp.where(lane >= starts[b], lane - starts[b], rank)
    at = jnp.zeros((128, 128), i32)
    for step in (64, 32, 16, 8, 4, 2, 1):
        probe = at + (step - 1)
        seen = take(counts[0], probe)
        for b in range(1, BLOCKS):
            seen = jnp.where(block == b, take(counts[b], probe), seen)
        at = jnp.where(seen <= rank, at + step, at)
    marks = jnp.zeros((128, 128), f32)
    for b in range(1, BLOCKS):
        marks = jnp.where((lane == 4 + b) | (lane == 8 + b), starts[b].astype(f32), marks)
    return take(cell, at), take(w, at), marks


def send_kernel(count, brick, times, offs_in, deps_in, lens_in, held, send, pay, offs, deps, lens, load_sem, meet_sem,
                send_sem, recv_sem):
    here = coords()
    loads = [
        pltpu.make_async_copy(src, dst, load_sem.at[k])
        for k, (src, dst) in enumerate(((offs_in, offs), (deps_in, deps), (lens_in, lens)))
    ]
    for load in loads:
        load.start()
    barrier = pltpu.get_barrier_semaphore()
    lines = [p for axis in range(4) for p in stage_peers(here, (axis,))]
    for peer in lines:
        pl.semaphore_signal(barrier, inc=1, device_id=peer, device_id_type=MESH)
    tb = brick[...].astype(f32)
    brick_row = jnp.concatenate([tb[k:k + 1, :] for k in range(TPR)], axis=1)
    time_row = jnp.concatenate([times[...]] * TPR, axis=1)
    ray_row = iota((1, 128), 1) & 31
    live = ray_row < count[0]
    as_rows = jnp.broadcast_to(brick_row, (128, 128))
    same = (as_rows == as_rows.T) & (iota((128, 128), 0) < iota((128, 128), 1))
    rank_row = jnp.sum(jnp.where(same, 1.0, 0.0), axis=0, keepdims=True)
    for load in loads:
        load.wait()
    cell = jnp.concatenate([offs[:, k, :] * DEP + deps[:, k, :] for k in range(TPR)], axis=0)
    w = jnp.concatenate([lens[:, k, :] * SCALE for k in range(TPR)], axis=0)
    cell, w, marks = by_block(cell, w)
    pay[:, 0:768] = as_payload(cell, w)
    pay[:, 768:896] = marks.astype(bf16)
    pl.semaphore_wait(barrier, len(lines))
    for s, axis in enumerate((0, 2, 3)):
        peers = stage_peers(here, (axis,))
        for peer in peers:
            pl.semaphore_signal(meet_sem.at[s], inc=1, device_id=peer, device_id_type=MESH)
        if s < 2:
            place_rank(s, brick_row, rank_row, live, time_row, ray_row, pay, send)
        pl.semaphore_wait(meet_sem.at[s], len(peers))
    me = flat(here)

    def go(step, carry):
        steps = (step // 32, (step // 16) % 2, (step // 4) % 4, step % 4)
        peer = tuple((v + d) % n for v, d, n in zip(here, steps, SIZES))
        pltpu.make_async_remote_copy(
            send.at[flat(peer)], held.at[me], send_sem, recv_sem, device_id=peer, device_id_type=MESH).start()
        return carry

    lax.fori_loop(1, NDEV, go, 0)
    held[me] = send[me]
    rest = pl.ds(0, NDEV - 1)
    every = pltpu.make_async_remote_copy(
        send.at[rest], held.at[rest], send_sem, recv_sem, device_id=here, device_id_type=MESH)
    every.wait_recv()
    every.wait_send()


def place_rank(k, brick_row, rank_row, live, time_row, ray_row, pay, send):
    lanes = iota((128, 128), 1)
    picked = jnp.where((iota((128, 128), 0).astype(f32) == brick_row) & (rank_row == k) & live, 1.0, 0.0)
    rows = jnp.dot(picked.astype(bf16), pay[...], preferred_element_type=f32)
    z, col, w = from_payload(rows)
    send[:, k, :] = col * 128.0 + z
    send[:, 2 + k, :] = w
    value = jnp.sum(picked * time_row, axis=1, keepdims=True)
    ray = jnp.sum(picked * (ray_row + 1).astype(f32), axis=1, keepdims=True)
    marks = rows[:, 768:896]
    if k == 0:
        send[:, 4, :] = jnp.where(lanes == 0, value, jnp.where(lanes == 2, ray, jnp.where(lanes < 8, marks, 0.0)))
    else:
        send[:, 4, :] = jnp.where(lanes == 1, value, jnp.where(lanes == 3, ray, jnp.where(lanes < 8, send[:, 4, :], marks)))


def onehot_cols(col_row):
    at = jnp.broadcast_to(col_row.astype(i16), (BLOCK, 128))
    return jnp.where(lax.broadcasted_iota(i16, (BLOCK, 128), 0) == at, jnp.ones((), bf16), jnp.zeros((), bf16))


def onehot_values(dep_row, val_row):
    at = jnp.broadcast_to(dep_row.astype(i16), (DEP, 128))
    here = lax.broadcasted_iota(i16, (DEP, 128), 0) == at
    return jnp.concatenate(
        [jnp.where(here, jnp.broadcast_to(part, (DEP, 128)), jnp.zeros((), bf16)) for part in split2(val_row)], axis=0)


def scatter_rows(acc, chunks, col, dep, val):
    acc[...] = jnp.zeros_like(acc)

    def body(c, carry):
        rows = [pl.ds(c * CHUNK + j, 1) for j in range(CHUNK)]
        for b in range(BLOCKS):
            left = jnp.concatenate([onehot_cols(col(b, r)) for r in rows], axis=1)
            right = jnp.concatenate([onehot_values(dep(b, r), val(b, r)) for r in rows], axis=1)
            acc[b] += lax.dot_general(left, right, (((1,), (1,)), ((), ())), preferred_element_type=f32)
        return carry

    lax.fori_loop(0, chunks, body, 0)


def gather_rows(gt, chunks, col, dep, w, out):
    out[...] = jnp.zeros_like(out)

    def body(c, carry):
        rows = [pl.ds(c * CHUNK + j, 1) for j in range(CHUNK)]
        for b in range(BLOCKS):
            right = jnp.concatenate([onehot_cols(col(b, r)) for r in rows], axis=1)
            res = jnp.dot(gt[:, b * BLOCK:(b + 1) * BLOCK], right, preferred_element_type=f32)
            for j, r in enumerate(rows):
                at = slice(j * 128, (j + 1) * 128)
                both = res[0:128, at] + res[128:256, at]
                here = jnp.where(iota((DEP, 128), 0) == dep(b, r), both, 0.0)
                out[b, r, :] = jnp.sum(here, axis=0, keepdims=True) * w(b, r)
        return carry

    lax.fori_loop(0, chunks, body, 0)


def bucket(n, starts, cell, w, bcol, bdep, bw, btile):
    groups = (n + TILES - 1) // TILES
    lane = iota((8, 128), 1)

    def body(g, carry):
        most, _ = carry
        rows = [pl.ds(pl.multiple_of(g * TILES + 8 * k, 8), 8) for k in range(SHARE)]
        cells, ws = [cell[r, :] for r in rows], [w[r, :] for r in rows]
        firsts = [[jnp.broadcast_to(starts[r, 4 + b:5 + b], (8, 128)) for b in range(BLOCKS)] for r in rows]
        alive = [iota((8, 128), 0) + (g * TILES + 8 * k) < n for k in range(SHARE)]
        ending = jnp.zeros((8, 128), f32)
        for b in range(BLOCKS):
            before = [jnp.zeros((8, 128), f32)]
            for k in range(SHARE):
                after = firsts[k][b + 1] if b + 1 < BLOCKS else float(SEG)
                before.append(before[-1] + jnp.where(alive[k], after - firsts[k][b], 0.0))
            for h in range(2):
                spot = lane + h * 128
                own_cell, own_w = jnp.zeros((8, 128), i32), jnp.zeros((8, 128), f32)
                tile = jnp.zeros((8, 128), i32)
                for k in range(SHARE):
                    start = before[k].astype(i32)
                    at = (firsts[k][b].astype(i32) - start + spot) & (SEG - 1)
                    mine = spot >= start
                    own_cell = jnp.where(mine, take(cells[k], at), own_cell)
                    own_w = jnp.where(mine, take(ws[k], at), own_w)
                    tile = jnp.where(mine, k, tile)
                own_w = jnp.where(spot < before[SHARE].astype(i32), own_w, 0.0)
                out = pl.ds(pl.multiple_of(g * 16 + h * 8, 8), 8)
                bcol[b, out, :] = (own_cell >> 7) - b * BLOCK
                bdep[b, out, :] = own_cell & 127
                bw[b, out, :] = own_w
                btile[b, out, :] = tile
            ending = jnp.maximum(ending, before[SHARE])
        return jnp.maximum(most, ending), ending

    none = jnp.zeros((8, 128), f32)
    most, ending = lax.fori_loop(0, groups, body, (none, none))
    chunks = 2 * groups - jnp.where(jnp.max(ending) <= 128.0, 1, 0)
    return jnp.max(most).astype(i32), jnp.where(n > 0, chunks, 0)


def per_entry(y_col, tile):
    y = y_col.reshape(GROUPS, SHARE, 8, 1)
    tile = tile.reshape(GROUPS, 2, 8, 128)
    spread = jnp.zeros((GROUPS, 2, 8, 128), f32)
    for k in range(SHARE):
        spread = jnp.where(tile == k, y[:, k:k + 1], spread)
    return spread.reshape(ROWS, 128)


def per_tile(vals, btile):
    sums = [jnp.zeros((GROUPS, 8, 128), f32)] * SHARE
    for b in range(BLOCKS):
        value = vals[b, 0:ROWS, :].reshape(GROUPS, 2, 8, 128)
        tile = btile[b].reshape(GROUPS, 2, 8, 128)
        for k in range(SHARE):
            mine = jnp.where(tile == k, value, 0.0)
            sums[k] = sums[k] + mine[:, 0] + mine[:, 1]
    columns = [jnp.sum(x, axis=2, keepdims=True)[:, None] for x in sums]
    return jnp.concatenate(columns, axis=1).reshape(PLACES, 1)


def both_passes(count, y_col, cell, w, bcol, bdep, bw, btile, finish_q, q_out, acc, gt, wy, vals, part):
    fits = count[1] <= 256

    def whole():
        q = finish_q(jnp.concatenate([acc[b, :, 0:128] + acc[b, :, 128:256] for b in range(BLOCKS)], axis=0))
        q_out[...] = q
        hi, lo = split2(q.T)
        gt[0:128, :] = hi
        gt[128:256, :] = lo

    @pl.when(fits)
    def _():
        for b in range(BLOCKS):
            wy[b, 0:ROWS, :] = bw[b] * per_entry(y_col, btile[b])
        cols, deps = (lambda b, r: bcol[b, r, :]), (lambda b, r: bdep[b, r, :])
        scatter_rows(acc, count[2], cols, deps, lambda b, r: wy[b, r, :])
        whole()
        gather_rows(gt, count[2], cols, deps, lambda b, r: bw[b, r, :], vals)
        part[...] = per_tile(vals, btile)

    @pl.when(jnp.logical_not(fits))
    def _():
        chunks = (count[0] + CHUNK - 1) // CHUNK
        wy[0] = w[...] * y_col
        cols, deps = (lambda b, r: (cell[r, :] >> 7) - b * BLOCK), (lambda b, r: cell[r, :] & 127)
        scatter_rows(acc, chunks, cols, deps, lambda b, r: wy[0, r, :])
        whole()
        gather_rows(gt, chunks, cols, deps, lambda b, r: w[r, :], vals)
        part[...] = jnp.sum((vals[0] + vals[1]) + (vals[2] + vals[3]), axis=1, keepdims=True)


def place_of(slot_info):
    return jnp.where(iota((PLACES, SLOTS), 0) == slot_info, 1.0, 0.0)


def to_rays(partial, place, rays):
    row = jnp.sum(place * partial, axis=0, keepdims=True)
    total = jnp.zeros((RAYS, NDEV), f32)
    for k in range(2):
        at = slice(k * 128, (k + 1) * 128)
        total += jnp.where(iota((RAYS, NDEV), 0) == rays[:, at], row[:, at], 0.0)
    return total


def from_rays(values, place, rays):
    rows = [
        jnp.sum(jnp.where(iota((RAYS, NDEV), 0) == rays[:, k * 128:(k + 1) * 128], values, 0.0), axis=0, keepdims=True)
        for k in range(2)
    ]
    return jnp.sum(place * jnp.concatenate(rows, axis=1), axis=1, keepdims=True)


def total_of(x):
    return jnp.sum(jnp.sum(x, axis=0, keepdims=True), axis=1, keepdims=True)


def as_row(values):
    row = jnp.zeros((8, NDEV), f32)
    for k, value in enumerate(values):
        row = jnp.where(iota((8, NDEV), 1) == k, value, row)
    return row


def first_kernel(held, times, q_out, p_out, times_out, cell, w, bcol, bdep, bw, btile, info, count, acc, gt, wy, vals, part,
                 starts):
    times_out[...] = times[...]
    meta = held[:, 4, :]
    across = meta.T
    y_row = jnp.concatenate([across[0:1, :], across[1:2, :]], axis=1)
    ray_row = jnp.concatenate([across[2:3, :], across[3:4, :]], axis=1).astype(i32) - 1
    live = ray_row >= 0
    flags = jnp.broadcast_to(jnp.where(live, 1.0, 0.0), (8, SLOTS)).astype(bf16)
    before = jnp.where(iota((SLOTS, SLOTS), 0) < iota((SLOTS, SLOTS), 1), 1.0, 0.0).astype(bf16)
    at = jnp.dot(flags, before, preferred_element_type=f32)[0:1, :].astype(i32)
    at = jnp.where(live, at, -1)
    info[0:1, :] = at
    info[1:2, :] = ray_row
    n = jnp.sum(jnp.where(live, 1.0, 0.0)).astype(i32)
    place = place_of(at)
    pay = jnp.concatenate([as_payload(held[:, k, :].astype(i32), held[:, 2 + k, :]) for k in range(2)], axis=0)
    marks = jnp.concatenate([meta, pltpu.roll(meta, 124, 1)], axis=0).astype(bf16)
    rows = jnp.dot(place.astype(bf16), jnp.concatenate([pay, marks], axis=1), preferred_element_type=f32)
    z, c, lens = from_payload(rows)
    cell[...] = (c * 128.0 + z).astype(i32)
    w[...] = lens
    starts[...] = rows[:, 768:896]
    most, chunks = bucket(n, starts, cell, w, bcol, bdep, bw, btile)
    count[0] = n
    count[1] = most
    count[2] = chunks
    y_col = jnp.sum(place * y_row, axis=1, keepdims=True)
    both_passes(count, y_col, cell, w, bcol, bdep, bw, btile, lambda q: q, q_out, acc, gt, wy, vals, part)
    p_out[0:RAYS, :] = to_rays(part[...], place_of(at), ray_row)
    q = q_out[...]
    p_out[RAYS:RAYS + 8, :] = as_row([total_of(q * q)])


def second_kernel(p, shift, q0, smooth, cell, w, bcol, bdep, bw, btile, info, count, e_out, p_out, dots, acc, gt, wy, vals,
                  part):
    place = place_of(info[0:1, :])
    ray_row = info[1:2, :]
    y_col = from_rays(p[...], place, ray_row)
    finish_q = lambda q: q + smooth[...] - shift[0:1, 0:1] * q0[...]
    both_passes(count, y_col, cell, w, bcol, bdep, bw, btile, finish_q, e_out, acc, gt, wy, vals, part)
    p_out[...] = to_rays(part[...], place, ray_row)
    e = e_out[...]
    dots[...] = as_row([total_of(e * q0[...]), total_of(e * e)])


def shape(dims, dtype=f32):
    return jax.ShapeDtypeStruct(dims, dtype)


SCRATCH = [
    pltpu.VMEM((BLOCKS, BLOCK, 256), f32),
    pltpu.VMEM((256, COLS), bf16),
    pltpu.VMEM((BLOCKS, PLACES, SEG), f32),
    pltpu.VMEM((BLOCKS, PLACES, SEG), f32),
    pltpu.VMEM((PLACES, 1), f32),
]


STAGES = ((1, 0), (2,), (3,))
ROUNDS = ((1, 0), (2, 3))


def send_stage(s, here, group, buf, got, send_sem, recv_sem):
    copies = []
    for k, peer in enumerate(stage_peers(here, group)):
        copy = pltpu.make_async_remote_copy(
            buf.at[s], got.at[s, k], send_sem.at[s, k], recv_sem.at[s, k], device_id=peer, device_id_type=MESH)
        copy.start()
        copies.append(copy)
    return copies


def add_stage(s, copies, buf, got):
    total = buf[s]
    for k, copy in enumerate(copies):
        copy.wait_recv()
        total = total + got[s, k]
    return total


def send_halo(here, field, edge, halo, send_sem, recv_sem):
    edge[0] = field[pl.ds(CLAT - 1, CLON, stride=CLAT), :]
    edge[1] = field[pl.ds(0, CLON, stride=CLAT), :]
    faces = (field.at[pl.ds(COLS - CLAT, CLAT)], field.at[pl.ds(0, CLAT)], edge.at[0], edge.at[1])
    copies = []
    for k, (face, peer) in enumerate(zip(faces, ring_peers(here))):
        copy = pltpu.make_async_remote_copy(
            face, halo.at[k], send_sem.at[k], recv_sem.at[k], device_id=peer, device_id_type=MESH)
        copy.start()
        copies.append(copy)
    return copies


def stencil_rows(here, field, halo, put):
    lat = here[2] * 4 + here[3]
    has_before = jnp.where(lat > 0, 1.0, 0.0)
    has_after = jnp.where(lat < 15, 1.0, 0.0)
    row, lane = iota((CLAT, DEP), 0), iota((CLAT, DEP), 1)

    def layer(i, before, after):
        mine = pl.ds(i * CLAT, CLAT)
        f = field[mine, :]
        lat_before = jnp.where(row == 0, halo[2, i:i + 1, :] * has_before, pltpu.roll(f, 1, 0))
        lat_after = jnp.where(row == CLAT - 1, halo[3, i:i + 1, :] * has_after, pltpu.roll(f, CLAT - 1, 0))
        up = jnp.where(lane == 0, 0.0, pltpu.roll(f, 1, 1))
        down = jnp.where(lane == DEP - 1, 0.0, pltpu.roll(f, DEP - 1, 1))
        put(mine, DAMP * (6.0 * f - before - after - lat_before - lat_after - up - down))

    for i in range(CLON):
        before = field[(i - 1) * CLAT:i * CLAT, :] if i else halo[0]
        after = field[(i + 1) * CLAT:(i + 2) * CLAT, :] if i < CLON - 1 else halo[1]
        layer(i, before, after)


def finish(copies):
    for copy in copies:
        copy.wait_send()


def middle_kernel(p_part, q, p_out, shift, smooth, buf, got, g, edge, halo, send_sem, recv_sem, face_send, face_recv):
    here = coords()
    meet([p for group in STAGES for p in stage_peers(here, group)] + ring_peers(here)[2:])
    buf[0] = p_part[...]
    first = send_stage(0, here, STAGES[0], buf, got, send_sem, recv_sem)
    faces = send_halo(here, q, edge.at[0], halo.at[0], face_send.at[0], face_recv.at[0])
    buf[1] = add_stage(0, first, buf, got)
    second = send_stage(1, here, STAGES[1], buf, got, send_sem, recv_sem)
    for copy in faces:
        copy.wait_recv()

    def to_g(rows, value):
        g[rows, :] = value

    stencil_rows(here, q, halo.at[0], to_g)
    more = send_halo(here, g, edge.at[1], halo.at[1], face_send.at[1], face_recv.at[1])
    buf[2] = add_stage(1, second, buf, got)
    third = send_stage(2, here, STAGES[2], buf, got, send_sem, recv_sem)
    for copy in more:
        copy.wait_recv()

    def to_smooth(rows, value):
        smooth[rows, :] = value

    stencil_rows(here, g, halo.at[1], to_smooth)
    total = add_stage(2, third, buf, got)
    p = total[0:RAYS, :]
    p_out[...] = p
    shift[...] = as_row([total_of(p * p) / total[RAYS:RAYS + 1, 0:1], total[RAYS:RAYS + 1, 0:1]])
    finish(first + second + third + faces + more)


def last_kernel(count, times, p_part, p0, shift, dots, q0, e, model, misfit, buf, got, small, small_got, norm, edge, halo,
                send_sem, recv_sem, small_send, small_recv, face_send, face_recv):
    here = coords()
    meet([p for group in ROUNDS for p in stage_peers(here, group)])
    faces = send_halo(here, e, edge, halo, face_send, face_recv)
    buf[0] = p_part[...]
    first = send_stage(0, here, STAGES[0], buf, got, send_sem, recv_sem)
    norm[...] = jnp.zeros_like(norm)
    for copy in faces:
        copy.wait_recv()

    def to_norm(rows, value):
        norm[...] += value * value

    stencil_rows(here, e, halo, to_norm)
    small[0] = jnp.where(iota((8, NDEV), 1) == 2, total_of(norm[...]), dots[...])
    one = send_stage(0, here, ROUNDS[0], small, small_got, small_send, small_recv)
    buf[1] = add_stage(0, first, buf, got)
    second = send_stage(1, here, STAGES[1], buf, got, send_sem, recv_sem)
    small[1] = add_stage(0, one, small, small_got)
    two = send_stage(1, here, ROUNDS[1], small, small_got, small_send, small_recv)
    buf[2] = add_stage(1, second, buf, got)
    third = send_stage(2, here, STAGES[2], buf, got, send_sem, recv_sem)
    moments = add_stage(1, two, small, small_got)
    pe = add_stage(2, third, buf, got)
    mu, m0 = shift[0:1, 0:1], shift[0:1, 1:2]
    s, big = moments[0:1, 0:1] / m0, moments[0:1, 1:2] / m0
    r = (moments[0:1, 2:3] + total_of(pe * pe)) / m0
    cross = big + mu * s
    det = (s + mu) * r - cross * cross
    a, b = (r - s * cross) / det, (s * s - big) / det
    model[...] = (SCALE * a) * q0[...] + (SCALE * b) * e[...]
    fit = jnp.where(iota((RAYS, NDEV), 1) == flat(here), a * p0[...] + b * pe, 0.0)
    column = jnp.sum(fit, axis=1, keepdims=True)
    own = jnp.sum(jnp.where(iota((RAYS, RAYS), 0) == iota((RAYS, RAYS), 1), column, 0.0), axis=0, keepdims=True)
    data = jnp.where(iota((1, RAYS), 1) < count[0], times[...], 0.0)
    misfit[...] = data - own
    finish(faces + first + second + third + one + two)


def comm_params(number, room=16 << 20):
    return pltpu.CompilerParams(vmem_limit_bytes=room, collective_id=number, has_side_effects=True)


def face_scratch(*dims):
    return [pltpu.VMEM(dims + (2, CLON, DEP), f32), pltpu.VMEM(dims + (4, CLON, DEP), f32)]


def sems(*dims):
    return [pltpu.SemaphoreType.DMA(dims), pltpu.SemaphoreType.DMA(dims)]


def shards(travel_times, ray_counts, tile_brick, cell_offsets, cell_depths, seg_lengths):
    times = travel_times.reshape(1, RAYS)
    held = pl.pallas_call(
        send_kernel,
        out_shape=shape((NDEV, 5, SEG)),
        in_specs=[SMEM] + [VMEM] * 2 + [pl.BlockSpec(memory_space=pltpu.MemorySpace.HBM)] * 3,
        out_specs=VMEM,
        scratch_shapes=[pltpu.VMEM((NDEV, 5, SEG), f32), pltpu.VMEM((128, 896), bf16)]
        + [pltpu.VMEM((RAYS, TPR, SEG), d) for d in (i32, i32, f32)]
        + [pltpu.SemaphoreType.DMA((3,)), pltpu.SemaphoreType.REGULAR((3,)), pltpu.SemaphoreType.DMA, pltpu.SemaphoreType.DMA],
        compiler_params=comm_params(2, 60 << 20),
    )(ray_counts, tile_brick.T, times, cell_offsets, cell_depths, seg_lengths)
    entries = [shape((PLACES, SEG), d) for d in (i32, f32)] + [shape((BLOCKS, ROWS, 128), d) for d in (i32, i32, f32, i32)]
    q0, p_part, times, *lists, info, count = pl.pallas_call(
        first_kernel,
        out_shape=(shape((COLS, DEP)), shape((RAYS + 8, NDEV)), shape((1, RAYS)), *entries, shape((2, SLOTS), i32), shape((3,), i32)),
        in_specs=[VMEM] * 2,
        out_specs=(VMEM,) * 10 + (SMEM,),
        scratch_shapes=SCRATCH + [pltpu.VMEM((PLACES, 128), f32)],
        compiler_params=PARAMS,
    )(held, times)
    p0, shift, smooth = pl.pallas_call(
        middle_kernel,
        out_shape=(shape((RAYS, NDEV)), shape((8, NDEV)), shape((COLS, DEP))),
        in_specs=[VMEM] * 2,
        out_specs=(VMEM,) * 3,
        scratch_shapes=[pltpu.VMEM((3, RAYS + 8, NDEV), f32), pltpu.VMEM((3, 7, RAYS + 8, NDEV), f32),
                        pltpu.VMEM((COLS, DEP), f32)] + face_scratch(2) + sems(3, 7) + sems(2, 4),
        compiler_params=comm_params(0),
    )(p_part, q0)
    e, p_part, dots = pl.pallas_call(
        second_kernel,
        out_shape=(shape((COLS, DEP)), shape((RAYS, NDEV)), shape((8, NDEV))),
        in_specs=[VMEM] * 11 + [SMEM],
        out_specs=(VMEM,) * 3,
        scratch_shapes=SCRATCH,
        compiler_params=PARAMS,
    )(p0, shift, q0, smooth, *lists, info, count)
    model, misfit = pl.pallas_call(
        last_kernel,
        out_shape=(shape((COLS, DEP)), shape((1, RAYS))),
        in_specs=[SMEM] + [VMEM] * 7,
        out_specs=(VMEM,) * 2,
        scratch_shapes=[pltpu.VMEM((3, RAYS, NDEV), f32), pltpu.VMEM((3, 7, RAYS, NDEV), f32),
                        pltpu.VMEM((2, 8, NDEV), f32), pltpu.VMEM((2, 15, 8, NDEV), f32), pltpu.VMEM((CLAT, DEP), f32)]
        + face_scratch() + sems(3, 7) + sems(2, 15) + sems(4),
        compiler_params=comm_params(1),
    )(ray_counts, times, p_part, p0, shift, dots, q0, e)
    return (model.reshape(CLON, CLAT, DEP), misfit.reshape(RAYS))


def solution(mesh):
    torus = Mesh(mesh.devices.reshape(4, 2, 4, 4), LON_LAT)
    in_specs = (
        P(LON_LAT),
        P(LON_LAT),
        P(LON_LAT, None),
        P(LON_LAT, None, None),
        P(LON_LAT, None, None),
        P(LON_LAT, None, None),
    )
    out_specs = (P(LON, LAT, None), P(LON_LAT))
    return jax.shard_map(shards, mesh=torus, in_specs=in_specs, out_specs=out_specs, check_vma=False)
```

```python
import itertools

import jax
import jax.numpy as jnp
from jax import lax
from jax.experimental import pallas as pl
from jax.experimental.pallas import tpu as pltpu
from jax.sharding import Mesh
from jax.sharding import PartitionSpec as P

CLON, CLAT, DEP, SEG = 32, 32, 128, 128
COLS = CLON * CLAT
RAYS, TPR = 32, 4
NDEV = 128
SLOTS = 2 * NDEV
CHUNK = 8
BLOCKS, BLOCK = 4, 256
GROUPS, SHARE = 6, 6
TILES, PLACES, ROWS = 8 * SHARE, 8 * SHARE * GROUPS, 16 * GROUPS
SCALE = 8.0
DAMP = 0.01 * SCALE
LON_LAT = ("lon_0", "lon_1", "lat_0", "lat_1")
LON = ("lon_0", "lon_1")
LAT = ("lat_0", "lat_1")

f32, bf16, i32, i16 = jnp.float32, jnp.bfloat16, jnp.int32, jnp.int16
VMEM = pl.BlockSpec(memory_space=pltpu.VMEM)
SMEM = pl.BlockSpec(memory_space=pltpu.SMEM)
PARAMS = pltpu.CompilerParams(vmem_limit_bytes=48 << 20)


MESH = pl.DeviceIdType.MESH
SIZES = (4, 2, 4, 4)


def coords():
    return tuple(lax.axis_index(a) for a in LON_LAT)


def flat(at):
    return ((at[0] * 2 + at[1]) * 4 + at[2]) * 4 + at[3]


def stage_peers(here, group):
    found = []
    for steps in itertools.product(*[range(SIZES[a]) for a in group]):
        if any(steps):
            add = dict(zip(group, steps))
            found.append(tuple((v + add.get(i, 0)) % SIZES[i] for i, v in enumerate(here)))
    return found


def ring_peers(here):
    lon, lat = here[0] * 2 + here[1], here[2] * 4 + here[3]
    found = []
    for step in (1, 7):
        to = (lon + step) % 8
        found.append((to // 2, to % 2, here[2], here[3]))
    for step in (1, 15):
        to = (lat + step) % 16
        found.append((here[0], here[1], to // 4, to % 4))
    return found


def meet(peers):
    barrier = pltpu.get_barrier_semaphore()
    for peer in peers:
        pl.semaphore_signal(barrier, inc=1, device_id=peer, device_id_type=MESH)
    pl.semaphore_wait(barrier, len(peers))


def iota(shape, dim):
    return lax.broadcasted_iota(i32, shape, dim)


def split2(x):
    hi = x.astype(bf16)
    return hi, (x - hi.astype(f32)).astype(bf16)


def split3(x):
    hi = x.astype(bf16)
    rest = x - hi.astype(f32)
    mid = rest.astype(bf16)
    return hi, mid, (rest - mid.astype(f32)).astype(bf16)


def as_payload(cell, lens):
    col = cell >> 7
    parts = [(cell & 127), (col & 127), (col >> 7)]
    return jnp.concatenate([p.astype(f32).astype(bf16) for p in parts] + list(split3(lens)), axis=1)


def from_payload(rows):
    z, low, high, hi, mid, lo = [rows[:, k * 128:(k + 1) * 128] for k in range(6)]
    return z, high * 128.0 + low, (hi + mid) + lo


def prefix(flags):
    upto = jnp.where(iota((128, 128), 0) <= iota((128, 128), 1), 1.0, 0.0).astype(bf16)
    return jnp.dot(jnp.where(flags, 1.0, 0.0).astype(bf16), upto, preferred_element_type=f32).astype(i32)


def take(x, index):
    return jnp.take_along_axis(x, index, axis=1, mode="promise_in_bounds")


def by_block(cell, w):
    counts = [prefix((cell >> 15) == b) for b in range(BLOCKS)]
    starts = [jnp.zeros((128, 1), i32)]
    for b in range(BLOCKS - 1):
        starts.append(starts[-1] + counts[b][:, 127:128])
    lane = iota((128, 128), 1)
    block, rank = jnp.zeros((128, 128), i32), lane
    for b in range(1, BLOCKS):
        block = jnp.where(lane >= starts[b], b, block)
        rank = jnp.where(lane >= starts[b], lane - starts[b], rank)
    at = jnp.zeros((128, 128), i32)
    for step in (64, 32, 16, 8, 4, 2, 1):
        probe = at + (step - 1)
        seen = take(counts[0], probe)
        for b in range(1, BLOCKS):
            seen = jnp.where(block == b, take(counts[b], probe), seen)
        at = jnp.where(seen <= rank, at + step, at)
    marks = jnp.zeros((128, 128), f32)
    for b in range(1, BLOCKS):
        marks = jnp.where((lane == 4 + b) | (lane == 8 + b), starts[b].astype(f32), marks)
    return take(cell, at), take(w, at), marks


def send_kernel(count, brick, times, offs_in, deps_in, lens_in, held, send, pay, offs, deps, lens, load_sem, meet_sem,
                send_sem, recv_sem):
    here = coords()
    loads = [
        pltpu.make_async_copy(src, dst, load_sem.at[k])
        for k, (src, dst) in enumerate(((offs_in, offs), (deps_in, deps), (lens_in, lens)))
    ]
    for load in loads:
        load.start()
    barrier = pltpu.get_barrier_semaphore()
    lines = [p for group in ((1, 0), (2,), (3,)) for p in stage_peers(here, group)]
    for peer in lines:
        pl.semaphore_signal(barrier, inc=1, device_id=peer, device_id_type=MESH)
    tb = brick[...].astype(f32)
    brick_row = jnp.concatenate([tb[k:k + 1, :] for k in range(TPR)], axis=1)
    time_row = jnp.concatenate([times[...]] * TPR, axis=1)
    ray_row = iota((1, 128), 1) & 31
    live = ray_row < count[0]
    as_rows = jnp.broadcast_to(brick_row, (128, 128))
    same = (as_rows == as_rows.T) & (iota((128, 128), 0) < iota((128, 128), 1))
    rank_row = jnp.sum(jnp.where(same, 1.0, 0.0), axis=0, keepdims=True)
    for load in loads:
        load.wait()
    cell = jnp.concatenate([offs[:, k, :] * DEP + deps[:, k, :] for k in range(TPR)], axis=0)
    w = jnp.concatenate([lens[:, k, :] * SCALE for k in range(TPR)], axis=0)
    cell, w, marks = by_block(cell, w)
    pay[:, 0:768] = as_payload(cell, w)
    pay[:, 768:896] = marks.astype(bf16)
    pl.semaphore_wait(barrier, len(lines))
    for s, axis in enumerate((2, 3)):
        peers = stage_peers(here, (axis,))
        for peer in peers:
            pl.semaphore_signal(meet_sem.at[s], inc=1, device_id=peer, device_id_type=MESH)
        place_rank(s, brick_row, rank_row, live, time_row, ray_row, pay, send)
        pl.semaphore_wait(meet_sem.at[s], len(peers))
    me = flat(here)

    def go(step, carry):
        steps = (step // 32, (step // 16) % 2, (step // 4) % 4, step % 4)
        peer = tuple((v + d) % n for v, d, n in zip(here, steps, SIZES))
        pltpu.make_async_remote_copy(
            send.at[flat(peer)], held.at[me], send_sem, recv_sem, device_id=peer, device_id_type=MESH).start()
        return carry

    lax.fori_loop(1, NDEV, go, 0)
    held[me] = send[me]
    rest = pl.ds(0, NDEV - 1)
    every = pltpu.make_async_remote_copy(
        send.at[rest], held.at[rest], send_sem, recv_sem, device_id=here, device_id_type=MESH)
    every.wait_recv()
    every.wait_send()


def place_rank(k, brick_row, rank_row, live, time_row, ray_row, pay, send):
    lanes = iota((128, 128), 1)
    picked = jnp.where((iota((128, 128), 0).astype(f32) == brick_row) & (rank_row == k) & live, 1.0, 0.0)
    rows = jnp.dot(picked.astype(bf16), pay[...], preferred_element_type=f32)
    z, col, w = from_payload(rows)
    send[:, k, :] = col * 128.0 + z
    send[:, 2 + k, :] = w
    value = jnp.sum(picked * time_row, axis=1, keepdims=True)
    ray = jnp.sum(picked * (ray_row + 1).astype(f32), axis=1, keepdims=True)
    marks = rows[:, 768:896]
    if k == 0:
        send[:, 4, :] = jnp.where(lanes == 0, value, jnp.where(lanes == 2, ray, jnp.where(lanes < 8, marks, 0.0)))
    else:
        send[:, 4, :] = jnp.where(lanes == 1, value, jnp.where(lanes == 3, ray, jnp.where(lanes < 8, send[:, 4, :], marks)))


def onehot_cols(col_row):
    at = jnp.broadcast_to(col_row.astype(i16), (BLOCK, 128))
    return jnp.where(lax.broadcasted_iota(i16, (BLOCK, 128), 0) == at, jnp.ones((), bf16), jnp.zeros((), bf16))


def onehot_values(dep_row, val_row):
    at = jnp.broadcast_to(dep_row.astype(i16), (DEP, 128))
    here = lax.broadcasted_iota(i16, (DEP, 128), 0) == at
    return jnp.concatenate(
        [jnp.where(here, jnp.broadcast_to(part, (DEP, 128)), jnp.zeros((), bf16)) for part in split2(val_row)], axis=0)


def scatter_rows(acc, chunks, col, dep, val):
    acc[...] = jnp.zeros_like(acc)

    def body(c, carry):
        rows = [pl.ds(c * CHUNK + j, 1) for j in range(CHUNK)]
        for b in range(BLOCKS):
            left = jnp.concatenate([onehot_cols(col(b, r)) for r in rows], axis=1)
            right = jnp.concatenate([onehot_values(dep(b, r), val(b, r)) for r in rows], axis=1)
            acc[b] += lax.dot_general(left, right, (((1,), (1,)), ((), ())), preferred_element_type=f32)
        return carry

    lax.fori_loop(0, chunks, body, 0)


def gather_rows(gt, chunks, col, dep, w, out):
    out[...] = jnp.zeros_like(out)

    def body(c, carry):
        rows = [pl.ds(c * CHUNK + j, 1) for j in range(CHUNK)]
        for b in range(BLOCKS):
            right = jnp.concatenate([onehot_cols(col(b, r)) for r in rows], axis=1)
            res = jnp.dot(gt[:, b * BLOCK:(b + 1) * BLOCK], right, preferred_element_type=f32)
            for j, r in enumerate(rows):
                at = slice(j * 128, (j + 1) * 128)
                both = res[0:128, at] + res[128:256, at]
                here = jnp.where(iota((DEP, 128), 0) == dep(b, r), both, 0.0)
                out[b, r, :] = jnp.sum(here, axis=0, keepdims=True) * w(b, r)
        return carry

    lax.fori_loop(0, chunks, body, 0)


def bucket(n, starts, cell, w, bcol, bdep, bw, btile):
    groups = (n + TILES - 1) // TILES
    lane = iota((8, 128), 1)

    def body(g, carry):
        most, _ = carry
        rows = [pl.ds(pl.multiple_of(g * TILES + 8 * k, 8), 8) for k in range(SHARE)]
        cells, ws = [cell[r, :] for r in rows], [w[r, :] for r in rows]
        firsts = [[jnp.broadcast_to(starts[r, 4 + b:5 + b], (8, 128)) for b in range(BLOCKS)] for r in rows]
        alive = [iota((8, 128), 0) + (g * TILES + 8 * k) < n for k in range(SHARE)]
        ending = jnp.zeros((8, 128), f32)
        for b in range(BLOCKS):
            before = [jnp.zeros((8, 128), f32)]
            for k in range(SHARE):
                after = firsts[k][b + 1] if b + 1 < BLOCKS else float(SEG)
                before.append(before[-1] + jnp.where(alive[k], after - firsts[k][b], 0.0))
            for h in range(2):
                spot = lane + h * 128
                own_cell, own_w = jnp.zeros((8, 128), i32), jnp.zeros((8, 128), f32)
                tile = jnp.zeros((8, 128), i32)
                for k in range(SHARE):
                    start = before[k].astype(i32)
                    at = (firsts[k][b].astype(i32) - start + spot) & (SEG - 1)
                    mine = spot >= start
                    own_cell = jnp.where(mine, take(cells[k], at), own_cell)
                    own_w = jnp.where(mine, take(ws[k], at), own_w)
                    tile = jnp.where(mine, k, tile)
                own_w = jnp.where(spot < before[SHARE].astype(i32), own_w, 0.0)
                out = pl.ds(pl.multiple_of(g * 16 + h * 8, 8), 8)
                bcol[b, out, :] = (own_cell >> 7) - b * BLOCK
                bdep[b, out, :] = own_cell & 127
                bw[b, out, :] = own_w
                btile[b, out, :] = tile
            ending = jnp.maximum(ending, before[SHARE])
        return jnp.maximum(most, ending), ending

    none = jnp.zeros((8, 128), f32)
    most, ending = lax.fori_loop(0, groups, body, (none, none))
    chunks = 2 * groups - jnp.where(jnp.max(ending) <= 128.0, 1, 0)
    return jnp.max(most).astype(i32), jnp.where(n > 0, chunks, 0)


def per_entry(y_col, tile):
    y = y_col.reshape(GROUPS, SHARE, 8, 1)
    tile = tile.reshape(GROUPS, 2, 8, 128)
    spread = jnp.zeros((GROUPS, 2, 8, 128), f32)
    for k in range(SHARE):
        spread = jnp.where(tile == k, y[:, k:k + 1], spread)
    return spread.reshape(ROWS, 128)


def per_tile(vals, btile):
    sums = [jnp.zeros((GROUPS, 8, 128), f32)] * SHARE
    for b in range(BLOCKS):
        value = vals[b, 0:ROWS, :].reshape(GROUPS, 2, 8, 128)
        tile = btile[b].reshape(GROUPS, 2, 8, 128)
        for k in range(SHARE):
            mine = jnp.where(tile == k, value, 0.0)
            sums[k] = sums[k] + mine[:, 0] + mine[:, 1]
    columns = [jnp.sum(x, axis=2, keepdims=True)[:, None] for x in sums]
    return jnp.concatenate(columns, axis=1).reshape(PLACES, 1)


def both_passes(count, y_col, cell, w, bcol, bdep, bw, btile, finish_q, q_out, acc, gt, wy, vals, part):
    fits = count[1] <= 256

    def whole():
        q = finish_q(jnp.concatenate([acc[b, :, 0:128] + acc[b, :, 128:256] for b in range(BLOCKS)], axis=0))
        q_out[...] = q
        hi, lo = split2(q.T)
        gt[0:128, :] = hi
        gt[128:256, :] = lo

    @pl.when(fits)
    def _():
        for b in range(BLOCKS):
            wy[b, 0:ROWS, :] = bw[b] * per_entry(y_col, btile[b])
        cols, deps = (lambda b, r: bcol[b, r, :]), (lambda b, r: bdep[b, r, :])
        scatter_rows(acc, count[2], cols, deps, lambda b, r: wy[b, r, :])
        whole()
        gather_rows(gt, count[2], cols, deps, lambda b, r: bw[b, r, :], vals)
        part[...] = per_tile(vals, btile)

    @pl.when(jnp.logical_not(fits))
    def _():
        chunks = (count[0] + CHUNK - 1) // CHUNK
        wy[0] = w[...] * y_col
        cols, deps = (lambda b, r: (cell[r, :] >> 7) - b * BLOCK), (lambda b, r: cell[r, :] & 127)
        scatter_rows(acc, chunks, cols, deps, lambda b, r: wy[0, r, :])
        whole()
        gather_rows(gt, chunks, cols, deps, lambda b, r: w[r, :], vals)
        part[...] = jnp.sum((vals[0] + vals[1]) + (vals[2] + vals[3]), axis=1, keepdims=True)


def place_of(slot_info):
    return jnp.where(iota((PLACES, SLOTS), 0) == slot_info, 1.0, 0.0)


def to_rays(partial, place, rays):
    row = jnp.sum(place * partial, axis=0, keepdims=True)
    total = jnp.zeros((RAYS, NDEV), f32)
    for k in range(2):
        at = slice(k * 128, (k + 1) * 128)
        total += jnp.where(iota((RAYS, NDEV), 0) == rays[:, at], row[:, at], 0.0)
    return total


def from_rays(values, place, rays):
    rows = [
        jnp.sum(jnp.where(iota((RAYS, NDEV), 0) == rays[:, k * 128:(k + 1) * 128], values, 0.0), axis=0, keepdims=True)
        for k in range(2)
    ]
    return jnp.sum(place * jnp.concatenate(rows, axis=1), axis=1, keepdims=True)


def total_of(x):
    return jnp.sum(jnp.sum(x, axis=0, keepdims=True), axis=1, keepdims=True)


def as_row(values):
    row = jnp.zeros((8, NDEV), f32)
    for k, value in enumerate(values):
        row = jnp.where(iota((8, NDEV), 1) == k, value, row)
    return row


def first_kernel(held, times, q_out, p_out, times_out, cell, w, bcol, bdep, bw, btile, info, count, acc, gt, wy, vals, part,
                 starts):
    times_out[...] = times[...]
    meta = held[:, 4, :]
    across = meta.T
    y_row = jnp.concatenate([across[0:1, :], across[1:2, :]], axis=1)
    ray_row = jnp.concatenate([across[2:3, :], across[3:4, :]], axis=1).astype(i32) - 1
    live = ray_row >= 0
    flags = jnp.broadcast_to(jnp.where(live, 1.0, 0.0), (8, SLOTS)).astype(bf16)
    before = jnp.where(iota((SLOTS, SLOTS), 0) < iota((SLOTS, SLOTS), 1), 1.0, 0.0).astype(bf16)
    at = jnp.dot(flags, before, preferred_element_type=f32)[0:1, :].astype(i32)
    at = jnp.where(live, at, -1)
    info[0:1, :] = at
    info[1:2, :] = ray_row
    n = jnp.sum(jnp.where(live, 1.0, 0.0)).astype(i32)
    place = place_of(at)
    pay = jnp.concatenate([as_payload(held[:, k, :].astype(i32), held[:, 2 + k, :]) for k in range(2)], axis=0)
    marks = jnp.concatenate([meta, pltpu.roll(meta, 124, 1)], axis=0).astype(bf16)
    rows = jnp.dot(place.astype(bf16), jnp.concatenate([pay, marks], axis=1), preferred_element_type=f32)
    z, c, lens = from_payload(rows)
    cell[...] = (c * 128.0 + z).astype(i32)
    w[...] = lens
    starts[...] = rows[:, 768:896]
    most, chunks = bucket(n, starts, cell, w, bcol, bdep, bw, btile)
    count[0] = n
    count[1] = most
    count[2] = chunks
    y_col = jnp.sum(place * y_row, axis=1, keepdims=True)
    both_passes(count, y_col, cell, w, bcol, bdep, bw, btile, lambda q: q, q_out, acc, gt, wy, vals, part)
    p_out[0:RAYS, :] = to_rays(part[...], place_of(at), ray_row)
    q = q_out[...]
    p_out[RAYS:RAYS + 8, :] = as_row([total_of(q * q)])


def second_kernel(p, shift, q0, smooth, cell, w, bcol, bdep, bw, btile, info, count, e_out, p_out, dots, acc, gt, wy, vals,
                  part):
    place = place_of(info[0:1, :])
    ray_row = info[1:2, :]
    y_col = from_rays(p[...], place, ray_row)
    finish_q = lambda q: q + smooth[...] - shift[0:1, 0:1] * q0[...]
    both_passes(count, y_col, cell, w, bcol, bdep, bw, btile, finish_q, e_out, acc, gt, wy, vals, part)
    p_out[...] = to_rays(part[...], place, ray_row)
    e = e_out[...]
    dots[...] = as_row([total_of(e * q0[...]), total_of(e * e)])


def shape(dims, dtype=f32):
    return jax.ShapeDtypeStruct(dims, dtype)


SCRATCH = [
    pltpu.VMEM((BLOCKS, BLOCK, 256), f32),
    pltpu.VMEM((256, COLS), bf16),
    pltpu.VMEM((BLOCKS, PLACES, SEG), f32),
    pltpu.VMEM((BLOCKS, PLACES, SEG), f32),
    pltpu.VMEM((PLACES, 1), f32),
]


STAGES = ((1, 0), (2,), (3,))
ROUNDS = ((1, 0), (2, 3))


def send_stage(s, here, group, buf, got, send_sem, recv_sem):
    copies = []
    for k, peer in enumerate(stage_peers(here, group)):
        copy = pltpu.make_async_remote_copy(
            buf.at[s], got.at[s, k], send_sem.at[s, k], recv_sem.at[s, k], device_id=peer, device_id_type=MESH)
        copy.start()
        copies.append(copy)
    return copies


def add_stage(s, copies, buf, got):
    total = buf[s]
    for k, copy in enumerate(copies):
        copy.wait_recv()
        total = total + got[s, k]
    return total


def send_halo(here, field, edge, halo, send_sem, recv_sem):
    edge[0] = field[pl.ds(CLAT - 1, CLON, stride=CLAT), :]
    edge[1] = field[pl.ds(0, CLON, stride=CLAT), :]
    faces = (field.at[pl.ds(COLS - CLAT, CLAT)], field.at[pl.ds(0, CLAT)], edge.at[0], edge.at[1])
    copies = []
    for k, (face, peer) in enumerate(zip(faces, ring_peers(here))):
        copy = pltpu.make_async_remote_copy(
            face, halo.at[k], send_sem.at[k], recv_sem.at[k], device_id=peer, device_id_type=MESH)
        copy.start()
        copies.append(copy)
    return copies


def stencil_rows(here, field, halo, put):
    lat = here[2] * 4 + here[3]
    has_before = jnp.where(lat > 0, 1.0, 0.0)
    has_after = jnp.where(lat < 15, 1.0, 0.0)
    row, lane = iota((CLAT, DEP), 0), iota((CLAT, DEP), 1)

    def layer(i, before, after):
        mine = pl.ds(i * CLAT, CLAT)
        f = field[mine, :]
        lat_before = jnp.where(row == 0, halo[2, i:i + 1, :] * has_before, pltpu.roll(f, 1, 0))
        lat_after = jnp.where(row == CLAT - 1, halo[3, i:i + 1, :] * has_after, pltpu.roll(f, CLAT - 1, 0))
        up = jnp.where(lane == 0, 0.0, pltpu.roll(f, 1, 1))
        down = jnp.where(lane == DEP - 1, 0.0, pltpu.roll(f, DEP - 1, 1))
        put(mine, DAMP * (6.0 * f - before - after - lat_before - lat_after - up - down))

    for i in range(CLON):
        before = field[(i - 1) * CLAT:i * CLAT, :] if i else halo[0]
        after = field[(i + 1) * CLAT:(i + 2) * CLAT, :] if i < CLON - 1 else halo[1]
        layer(i, before, after)


def finish(copies):
    for copy in copies:
        copy.wait_send()


def middle_kernel(p_part, q, p_out, shift, smooth, buf, got, g, edge, halo, send_sem, recv_sem, face_send, face_recv):
    here = coords()
    meet([p for group in STAGES for p in stage_peers(here, group)] + ring_peers(here)[2:])
    buf[0] = p_part[...]
    first = send_stage(0, here, STAGES[0], buf, got, send_sem, recv_sem)
    faces = send_halo(here, q, edge.at[0], halo.at[0], face_send.at[0], face_recv.at[0])
    buf[1] = add_stage(0, first, buf, got)
    second = send_stage(1, here, STAGES[1], buf, got, send_sem, recv_sem)
    for copy in faces:
        copy.wait_recv()

    def to_g(rows, value):
        g[rows, :] = value

    stencil_rows(here, q, halo.at[0], to_g)
    more = send_halo(here, g, edge.at[1], halo.at[1], face_send.at[1], face_recv.at[1])
    buf[2] = add_stage(1, second, buf, got)
    third = send_stage(2, here, STAGES[2], buf, got, send_sem, recv_sem)
    for copy in more:
        copy.wait_recv()

    def to_smooth(rows, value):
        smooth[rows, :] = value

    stencil_rows(here, g, halo.at[1], to_smooth)
    total = add_stage(2, third, buf, got)
    p = total[0:RAYS, :]
    p_out[...] = p
    shift[...] = as_row([total_of(p * p) / total[RAYS:RAYS + 1, 0:1], total[RAYS:RAYS + 1, 0:1]])
    finish(first + second + third + faces + more)


def last_kernel(count, times, p_part, p0, shift, dots, q0, e, model, misfit, buf, got, small, small_got, norm, edge, halo,
                send_sem, recv_sem, small_send, small_recv, face_send, face_recv):
    here = coords()
    meet([p for group in ROUNDS for p in stage_peers(here, group)])
    faces = send_halo(here, e, edge, halo, face_send, face_recv)
    buf[0] = p_part[...]
    first = send_stage(0, here, STAGES[0], buf, got, send_sem, recv_sem)
    norm[...] = jnp.zeros_like(norm)
    for copy in faces:
        copy.wait_recv()

    def to_norm(rows, value):
        norm[...] += value * value

    stencil_rows(here, e, halo, to_norm)
    small[0] = jnp.where(iota((8, NDEV), 1) == 2, total_of(norm[...]), dots[...])
    one = send_stage(0, here, ROUNDS[0], small, small_got, small_send, small_recv)
    buf[1] = add_stage(0, first, buf, got)
    second = send_stage(1, here, STAGES[1], buf, got, send_sem, recv_sem)
    small[1] = add_stage(0, one, small, small_got)
    two = send_stage(1, here, ROUNDS[1], small, small_got, small_send, small_recv)
    buf[2] = add_stage(1, second, buf, got)
    third = send_stage(2, here, STAGES[2], buf, got, send_sem, recv_sem)
    moments = add_stage(1, two, small, small_got)
    pe = add_stage(2, third, buf, got)
    mu, m0 = shift[0:1, 0:1], shift[0:1, 1:2]
    s, big = moments[0:1, 0:1] / m0, moments[0:1, 1:2] / m0
    r = (moments[0:1, 2:3] + total_of(pe * pe)) / m0
    cross = big + mu * s
    det = (s + mu) * r - cross * cross
    a, b = (r - s * cross) / det, (s * s - big) / det
    model[...] = (SCALE * a) * q0[...] + (SCALE * b) * e[...]
    fit = jnp.where(iota((RAYS, NDEV), 1) == flat(here), a * p0[...] + b * pe, 0.0)
    column = jnp.sum(fit, axis=1, keepdims=True)
    own = jnp.sum(jnp.where(iota((RAYS, RAYS), 0) == iota((RAYS, RAYS), 1), column, 0.0), axis=0, keepdims=True)
    data = jnp.where(iota((1, RAYS), 1) < count[0], times[...], 0.0)
    misfit[...] = data - own
    finish(faces + first + second + third + one + two)


def comm_params(number, room=16 << 20):
    return pltpu.CompilerParams(vmem_limit_bytes=room, collective_id=number, has_side_effects=True)


def face_scratch(*dims):
    return [pltpu.VMEM(dims + (2, CLON, DEP), f32), pltpu.VMEM(dims + (4, CLON, DEP), f32)]


def sems(*dims):
    return [pltpu.SemaphoreType.DMA(dims), pltpu.SemaphoreType.DMA(dims)]


def shards(travel_times, ray_counts, tile_brick, cell_offsets, cell_depths, seg_lengths):
    times = travel_times.reshape(1, RAYS)
    held = pl.pallas_call(
        send_kernel,
        out_shape=shape((NDEV, 5, SEG)),
        in_specs=[SMEM] + [VMEM] * 2 + [pl.BlockSpec(memory_space=pltpu.MemorySpace.HBM)] * 3,
        out_specs=VMEM,
        scratch_shapes=[pltpu.VMEM((NDEV, 5, SEG), f32), pltpu.VMEM((128, 896), bf16)]
        + [pltpu.VMEM((RAYS, TPR, SEG), d) for d in (i32, i32, f32)]
        + [pltpu.SemaphoreType.DMA((3,)), pltpu.SemaphoreType.REGULAR((2,)), pltpu.SemaphoreType.DMA, pltpu.SemaphoreType.DMA],
        compiler_params=comm_params(2, 60 << 20),
    )(ray_counts, tile_brick.T, times, cell_offsets, cell_depths, seg_lengths)
    entries = [shape((PLACES, SEG), d) for d in (i32, f32)] + [shape((BLOCKS, ROWS, 128), d) for d in (i32, i32, f32, i32)]
    q0, p_part, times, *lists, info, count = pl.pallas_call(
        first_kernel,
        out_shape=(shape((COLS, DEP)), shape((RAYS + 8, NDEV)), shape((1, RAYS)), *entries, shape((2, SLOTS), i32), shape((3,), i32)),
        in_specs=[VMEM] * 2,
        out_specs=(VMEM,) * 10 + (SMEM,),
        scratch_shapes=SCRATCH + [pltpu.VMEM((PLACES, 128), f32)],
        compiler_params=PARAMS,
    )(held, times)
    p0, shift, smooth = pl.pallas_call(
        middle_kernel,
        out_shape=(shape((RAYS, NDEV)), shape((8, NDEV)), shape((COLS, DEP))),
        in_specs=[VMEM] * 2,
        out_specs=(VMEM,) * 3,
        scratch_shapes=[pltpu.VMEM((3, RAYS + 8, NDEV), f32), pltpu.VMEM((3, 7, RAYS + 8, NDEV), f32),
                        pltpu.VMEM((COLS, DEP), f32)] + face_scratch(2) + sems(3, 7) + sems(2, 4),
        compiler_params=comm_params(0),
    )(p_part, q0)
    e, p_part, dots = pl.pallas_call(
        second_kernel,
        out_shape=(shape((COLS, DEP)), shape((RAYS, NDEV)), shape((8, NDEV))),
        in_specs=[VMEM] * 11 + [SMEM],
        out_specs=(VMEM,) * 3,
        scratch_shapes=SCRATCH,
        compiler_params=PARAMS,
    )(p0, shift, q0, smooth, *lists, info, count)
    model, misfit = pl.pallas_call(
        last_kernel,
        out_shape=(shape((COLS, DEP)), shape((1, RAYS))),
        in_specs=[SMEM] + [VMEM] * 7,
        out_specs=(VMEM,) * 2,
        scratch_shapes=[pltpu.VMEM((3, RAYS, NDEV), f32), pltpu.VMEM((3, 7, RAYS, NDEV), f32),
                        pltpu.VMEM((2, 8, NDEV), f32), pltpu.VMEM((2, 15, 8, NDEV), f32), pltpu.VMEM((CLAT, DEP), f32)]
        + face_scratch() + sems(3, 7) + sems(2, 15) + sems(4),
        compiler_params=comm_params(1),
    )(ray_counts, times, p_part, p0, shift, dots, q0, e)
    return (model.reshape(CLON, CLAT, DEP), misfit.reshape(RAYS))


def solution(mesh):
    torus = Mesh(mesh.devices.reshape(4, 2, 4, 4), LON_LAT)
    in_specs = (
        P(LON_LAT),
        P(LON_LAT),
        P(LON_LAT, None),
        P(LON_LAT, None, None),
        P(LON_LAT, None, None),
        P(LON_LAT, None, None),
    )
    out_specs = (P(LON, LAT, None), P(LON_LAT))
    return jax.shard_map(shards, mesh=torus, in_specs=in_specs, out_specs=out_specs, check_vma=False)
```

```python
import itertools

import jax
import jax.numpy as jnp
from jax import lax
from jax.experimental import pallas as pl
from jax.experimental.pallas import tpu as pltpu
from jax.sharding import Mesh
from jax.sharding import PartitionSpec as P

CLON, CLAT, DEP, SEG = 32, 32, 128, 128
COLS = CLON * CLAT
RAYS, TPR = 32, 4
NDEV = 128
SLOTS = 2 * NDEV
CHUNK = 8
BLOCKS, BLOCK = 4, 256
GROUPS, SHARE = 6, 6
TILES, PLACES, ROWS = 8 * SHARE, 8 * SHARE * GROUPS, 16 * GROUPS
SCALE = 8.0
DAMP = 0.01 * SCALE
LON_LAT = ("lon_0", "lon_1", "lat_0", "lat_1")
LON = ("lon_0", "lon_1")
LAT = ("lat_0", "lat_1")

f32, bf16, i32, i16 = jnp.float32, jnp.bfloat16, jnp.int32, jnp.int16
VMEM = pl.BlockSpec(memory_space=pltpu.VMEM)
SMEM = pl.BlockSpec(memory_space=pltpu.SMEM)
PARAMS = pltpu.CompilerParams(vmem_limit_bytes=48 << 20)


MESH = pl.DeviceIdType.MESH
SIZES = (4, 2, 4, 4)


def coords():
    return tuple(lax.axis_index(a) for a in LON_LAT)


def flat(at):
    return ((at[0] * 2 + at[1]) * 4 + at[2]) * 4 + at[3]


def stage_peers(here, group):
    found = []
    for steps in itertools.product(*[range(SIZES[a]) for a in group]):
        if any(steps):
            add = dict(zip(group, steps))
            found.append(tuple((v + add.get(i, 0)) % SIZES[i] for i, v in enumerate(here)))
    return found


def ring_peers(here):
    lon, lat = here[0] * 2 + here[1], here[2] * 4 + here[3]
    found = []
    for step in (1, 7):
        to = (lon + step) % 8
        found.append((to // 2, to % 2, here[2], here[3]))
    for step in (1, 15):
        to = (lat + step) % 16
        found.append((here[0], here[1], to // 4, to % 4))
    return found


def meet(peers):
    barrier = pltpu.get_barrier_semaphore()
    for peer in peers:
        pl.semaphore_signal(barrier, inc=1, device_id=peer, device_id_type=MESH)
    pl.semaphore_wait(barrier, len(peers))


def iota(shape, dim):
    return lax.broadcasted_iota(i32, shape, dim)


def split2(x):
    hi = x.astype(bf16)
    return hi, (x - hi.astype(f32)).astype(bf16)


def split3(x):
    hi = x.astype(bf16)
    rest = x - hi.astype(f32)
    mid = rest.astype(bf16)
    return hi, mid, (rest - mid.astype(f32)).astype(bf16)


def as_payload(cell, lens):
    col = cell >> 7
    parts = [(cell & 127), (col & 127), (col >> 7)]
    return jnp.concatenate([p.astype(f32).astype(bf16) for p in parts] + list(split3(lens)), axis=1)


def from_payload(rows):
    z, low, high, hi, mid, lo = [rows[:, k * 128:(k + 1) * 128] for k in range(6)]
    return z, high * 128.0 + low, (hi + mid) + lo


def prefix(flags):
    upto = jnp.where(iota((128, 128), 0) <= iota((128, 128), 1), 1.0, 0.0).astype(bf16)
    return jnp.dot(jnp.where(flags, 1.0, 0.0).astype(bf16), upto, preferred_element_type=f32).astype(i32)


def take(x, index):
    return jnp.take_along_axis(x, index, axis=1, mode="promise_in_bounds")


def by_block(cell, w):
    counts = [prefix((cell >> 15) == b) for b in range(BLOCKS)]
    starts = [jnp.zeros((128, 1), i32)]
    for b in range(BLOCKS - 1):
        starts.append(starts[-1] + counts[b][:, 127:128])
    lane = iota((128, 128), 1)
    block, rank = jnp.zeros((128, 128), i32), lane
    for b in range(1, BLOCKS):
        block = jnp.where(lane >= starts[b], b, block)
        rank = jnp.where(lane >= starts[b], lane - starts[b], rank)
    at = jnp.zeros((128, 128), i32)
    for step in (64, 32, 16, 8, 4, 2, 1):
        probe = at + (step - 1)
        seen = take(counts[0], probe)
        for b in range(1, BLOCKS):
            seen = jnp.where(block == b, take(counts[b], probe), seen)
        at = jnp.where(seen <= rank, at + step, at)
    marks = jnp.zeros((128, 128), f32)
    for b in range(1, BLOCKS):
        marks = jnp.where((lane == 4 + b) | (lane == 8 + b), starts[b].astype(f32), marks)
    return take(cell, at), take(w, at), marks


def send_kernel(count, brick, times, offs_in, deps_in, lens_in, held, send, pay, offs, deps, lens, load_sem, meet_sem,
                send_sem, recv_sem):
    here = coords()
    loads = [
        pltpu.make_async_copy(src, dst, load_sem.at[k])
        for k, (src, dst) in enumerate(((offs_in, offs), (deps_in, deps), (lens_in, lens)))
    ]
    for load in loads:
        load.start()
    barrier = pltpu.get_barrier_semaphore()
    lines = [p for group in ((1, 0), (2,), (3,)) for p in stage_peers(here, group)]
    for peer in lines:
        pl.semaphore_signal(barrier, inc=1, device_id=peer, device_id_type=MESH)
    tb = brick[...].astype(f32)
    brick_row = jnp.concatenate([tb[k:k + 1, :] for k in range(TPR)], axis=1)
    time_row = jnp.concatenate([times[...]] * TPR, axis=1)
    ray_row = iota((1, 128), 1) & 31
    live = ray_row < count[0]
    as_rows = jnp.broadcast_to(brick_row, (128, 128))
    same = (as_rows == as_rows.T) & (iota((128, 128), 0) < iota((128, 128), 1))
    rank_row = jnp.sum(jnp.where(same, 1.0, 0.0), axis=0, keepdims=True)
    for load in loads:
        load.wait()
    cell = jnp.concatenate([offs[:, k, :] * DEP + deps[:, k, :] for k in range(TPR)], axis=0)
    w = jnp.concatenate([lens[:, k, :] * SCALE for k in range(TPR)], axis=0)
    cell, w, marks = by_block(cell, w)
    pay[:, 0:768] = as_payload(cell, w)
    pay[:, 768:896] = marks.astype(bf16)
    pl.semaphore_wait(barrier, len(lines))
    for s, axis in enumerate((2, 3)):
        peers = stage_peers(here, (axis,))
        for peer in peers:
            pl.semaphore_signal(meet_sem.at[s], inc=1, device_id=peer, device_id_type=MESH)
        place_rank(s, brick_row, rank_row, live, time_row, ray_row, pay, send)
        pl.semaphore_wait(meet_sem.at[s], len(peers))
    me = flat(here)

    def go(step, carry):
        steps = (step // 32, (step // 16) % 2, (step // 4) % 4, step % 4)
        peer = tuple((v + d) % n for v, d, n in zip(here, steps, SIZES))
        pltpu.make_async_remote_copy(
            send.at[flat(peer)], held.at[me], send_sem, recv_sem, device_id=peer, device_id_type=MESH).start()
        return carry

    lax.fori_loop(1, NDEV, go, 0)
    held[me] = send[me]
    rest = pl.ds(0, NDEV - 1)
    every = pltpu.make_async_remote_copy(
        send.at[rest], held.at[rest], send_sem, recv_sem, device_id=here, device_id_type=MESH)
    every.wait_recv()
    every.wait_send()


def place_rank(k, brick_row, rank_row, live, time_row, ray_row, pay, send):
    lanes = iota((128, 128), 1)
    picked = jnp.where((iota((128, 128), 0).astype(f32) == brick_row) & (rank_row == k) & live, 1.0, 0.0)
    rows = jnp.dot(picked.astype(bf16), pay[...], preferred_element_type=f32)
    z, col, w = from_payload(rows)
    send[:, k, :] = col * 128.0 + z
    send[:, 2 + k, :] = w
    value = jnp.sum(picked * time_row, axis=1, keepdims=True)
    ray = jnp.sum(picked * (ray_row + 1).astype(f32), axis=1, keepdims=True)
    marks = rows[:, 768:896]
    if k == 0:
        send[:, 4, :] = jnp.where(lanes == 0, value, jnp.where(lanes == 2, ray, jnp.where(lanes < 8, marks, 0.0)))
    else:
        send[:, 4, :] = jnp.where(lanes == 1, value, jnp.where(lanes == 3, ray, jnp.where(lanes < 8, send[:, 4, :], marks)))


def onehot_cols(col_row):
    at = jnp.broadcast_to(col_row.astype(i16), (BLOCK, 128))
    return jnp.where(lax.broadcasted_iota(i16, (BLOCK, 128), 0) == at, jnp.ones((), bf16), jnp.zeros((), bf16))


def onehot_values(dep_row, val_row):
    at = jnp.broadcast_to(dep_row.astype(i16), (DEP, 128))
    here = lax.broadcasted_iota(i16, (DEP, 128), 0) == at
    return jnp.concatenate(
        [jnp.where(here, jnp.broadcast_to(part, (DEP, 128)), jnp.zeros((), bf16)) for part in split2(val_row)], axis=0)


def scatter_rows(acc, chunks, col, dep, val):
    acc[...] = jnp.zeros_like(acc)

    def body(c, carry):
        rows = [pl.ds(c * CHUNK + j, 1) for j in range(CHUNK)]
        for b in range(BLOCKS):
            left = jnp.concatenate([onehot_cols(col(b, r)) for r in rows], axis=1)
            right = jnp.concatenate([onehot_values(dep(b, r), val(b, r)) for r in rows], axis=1)
            acc[b] += lax.dot_general(left, right, (((1,), (1,)), ((), ())), preferred_element_type=f32)
        return carry

    lax.fori_loop(0, chunks, body, 0)


def gather_rows(gt, chunks, col, dep, w, out):
    out[...] = jnp.zeros_like(out)

    def body(c, carry):
        rows = [pl.ds(c * CHUNK + j, 1) for j in range(CHUNK)]
        for b in range(BLOCKS):
            right = jnp.concatenate([onehot_cols(col(b, r)) for r in rows], axis=1)
            res = jnp.dot(gt[:, b * BLOCK:(b + 1) * BLOCK], right, preferred_element_type=f32)
            for j, r in enumerate(rows):
                at = slice(j * 128, (j + 1) * 128)
                both = res[0:128, at] + res[128:256, at]
                here = jnp.where(iota((DEP, 128), 0) == dep(b, r), both, 0.0)
                out[b, r, :] = jnp.sum(here, axis=0, keepdims=True) * w(b, r)
        return carry

    lax.fori_loop(0, chunks, body, 0)


def bucket(n, starts, cell, w, bcol, bdep, bw, btile):
    groups = (n + TILES - 1) // TILES
    lane = iota((8, 128), 1)

    def body(g, carry):
        most, _ = carry
        rows = [pl.ds(pl.multiple_of(g * TILES + 8 * k, 8), 8) for k in range(SHARE)]
        cells, ws = [cell[r, :] for r in rows], [w[r, :] for r in rows]
        firsts = [[jnp.broadcast_to(starts[r, 4 + b:5 + b], (8, 128)) for b in range(BLOCKS)] for r in rows]
        alive = [iota((8, 128), 0) + (g * TILES + 8 * k) < n for k in range(SHARE)]
        ending = jnp.zeros((8, 128), f32)
        for b in range(BLOCKS):
            before = [jnp.zeros((8, 128), f32)]
            for k in range(SHARE):
                after = firsts[k][b + 1] if b + 1 < BLOCKS else float(SEG)
                before.append(before[-1] + jnp.where(alive[k], after - firsts[k][b], 0.0))
            for h in range(2):
                spot = lane + h * 128
                own_cell, own_w = jnp.zeros((8, 128), i32), jnp.zeros((8, 128), f32)
                tile = jnp.zeros((8, 128), i32)
                for k in range(SHARE):
                    start = before[k].astype(i32)
                    at = (firsts[k][b].astype(i32) - start + spot) & (SEG - 1)
                    mine = spot >= start
                    own_cell = jnp.where(mine, take(cells[k], at), own_cell)
                    own_w = jnp.where(mine, take(ws[k], at), own_w)
                    tile = jnp.where(mine, k, tile)
                own_w = jnp.where(spot < before[SHARE].astype(i32), own_w, 0.0)
                out = pl.ds(pl.multiple_of(g * 16 + h * 8, 8), 8)
                bcol[b, out, :] = (own_cell >> 7) - b * BLOCK
                bdep[b, out, :] = own_cell & 127
                bw[b, out, :] = own_w
                btile[b, out, :] = tile
            ending = jnp.maximum(ending, before[SHARE])
        return jnp.maximum(most, ending), ending

    none = jnp.zeros((8, 128), f32)
    most, ending = lax.fori_loop(0, groups, body, (none, none))
    chunks = 2 * groups - jnp.where(jnp.max(ending) <= 128.0, 1, 0)
    return jnp.max(most).astype(i32), jnp.where(n > 0, chunks, 0)


def per_entry(y_col, tile):
    y = y_col.reshape(GROUPS, SHARE, 8, 1)
    tile = tile.reshape(GROUPS, 2, 8, 128)
    spread = jnp.zeros((GROUPS, 2, 8, 128), f32)
    for k in range(SHARE):
        spread = jnp.where(tile == k, y[:, k:k + 1], spread)
    return spread.reshape(ROWS, 128)


def per_tile(vals, btile):
    sums = [jnp.zeros((GROUPS, 8, 128), f32)] * SHARE
    for b in range(BLOCKS):
        value = vals[b, 0:ROWS, :].reshape(GROUPS, 2, 8, 128)
        tile = btile[b].reshape(GROUPS, 2, 8, 128)
        for k in range(SHARE):
            mine = jnp.where(tile == k, value, 0.0)
            sums[k] = sums[k] + mine[:, 0] + mine[:, 1]
    columns = [jnp.sum(x, axis=2, keepdims=True)[:, None] for x in sums]
    return jnp.concatenate(columns, axis=1).reshape(PLACES, 1)


def both_passes(count, y_col, cell, w, bcol, bdep, bw, btile, finish_q, q_out, acc, gt, wy, vals, part):
    fits = count[1] <= 256

    def whole():
        q = finish_q(jnp.concatenate([acc[b, :, 0:128] + acc[b, :, 128:256] for b in range(BLOCKS)], axis=0))
        q_out[...] = q
        hi, lo = split2(q.T)
        gt[0:128, :] = hi
        gt[128:256, :] = lo

    @pl.when(fits)
    def _():
        for b in range(BLOCKS):
            wy[b, 0:ROWS, :] = bw[b] * per_entry(y_col, btile[b])
        cols, deps = (lambda b, r: bcol[b, r, :]), (lambda b, r: bdep[b, r, :])
        scatter_rows(acc, count[2], cols, deps, lambda b, r: wy[b, r, :])
        whole()
        gather_rows(gt, count[2], cols, deps, lambda b, r: bw[b, r, :], vals)
        part[...] = per_tile(vals, btile)

    @pl.when(jnp.logical_not(fits))
    def _():
        chunks = (count[0] + CHUNK - 1) // CHUNK
        wy[0] = w[...] * y_col
        cols, deps = (lambda b, r: (cell[r, :] >> 7) - b * BLOCK), (lambda b, r: cell[r, :] & 127)
        scatter_rows(acc, chunks, cols, deps, lambda b, r: wy[0, r, :])
        whole()
        gather_rows(gt, chunks, cols, deps, lambda b, r: w[r, :], vals)
        part[...] = jnp.sum((vals[0] + vals[1]) + (vals[2] + vals[3]), axis=1, keepdims=True)


def place_of(slot_info):
    return jnp.where(iota((PLACES, SLOTS), 0) == slot_info, 1.0, 0.0)


def to_rays(partial, place, rays):
    row = jnp.sum(place * partial, axis=0, keepdims=True)
    total = jnp.zeros((RAYS, NDEV), f32)
    for k in range(2):
        at = slice(k * 128, (k + 1) * 128)
        total += jnp.where(iota((RAYS, NDEV), 0) == rays[:, at], row[:, at], 0.0)
    return total


def from_rays(values, place, rays):
    rows = [
        jnp.sum(jnp.where(iota((RAYS, NDEV), 0) == rays[:, k * 128:(k + 1) * 128], values, 0.0), axis=0, keepdims=True)
        for k in range(2)
    ]
    return jnp.sum(place * jnp.concatenate(rows, axis=1), axis=1, keepdims=True)


def total_of(x):
    return jnp.sum(jnp.sum(x, axis=0, keepdims=True), axis=1, keepdims=True)


def as_row(values):
    row = jnp.zeros((8, NDEV), f32)
    for k, value in enumerate(values):
        row = jnp.where(iota((8, NDEV), 1) == k, value, row)
    return row


def first_kernel(held, times, q_out, p_out, times_out, cell, w, bcol, bdep, bw, btile, info, count, acc, gt, wy, vals, part,
                 starts):
    times_out[...] = times[...]
    meta = held[:, 4, :]
    across = meta.T
    y_row = jnp.concatenate([across[0:1, :], across[1:2, :]], axis=1)
    ray_row = jnp.concatenate([across[2:3, :], across[3:4, :]], axis=1).astype(i32) - 1
    live = ray_row >= 0
    flags = jnp.broadcast_to(jnp.where(live, 1.0, 0.0), (8, SLOTS)).astype(bf16)
    before = jnp.where(iota((SLOTS, SLOTS), 0) < iota((SLOTS, SLOTS), 1), 1.0, 0.0).astype(bf16)
    at = jnp.dot(flags, before, preferred_element_type=f32)[0:1, :].astype(i32)
    at = jnp.where(live, at, -1)
    info[0:1, :] = at
    info[1:2, :] = ray_row
    n = jnp.sum(jnp.where(live, 1.0, 0.0)).astype(i32)
    place = place_of(at)
    pay = jnp.concatenate([as_payload(held[:, k, :].astype(i32), held[:, 2 + k, :]) for k in range(2)], axis=0)
    marks = jnp.concatenate([meta, pltpu.roll(meta, 124, 1)], axis=0).astype(bf16)
    rows = jnp.dot(place.astype(bf16), jnp.concatenate([pay, marks], axis=1), preferred_element_type=f32)
    z, c, lens = from_payload(rows)
    cell[...] = (c * 128.0 + z).astype(i32)
    w[...] = lens
    starts[...] = rows[:, 768:896]
    most, chunks = bucket(n, starts, cell, w, bcol, bdep, bw, btile)
    count[0] = n
    count[1] = most
    count[2] = chunks
    y_col = jnp.sum(place * y_row, axis=1, keepdims=True)
    both_passes(count, y_col, cell, w, bcol, bdep, bw, btile, lambda q: q, q_out, acc, gt, wy, vals, part)
    p_out[0:RAYS, :] = to_rays(part[...], place_of(at), ray_row)
    q = q_out[...]
    p_out[RAYS:RAYS + 8, :] = as_row([total_of(q * q)])


def second_kernel(p, shift, q0, smooth, cell, w, bcol, bdep, bw, btile, info, count, e_out, p_out, dots, acc, gt, wy, vals,
                  part):
    place = place_of(info[0:1, :])
    ray_row = info[1:2, :]
    y_col = from_rays(p[...], place, ray_row)
    finish_q = lambda q: q + smooth[...] - shift[0:1, 0:1] * q0[...]
    both_passes(count, y_col, cell, w, bcol, bdep, bw, btile, finish_q, e_out, acc, gt, wy, vals, part)
    p_out[...] = to_rays(part[...], place, ray_row)
    e = e_out[...]
    dots[...] = as_row([total_of(e * q0[...]), total_of(e * e)])


def shape(dims, dtype=f32):
    return jax.ShapeDtypeStruct(dims, dtype)


SCRATCH = [
    pltpu.VMEM((BLOCKS, BLOCK, 256), f32),
    pltpu.VMEM((256, COLS), bf16),
    pltpu.VMEM((BLOCKS, PLACES, SEG), f32),
    pltpu.VMEM((BLOCKS, PLACES, SEG), f32),
    pltpu.VMEM((PLACES, 1), f32),
]


STAGES = ((1, 0), (2,), (3,))
ROUNDS = ((1, 0), (2, 3))


def send_stage(s, here, group, buf, got, send_sem, recv_sem):
    copies = []
    for k, peer in enumerate(stage_peers(here, group)):
        copy = pltpu.make_async_remote_copy(
            buf.at[s], got.at[s, k], send_sem.at[s, k], recv_sem.at[s, k], device_id=peer, device_id_type=MESH)
        copy.start()
        copies.append(copy)
    return copies


def add_stage(s, copies, buf, got):
    total = buf[s]
    for k, copy in enumerate(copies):
        copy.wait_recv()
        total = total + got[s, k]
    return total


def send_halo(here, field, edge, halo, send_sem, recv_sem):
    edge[0] = field[pl.ds(CLAT - 1, CLON, stride=CLAT), :]
    edge[1] = field[pl.ds(0, CLON, stride=CLAT), :]
    faces = (field.at[pl.ds(COLS - CLAT, CLAT)], field.at[pl.ds(0, CLAT)], edge.at[0], edge.at[1])
    copies = []
    for k, (face, peer) in enumerate(zip(faces, ring_peers(here))):
        copy = pltpu.make_async_remote_copy(
            face, halo.at[k], send_sem.at[k], recv_sem.at[k], device_id=peer, device_id_type=MESH)
        copy.start()
        copies.append(copy)
    return copies


def stencil_rows(here, field, halo, put):
    lat = here[2] * 4 + here[3]
    has_before = jnp.where(lat > 0, 1.0, 0.0)
    has_after = jnp.where(lat < 15, 1.0, 0.0)
    row, lane = iota((CLAT, DEP), 0), iota((CLAT, DEP), 1)

    def layer(i, before, after):
        mine = pl.ds(i * CLAT, CLAT)
        f = field[mine, :]
        lat_before = jnp.where(row == 0, halo[2, i:i + 1, :] * has_before, pltpu.roll(f, 1, 0))
        lat_after = jnp.where(row == CLAT - 1, halo[3, i:i + 1, :] * has_after, pltpu.roll(f, CLAT - 1, 0))
        up = jnp.where(lane == 0, 0.0, pltpu.roll(f, 1, 1))
        down = jnp.where(lane == DEP - 1, 0.0, pltpu.roll(f, DEP - 1, 1))
        put(mine, DAMP * (6.0 * f - before - after - lat_before - lat_after - up - down))

    for i in range(CLON):
        before = field[(i - 1) * CLAT:i * CLAT, :] if i else halo[0]
        after = field[(i + 1) * CLAT:(i + 2) * CLAT, :] if i < CLON - 1 else halo[1]
        layer(i, before, after)


def finish(copies):
    for copy in copies:
        copy.wait_send()


def middle_kernel(p_part, q, p_out, shift, smooth, buf, got, g, edge, halo, send_sem, recv_sem, face_send, face_recv):
    here = coords()
    meet([p for group in STAGES for p in stage_peers(here, group)] + ring_peers(here)[2:])
    buf[0] = p_part[...]
    first = send_stage(0, here, STAGES[0], buf, got, send_sem, recv_sem)
    faces = send_halo(here, q, edge.at[0], halo.at[0], face_send.at[0], face_recv.at[0])
    buf[1] = add_stage(0, first, buf, got)
    second = send_stage(1, here, STAGES[1], buf, got, send_sem, recv_sem)
    for copy in faces:
        copy.wait_recv()

    def to_g(rows, value):
        g[rows, :] = value

    stencil_rows(here, q, halo.at[0], to_g)
    more = send_halo(here, g, edge.at[1], halo.at[1], face_send.at[1], face_recv.at[1])
    buf[2] = add_stage(1, second, buf, got)
    third = send_stage(2, here, STAGES[2], buf, got, send_sem, recv_sem)
    for copy in more:
        copy.wait_recv()

    def to_smooth(rows, value):
        smooth[rows, :] = value

    stencil_rows(here, g, halo.at[1], to_smooth)
    total = add_stage(2, third, buf, got)
    p = total[0:RAYS, :]
    p_out[...] = p
    shift[...] = as_row([total_of(p * p) / total[RAYS:RAYS + 1, 0:1], total[RAYS:RAYS + 1, 0:1]])
    finish(first + second + third + faces + more)


def last_kernel(count, times, p_part, p0, shift, dots, q0, e, model, misfit, buf, got, small, small_got, norm, edge, halo,
                send_sem, recv_sem, small_send, small_recv, face_send, face_recv):
    here = coords()
    meet([p for group in STAGES for p in stage_peers(here, group)] + ring_peers(here)[2:])
    faces = send_halo(here, e, edge, halo, face_send, face_recv)
    buf[0] = p_part[...]
    first = send_stage(0, here, STAGES[0], buf, got, send_sem, recv_sem)
    norm[...] = jnp.zeros_like(norm)
    for copy in faces:
        copy.wait_recv()

    def to_norm(rows, value):
        norm[...] += value * value

    stencil_rows(here, e, halo, to_norm)
    small[0] = jnp.where(iota((8, NDEV), 1) == 2, total_of(norm[...]), dots[...])
    one = send_stage(0, here, ROUNDS[0], small, small_got, small_send, small_recv)
    buf[1] = add_stage(0, first, buf, got)
    second = send_stage(1, here, STAGES[1], buf, got, send_sem, recv_sem)
    small[1] = add_stage(0, one, small, small_got)
    buf[2] = add_stage(1, second, buf, got)
    two = send_stage(1, here, ROUNDS[1], small, small_got, small_send, small_recv)
    third = send_stage(2, here, STAGES[2], buf, got, send_sem, recv_sem)
    moments = add_stage(1, two, small, small_got)
    pe = add_stage(2, third, buf, got)
    mu, m0 = shift[0:1, 0:1], shift[0:1, 1:2]
    s, big = moments[0:1, 0:1] / m0, moments[0:1, 1:2] / m0
    r = (moments[0:1, 2:3] + total_of(pe * pe)) / m0
    cross = big + mu * s
    det = (s + mu) * r - cross * cross
    a, b = (r - s * cross) / det, (s * s - big) / det
    model[...] = (SCALE * a) * q0[...] + (SCALE * b) * e[...]
    fit = jnp.where(iota((RAYS, NDEV), 1) == flat(here), a * p0[...] + b * pe, 0.0)
    column = jnp.sum(fit, axis=1, keepdims=True)
    own = jnp.sum(jnp.where(iota((RAYS, RAYS), 0) == iota((RAYS, RAYS), 1), column, 0.0), axis=0, keepdims=True)
    data = jnp.where(iota((1, RAYS), 1) < count[0], times[...], 0.0)
    misfit[...] = data - own
    finish(faces + first + second + third + one + two)


def comm_params(number, room=16 << 20):
    return pltpu.CompilerParams(vmem_limit_bytes=room, collective_id=number, has_side_effects=True)


def face_scratch(*dims):
    return [pltpu.VMEM(dims + (2, CLON, DEP), f32), pltpu.VMEM(dims + (4, CLON, DEP), f32)]


def sems(*dims):
    return [pltpu.SemaphoreType.DMA(dims), pltpu.SemaphoreType.DMA(dims)]


def shards(travel_times, ray_counts, tile_brick, cell_offsets, cell_depths, seg_lengths):
    times = travel_times.reshape(1, RAYS)
    held = pl.pallas_call(
        send_kernel,
        out_shape=shape((NDEV, 5, SEG)),
        in_specs=[SMEM] + [VMEM] * 2 + [pl.BlockSpec(memory_space=pltpu.MemorySpace.HBM)] * 3,
        out_specs=VMEM,
        scratch_shapes=[pltpu.VMEM((NDEV, 5, SEG), f32), pltpu.VMEM((128, 896), bf16)]
        + [pltpu.VMEM((RAYS, TPR, SEG), d) for d in (i32, i32, f32)]
        + [pltpu.SemaphoreType.DMA((3,)), pltpu.SemaphoreType.REGULAR((2,)), pltpu.SemaphoreType.DMA, pltpu.SemaphoreType.DMA],
        compiler_params=comm_params(2, 60 << 20),
    )(ray_counts, tile_brick.T, times, cell_offsets, cell_depths, seg_lengths)
    entries = [shape((PLACES, SEG), d) for d in (i32, f32)] + [shape((BLOCKS, ROWS, 128), d) for d in (i32, i32, f32, i32)]
    q0, p_part, times, *lists, info, count = pl.pallas_call(
        first_kernel,
        out_shape=(shape((COLS, DEP)), shape((RAYS + 8, NDEV)), shape((1, RAYS)), *entries, shape((2, SLOTS), i32), shape((3,), i32)),
        in_specs=[VMEM] * 2,
        out_specs=(VMEM,) * 10 + (SMEM,),
        scratch_shapes=SCRATCH + [pltpu.VMEM((PLACES, 128), f32)],
        compiler_params=PARAMS,
    )(held, times)
    p0, shift, smooth = pl.pallas_call(
        middle_kernel,
        out_shape=(shape((RAYS, NDEV)), shape((8, NDEV)), shape((COLS, DEP))),
        in_specs=[VMEM] * 2,
        out_specs=(VMEM,) * 3,
        scratch_shapes=[pltpu.VMEM((3, RAYS + 8, NDEV), f32), pltpu.VMEM((3, 7, RAYS + 8, NDEV), f32),
                        pltpu.VMEM((COLS, DEP), f32)] + face_scratch(2) + sems(3, 7) + sems(2, 4),
        compiler_params=comm_params(0),
    )(p_part, q0)
    e, p_part, dots = pl.pallas_call(
        second_kernel,
        out_shape=(shape((COLS, DEP)), shape((RAYS, NDEV)), shape((8, NDEV))),
        in_specs=[VMEM] * 11 + [SMEM],
        out_specs=(VMEM,) * 3,
        scratch_shapes=SCRATCH,
        compiler_params=PARAMS,
    )(p0, shift, q0, smooth, *lists, info, count)
    model, misfit = pl.pallas_call(
        last_kernel,
        out_shape=(shape((COLS, DEP)), shape((1, RAYS))),
        in_specs=[SMEM] + [VMEM] * 7,
        out_specs=(VMEM,) * 2,
        scratch_shapes=[pltpu.VMEM((3, RAYS, NDEV), f32), pltpu.VMEM((3, 7, RAYS, NDEV), f32),
                        pltpu.VMEM((2, 8, NDEV), f32), pltpu.VMEM((2, 15, 8, NDEV), f32), pltpu.VMEM((CLAT, DEP), f32)]
        + face_scratch() + sems(3, 7) + sems(2, 15) + sems(4),
        compiler_params=comm_params(1),
    )(ray_counts, times, p_part, p0, shift, dots, q0, e)
    return (model.reshape(CLON, CLAT, DEP), misfit.reshape(RAYS))


def solution(mesh):
    torus = Mesh(mesh.devices.reshape(4, 2, 4, 4), LON_LAT)
    in_specs = (
        P(LON_LAT),
        P(LON_LAT),
        P(LON_LAT, None),
        P(LON_LAT, None, None),
        P(LON_LAT, None, None),
        P(LON_LAT, None, None),
    )
    out_specs = (P(LON, LAT, None), P(LON_LAT))
    return jax.shard_map(shards, mesh=torus, in_specs=in_specs, out_specs=out_specs, check_vma=False)
```
